128 devices in a mesh: dp: 32 (over y_hi, z, x), tensor: 4 (over y_lo, core).
Axes of the slice: x: 4, y: 4 (y_hi: 2, y_lo: 2; y = y_hi * 2 + y_lo), z: 4, core: 2. Of those that a mesh axis runs over, the one named last changes fastest.
Arguments:
- hidden_in: float32 [16384, 1024], P(('dp', 'tensor')), may hold values from -6 to 6
- segments: int32 [32, 512], P('dp'), may hold values from 0 to 3, never falling along the last dimension, each value on 1 to 256 neighbouring positions
- w_qkv: bfloat16 [2, 1024, 3, 1024], P(None, 'dp', None, 'tensor'), may hold values from -0.1875 to 0.1875
- w_out: bfloat16 [2, 1024, 1024], P(None, 'dp', 'tensor'), may hold values from -0.75 to 0.75
- w_up: bfloat16 [2, 1024, 4096], P(None, 'dp', 'tensor'), may hold values from -0.1875 to 0.1875
- w_down: bfloat16 [2, 1024, 4096], P(None, 'dp', 'tensor'), may hold values from -0.09375 to 0.09375
- qv_bias: float32 [2, 2, 1024], replicated, may hold values from -2 to 2
- proj_bias: float32 [2, 2, 1024], replicated, may hold values from -2 to 2
- up_bias: float32 [2, 4096], replicated, may hold values from -3 to 3
- ln_gain: float32 [2, 2, 1024], replicated, may hold values from 0.5 to 1.5
- ln_shift: float32 [2, 2, 1024], replicated, may hold values from -2 to 2
- cotangent: float32 [16384, 1024], P(('dp', 'tensor')), may hold values from -6 to 6
Outputs:
- layer_out: float32 [16384, 1024], P(('dp', 'tensor'))
- grad_in: float32 [16384, 1024], P(('dp', 'tensor'))
- grad_qkv: float32 [2, 1024, 3, 1024], P(None, 'dp', None, 'tensor')
- grad_out: float32 [2, 1024, 1024], P(None, 'dp', 'tensor')
- grad_up: float32 [2, 1024, 4096], P(None, 'dp', 'tensor')
- grad_down: float32 [2, 1024, 4096], P(None, 'dp', 'tensor')
- grad_qv_bias: float32 [2, 2, 1024], replicated
- grad_proj_bias: float32 [2, 2, 1024], replicated
- grad_up_bias: float32 [2, 4096], replicated
- grad_ln_gain: float32 [2, 2, 1024], replicated
- grad_ln_shift: float32 [2, 2, 1024], replicated
The draws below stay inside these ranges and needn't reach their ends.
Inputs may be any that keep to these rules, and one draw needn't show every extreme that they name: `segments`: in each sequence the document numbers never fall; every document holds 1 to 256 tokens and one holds exactly 256.
All inputs are finite; a program needn't handle non-finite values.
Results may differ from the reference program's by a relative error of at most 0.025.
Values may be sent and summed in bfloat16 or wider, within the bound.
No kernel may reach another device: no remote copies, remote signals or barrier semaphores. Data moves between devices by JAX's collectives and lax.ppermute only.
A program may use at most 128 MiB of HBM per device.

```python
import math
import jax
import jax.numpy as jnp
import numpy as np
from jax import lax

D = 1024
HEADS = 16
HEAD_DIM = 64
FF = 4096
LAYERS = 2
SEQ_LEN = 512
DOCS = 4
DOC_MOST = 256
SEQS = 32
TOKENS = 16384


def steps_of(key, shape, split, low, top_value):
    def one(dim, blocks):
        heights = jax.random.uniform(jax.random.fold_in(jax.random.fold_in(key, 6), dim), (blocks,), jnp.float32, low / len(split), top_value / len(split))
        return jnp.repeat(jnp.exp(heights), shape[dim] // blocks).reshape((-1,) + (1,) * (len(shape) - dim - 1))

    loudness = one(*split[0])
    for cut in split[1:]:
        loudness = loudness * one(*cut)
    return loudness


def split_up(count, total, bound, skew):
    loads = [(1 << 20) // math.isqrt(rank ** skew) + 1 for rank in range(2, count + 1)]
    surplus, given = total - bound - (count - 1), [1] * (count - 1)
    while surplus > 0:
        free = [i for i in range(count - 1) if given[i] < bound]
        pool, budget = sum([loads[i] for i in free]), surplus
        for i in free:
            more = min(bound - given[i], max(1, budget * loads[i] // pool), surplus)
            given[i] = given[i] + more
            surplus = surplus - more
    return np.array([bound] + given)


def ragged(key, count, total, most, slope):
    if count == 2:
        one = jax.random.randint(key, (), max(1, total - most), min(most, total - 1) + 1)
        return jnp.stack([one, total - one])
    sizes = jnp.asarray(split_up(count, total, most, slope), jnp.int32)
    pairs = (count - 1) // 2
    source_of, receiver = sizes[1:1 + 2 * pairs:2], sizes[2:2 + 2 * pairs:2]
    margin = jnp.minimum(source_of - 1, most - receiver)
    moved = jax.random.randint(jax.random.fold_in(key, 1), (pairs,), 0, 1 << 20) % (margin + 1)
    sizes = sizes.at[1:1 + 2 * pairs:2].set(source_of - moved).at[2:2 + 2 * pairs:2].set(receiver + moved)
    return sizes[jax.random.permutation(jax.random.fold_in(key, 2), count)]


def centred(rng, dims, scale, bound, cuts=(), dtype=jnp.bfloat16):
    array = scale * jax.random.normal(rng, dims, jnp.float32)
    if cuts:
        array = array * steps_of(rng, dims, cuts, -0.22, 0.18)
    return jnp.clip(array, -bound, bound).astype(dtype)


def setup_inputs(seed: int = 0) -> dict:
    streams_of = jax.random.split(jax.random.key(seed), 13)
    hidden_in = centred(streams_of[0], (TOKENS, D), 1.0, 6.0, ((0, 128),), jnp.float32)
    segments = jax.vmap(lambda own: jnp.searchsorted(jnp.cumsum(ragged(own, DOCS, SEQ_LEN, DOC_MOST, 2)), jnp.arange(SEQ_LEN), side="right"))(jax.random.split(streams_of[1], SEQS)).reshape((SEQS, SEQ_LEN)).astype(jnp.int32)
    w_qkv = centred(streams_of[2], (LAYERS, D, 3, D), D ** -0.5, 0.1875, ((1, 32), (3, 4)))
    w_out = centred(streams_of[3], (LAYERS, D, D), (D // 16) ** -0.5, 0.75, ((1, 32), (2, 4)))
    w_up = centred(streams_of[4], (LAYERS, D, FF), D ** -0.5, 0.1875, ((1, 32), (2, 4)))
    w_down = centred(streams_of[5], (LAYERS, D, FF), FF ** -0.5, 0.09375, ((1, 32), (2, 4)))
    qv_bias = centred(streams_of[6], (LAYERS, 2, D), 0.3, 2.0, (), jnp.float32)
    proj_bias = centred(streams_of[7], (LAYERS, 2, D), 0.3, 2.0, (), jnp.float32)
    up_bias = centred(streams_of[8], (LAYERS, FF), 0.5, 3.0, (), jnp.float32)
    ln_gain = jnp.clip(1.0 + 0.1 * jax.random.normal(streams_of[9], (LAYERS, 2, D), jnp.float32), 0.5, 1.5)
    ln_shift = centred(streams_of[10], (LAYERS, 2, D), 0.3, 2.0, (), jnp.float32)
    cotangent = centred(streams_of[11], (TOKENS, D), 1.0, 6.0, ((0, 128),), jnp.float32)
    return dict(hidden_in=hidden_in, segments=segments, w_qkv=w_qkv, w_out=w_out, w_up=w_up, w_down=w_down, qv_bias=qv_bias, proj_bias=proj_bias, up_bias=up_bias, ln_gain=ln_gain, ln_shift=ln_shift, cotangent=cotangent)


NORM_EPS = 1e-12
HALF_ROOT = 0.7071067811865476
DENSITY = 0.3989422804014327

def normal_cdf(values):
    return 0.5 * (1.0 + lax.erf(values * HALF_ROOT))

def gelu_slope(values):
    return normal_cdf(values) + values * jnp.exp(-0.5 * values * values) * DENSITY

def layer_norm(activations, gain_row, shift_row):
    center = activations - lax.optimization_barrier(jnp.mean(activations, axis=-1, keepdims=True))
    inv_std = lax.rsqrt(lax.optimization_barrier(jnp.mean(center * center, axis=-1, keepdims=True)) + NORM_EPS)
    normed = center * inv_std
    return (normed * gain_row + shift_row, normed, inv_std)

def norm_back(upstream, normed, inv_std, gain_row):
    scaled = upstream * gain_row
    return inv_std * (scaled - lax.optimization_barrier(jnp.mean(scaled, axis=-1, keepdims=True)) - normed * lax.optimization_barrier(jnp.mean(scaled * normed, axis=-1, keepdims=True)))

def masked_scores(query_heads, key_heads, seg_ids):
    raw_scores = jnp.einsum('qhe,khe->hqk', query_heads.astype(jnp.float32), key_heads.astype(jnp.float32))
    scores = raw_scores * (1.0 / math.sqrt(HEAD_DIM))
    same_doc = seg_ids[:, None] == seg_ids[None, :]
    return jnp.where(same_doc[None, :, :], scores, -jnp.inf)

def attend(packed):
    head_view, seg_ids = packed
    scores = masked_scores(head_view[:, 0], head_view[:, 1], seg_ids)
    row_peak = lax.optimization_barrier(jnp.max(scores, axis=-1, keepdims=True))
    log_total = row_peak + jnp.log(lax.optimization_barrier(jnp.sum(jnp.exp(scores - row_peak), axis=-1, keepdims=True)))
    attn_probs = jnp.exp(scores - log_total).astype(jnp.bfloat16)
    context = jnp.einsum('hqk,khe->qhe', attn_probs.astype(jnp.float32), head_view[:, 2].astype(jnp.float32)).astype(jnp.bfloat16)
    return (context, log_total)

def attend_back(packed):
    head_view, seg_ids, log_total, grad_context = packed
    query_heads = head_view[:, 0]
    key_heads = head_view[:, 1]
    value_heads = head_view[:, 2]
    scores = masked_scores(query_heads, key_heads, seg_ids)
    attn_probs = jnp.exp(scores - log_total)
    probs_bf = attn_probs.astype(jnp.bfloat16)
    grad_f = grad_context.astype(jnp.float32)
    grad_probs = jnp.einsum('qhe,khe->hqk', grad_f, value_heads.astype(jnp.float32))
    grad_value = jnp.einsum('hqk,qhe->khe', probs_bf.astype(jnp.float32), grad_f)
    row_dot = lax.optimization_barrier(jnp.sum(attn_probs * grad_probs, axis=-1, keepdims=True))
    grad_scores = (attn_probs * (grad_probs - row_dot) * (1.0 / math.sqrt(HEAD_DIM))).astype(jnp.bfloat16)
    grad_scores_f = grad_scores.astype(jnp.float32)
    grad_query = jnp.einsum('hqk,khe->qhe', grad_scores_f, key_heads.astype(jnp.float32))
    grad_key = jnp.einsum('hqk,qhe->khe', grad_scores_f, query_heads.astype(jnp.float32))
    return jnp.stack([grad_query, grad_key, grad_value], axis=1)

def reference(hidden_in, segments, w_qkv, w_out, w_up, w_down, qv_bias, proj_bias, up_bias, ln_gain, ln_shift, cotangent):
    single = jnp.float32
    bfloat = jnp.bfloat16
    tokens = hidden_in.shape[0]
    current = hidden_in
    stored = []
    for layer_index in range(LAYERS):
        inputs_bf = current.astype(bfloat)
        mixed_rows = jnp.dot(inputs_bf, w_qkv[layer_index].reshape(D, 3 * D), preferred_element_type=single).reshape(tokens, 3, D)
        bias_three = jnp.stack([qv_bias[layer_index, 0], jnp.zeros((D,), single), qv_bias[layer_index, 1]])
        qkv_bf = (mixed_rows + bias_three).astype(bfloat)
        head_view = qkv_bf.reshape(SEQS, SEQ_LEN, 3, HEADS, HEAD_DIM)
        context, log_total = lax.map(attend, (head_view, segments))
        context_rows = context.reshape(tokens, D)
        attn_full = jnp.dot(context_rows, w_out[layer_index].T, preferred_element_type=single)
        resid_one = current + attn_full + proj_bias[layer_index, 0]
        middle, normed_one, inv_one = layer_norm(resid_one, ln_gain[layer_index, 0], ln_shift[layer_index, 0])
        middle_bf = middle.astype(bfloat)
        hidden_pre = jnp.dot(middle_bf, w_up[layer_index], preferred_element_type=single) + up_bias[layer_index]
        hidden_bf = (hidden_pre * normal_cdf(hidden_pre)).astype(bfloat)
        down_full = jnp.dot(hidden_bf, w_down[layer_index].T, preferred_element_type=single)
        resid_two = middle + down_full + proj_bias[layer_index, 1]
        output_rows, normed_two, inv_two = layer_norm(resid_two, ln_gain[layer_index, 1], ln_shift[layer_index, 1])
        stored.append((inputs_bf, qkv_bf, log_total, context_rows, normed_one, inv_one, middle_bf, hidden_pre, hidden_bf, normed_two, inv_two))
        current = output_rows
    final_out = current
    upstream = cotangent
    grads_qkv, grads_out, grads_up, grads_down = ([], [], [], [])
    grads_qv, grads_proj, grads_upb, grads_gain, grads_shift = ([], [], [], [], [])
    for layer_index in reversed(range(LAYERS)):
        inputs_bf, qkv_bf, log_total, context_rows, normed_one, inv_one, middle_bf, hidden_pre, hidden_bf, normed_two, inv_two = stored[layer_index]
        gain_two = lax.optimization_barrier(jnp.sum(upstream * normed_two, axis=0))
        shift_two = lax.optimization_barrier(jnp.sum(upstream, axis=0))
        grad_two = norm_back(upstream, normed_two, inv_two, ln_gain[layer_index, 1])
        bias_two = lax.optimization_barrier(jnp.sum(grad_two, axis=0))
        grad_two_bf = grad_two.astype(bfloat)
        grad_hidden = jnp.dot(grad_two_bf, w_down[layer_index], preferred_element_type=single)
        grad_pre = grad_hidden * gelu_slope(hidden_pre)
        grad_pre_bf = grad_pre.astype(bfloat)
        up_term = lax.optimization_barrier(jnp.sum(grad_pre, axis=0))
        grad_mid = grad_two + jnp.dot(grad_pre_bf, w_up[layer_index].T, preferred_element_type=single)
        gain_one = lax.optimization_barrier(jnp.sum(grad_mid * normed_one, axis=0))
        shift_one = lax.optimization_barrier(jnp.sum(grad_mid, axis=0))
        grad_one = norm_back(grad_mid, normed_one, inv_one, ln_gain[layer_index, 0])
        bias_one = lax.optimization_barrier(jnp.sum(grad_one, axis=0))
        grad_one_bf = grad_one.astype(bfloat)
        grad_context = jnp.dot(grad_one_bf, w_out[layer_index], preferred_element_type=single).astype(bfloat)
        head_view = qkv_bf.reshape(SEQS, SEQ_LEN, 3, HEADS, HEAD_DIM)
        grad_heads = lax.map(attend_back, (head_view, segments, log_total, grad_context.reshape(SEQS, SEQ_LEN, HEADS, HEAD_DIM)))
        grad_mixed = grad_heads.reshape(tokens, 3, D)
        bias_qv = jnp.stack([lax.optimization_barrier(jnp.sum(grad_mixed[:, 0], axis=0)), lax.optimization_barrier(jnp.sum(grad_mixed[:, 2], axis=0))])
        grad_mixed_bf = grad_mixed.astype(bfloat).reshape(tokens, 3 * D)
        grads_qkv.append(jnp.dot(inputs_bf.T, grad_mixed_bf, preferred_element_type=single).reshape(D, 3, D))
        grads_out.append(jnp.dot(grad_one_bf.T, context_rows, preferred_element_type=single))
        grads_up.append(jnp.dot(middle_bf.T, grad_pre_bf, preferred_element_type=single))
        grads_down.append(jnp.dot(grad_two_bf.T, hidden_bf, preferred_element_type=single))
        grads_qv.append(bias_qv)
        grads_proj.append(jnp.stack([bias_one, bias_two]))
        grads_upb.append(up_term)
        grads_gain.append(jnp.stack([gain_one, gain_two]))
        grads_shift.append(jnp.stack([shift_one, shift_two]))
        upstream = grad_one + jnp.dot(grad_mixed_bf, w_qkv[layer_index].reshape(D, 3 * D).T, preferred_element_type=single)
    return (final_out, upstream, jnp.stack(grads_qkv[::-1]), jnp.stack(grads_out[::-1]), jnp.stack(grads_up[::-1]), jnp.stack(grads_down[::-1]), jnp.stack(grads_qv[::-1]), jnp.stack(grads_proj[::-1]), jnp.stack(grads_upb[::-1]), jnp.stack(grads_gain[::-1]), jnp.stack(grads_shift[::-1]))
```

```python
import jax
import jax.numpy as jnp
from jax import lax
from jax.experimental import pallas as pl
from jax.experimental.pallas import tpu as pltpu
from jax.sharding import PartitionSpec as P

HEADS = 16
HEAD_DIM = 64
LAYERS = 2


NORM_EPS = 1e-12
HALF_ROOT = 0.7071067811865476
DENSITY = 0.3989422804014327


def normal_cdf(values):
    return 0.5 * (1.0 + lax.erf(values * HALF_ROOT))


def gelu_slope(values):
    return normal_cdf(values) + values * jnp.exp(-0.5 * values * values) * DENSITY


def layer_norm(activations, gain_row, shift_row):
    center = activations - jnp.mean(activations, axis=-1, keepdims=True)
    inv_std = lax.rsqrt(jnp.mean(center * center, axis=-1, keepdims=True) + NORM_EPS)
    normed = center * inv_std
    return (normed * gain_row + shift_row, normed, inv_std)


def norm_back(upstream, normed, inv_std, gain_row):
    scaled = upstream * gain_row
    return inv_std * (
        scaled
        - jnp.mean(scaled, axis=-1, keepdims=True)
        - normed * jnp.mean(scaled * normed, axis=-1, keepdims=True)
    )


def attention_weights(qkv_ref, seg_row, seg_col, head):
    width = HEADS // 4 * HEAD_DIM
    cols = [slice(third * width + head * HEAD_DIM, third * width + (head + 1) * HEAD_DIM) for third in range(3)]
    query = qkv_ref[:, cols[0]] * jnp.bfloat16(HEAD_DIM**-0.5)
    key = qkv_ref[:, cols[1]]
    value = qkv_ref[:, cols[2]]
    scores = right_product(key, query)
    scores = jnp.where(seg_col[...] == seg_row[...], scores, -1e30)
    raised = jnp.exp(scores - jnp.max(scores, axis=0, keepdims=True))
    probs = raised * (1.0 / jnp.sum(raised, axis=0, keepdims=True))
    return query, key, value, probs, cols


def attend_kernel(qkv_ref, seg_row, seg_col, context_ref):
    for head in range(context_ref.shape[1] // HEAD_DIM):
        _, _, value, probs, cols = attention_weights(qkv_ref, seg_row, seg_col, head)
        context = outer_sum(value, probs.astype(jnp.bfloat16))
        context_ref[:, cols[0]] = context.T.astype(jnp.bfloat16)


def attend_back_kernel(qkv_ref, seg_row, seg_col, grad_ref, mixed_ref, total_ref):
    total_ref[...] = jnp.zeros_like(total_ref)
    for head in range(grad_ref.shape[1] // HEAD_DIM):
        query, key, value, probs, cols = attention_weights(qkv_ref, seg_row, seg_col, head)
        grad = grad_ref[:, cols[0]]
        grad_probs = right_product(value, grad)
        row_dot = jnp.sum(probs * grad_probs, axis=0, keepdims=True)
        grad_scores = (probs * (grad_probs - row_dot)).astype(jnp.bfloat16)
        grad_query = outer_sum(key, grad_scores).T * (HEAD_DIM**-0.5)
        grad_key = jnp.dot(grad_scores, query, preferred_element_type=jnp.float32)
        grad_value = jnp.dot(
            probs.astype(jnp.bfloat16), grad, preferred_element_type=jnp.float32
        )
        for col, part in zip(cols, (grad_query, grad_key, grad_value)):
            mixed_ref[:, col] = part.astype(jnp.bfloat16)
            total_ref[0:1, col] = jnp.sum(part, axis=0, keepdims=True)


def attend(qkv_bf, seg_row, seg_col):
    rows, cols = qkv_bf.shape
    return pl.pallas_call(
        attend_kernel,
        out_shape=jax.ShapeDtypeStruct((rows, cols // 3), jnp.bfloat16),
    )(qkv_bf, seg_row, seg_col)


def attend_back(qkv_bf, seg_row, seg_col, grad_context):
    rows, cols = qkv_bf.shape
    return pl.pallas_call(
        attend_back_kernel,
        out_shape=(
            jax.ShapeDtypeStruct((rows, cols), jnp.bfloat16),
            jax.ShapeDtypeStruct((8, cols), jnp.float32),
        ),
    )(qkv_bf, seg_row, seg_col, grad_context)


def right_product(left_side, right_side):
    return lax.dot_general(
        left_side, right_side, (((1,), (1,)), ((), ())), preferred_element_type=jnp.float32
    )


def outer_sum(left_side, right_side):
    return lax.dot_general(
        left_side, right_side, (((0,), (0,)), ((), ())), preferred_element_type=jnp.float32
    )


def weight_grads_kernel(*refs):
    result = refs[-1]
    first = 0
    for left_ref, right_ref in zip(refs[0:-1:2], refs[1:-1:2]):
        last = first + right_ref.shape[1]
        result[:, first:last] = outer_sum(left_ref[...], right_ref[...]).astype(jnp.bfloat16)
        first = last


def weight_grads(*pairs):
    tile = 256
    rows, width = pairs[0][0].shape
    total = sum(right.shape[1] for _, right in pairs)
    specs = []
    for _, right in pairs:
        specs.append(pl.BlockSpec((rows, tile), lambda i: (0, i)))
        specs.append(pl.BlockSpec(right.shape, lambda i: (0, 0)))
    return pl.pallas_call(
        weight_grads_kernel,
        grid=(width // tile,),
        in_specs=specs,
        out_specs=pl.BlockSpec((tile, total), lambda i: (i, 0)),
        out_shape=jax.ShapeDtypeStruct((width, total), jnp.bfloat16),
    )(*[side for pair in pairs for side in pair])


def swap(values, bit):
    return lax.ppermute(values, "tensor", [(i, i ^ bit) for i in range(4)])


def gather_rows(own):
    across = swap(own, 2)
    return jnp.concatenate([own, across, swap(own, 1), swap(across, 1)], axis=0)


def sum_rows(partial_sum):
    half = partial_sum.shape[0] // 2
    quarter = half // 2
    part = partial_sum.astype(jnp.bfloat16)
    both = part[:half].astype(jnp.float32) + swap(part[half:], 1).astype(jnp.float32)
    far = swap(both[quarter:].astype(jnp.bfloat16), 2)
    return both[:quarter] + far.astype(jnp.float32)


PLANE = [[half * 16 + place for place in range(16)] for half in range(2)]


def swap_half(values):
    return lax.ppermute(values, "dp", [(i, i ^ 16) for i in range(32)])


def mix_features(values):
    lead = values.shape[:-1]
    values = values.reshape(lead + (2, 16, 32))
    return jnp.swapaxes(values, -3, -2).reshape(lead + (1024,))


def unmix_features(values):
    lead = values.shape[:-1]
    values = values.reshape(lead + (16, 2, 32))
    return jnp.swapaxes(values, -3, -2).reshape(lead + (1024,))


def pair_halves(shard, first_half):
    other = swap_half(shard)
    return jnp.where(
        first_half, jnp.concatenate([shard, other]), jnp.concatenate([other, shard])
    )


def spread(shard, axes, groups=None):
    count = lax.axis_size(axes) if groups is None else len(groups[0])
    copies = jnp.broadcast_to(shard[None], (count,) + shard.shape)
    copies = copies.reshape((count * shard.shape[0],) + shard.shape[1:])
    return lax.all_to_all(copies, axes, 0, 0, tiled=True, axis_index_groups=groups)


def sum_owned(partial_sum, axes, groups=None):
    count = lax.axis_size(axes) if groups is None else len(groups[0])
    pieces = lax.all_to_all(partial_sum, axes, 0, 0, tiled=True, axis_index_groups=groups)
    pieces = pieces.reshape((count, -1) + partial_sum.shape[1:])
    return jnp.sum(pieces.astype(jnp.float32), axis=0)


def sum_halves(pair, first_half):
    rows = pair.shape[0] // 2
    own = jnp.where(first_half, pair[:rows], pair[rows:])
    other = jnp.where(first_half, pair[rows:], pair[:rows])
    return own.astype(jnp.float32) + swap_half(other.astype(jnp.bfloat16)).astype(jnp.float32)


def shards(
    hidden_in,
    segments,
    w_qkv,
    w_out,
    w_up,
    w_down,
    qv_bias,
    proj_bias,
    up_bias,
    ln_gain,
    ln_shift,
    cotangent,
):
    single = jnp.float32
    bfloat = jnp.bfloat16
    model_width = hidden_in.shape[1]
    tensor_count = lax.axis_size("tensor")
    tensor_pos = lax.axis_index("tensor")
    head_count = HEADS // tensor_count
    head_cols = head_count * HEAD_DIM
    hidden_cols = w_up.shape[2]
    seq_count, seq_length = segments.shape
    all_rows = seq_count * seq_length
    owner_rows = model_width // lax.axis_size("dp")
    own_rows = hidden_in.shape[0]
    three_cols = 3 * head_cols
    seg_local = jnp.concatenate(
        [
            lax.dynamic_slice_in_dim(segments, (tensor_pos ^ bit) * own_rows, own_rows, 1)
            for bit in (0, 2, 1, 3)
        ],
        axis=1,
    )

    seg_row, seg_col = seg_local, seg_local.reshape(-1, 1)

    def shard_of(layer_index):
        return (
            w_qkv[layer_index].reshape(owner_rows, three_cols),
            w_out[layer_index],
            w_up[layer_index],
            w_down[layer_index],
        )

    first_half = lax.axis_index("dp") < 16
    first, second = shard_of(0), shard_of(1)
    early = jnp.concatenate(first[:2], axis=1)
    middle_part = jnp.concatenate(first[2:] + second[:2], axis=1)
    late = jnp.concatenate(second[2:], axis=1)
    early = spread(early, "dp").reshape(2, 16, owner_rows, -1)
    early = jnp.swapaxes(early, 0, 1).reshape(model_width, -1)
    pairs = pair_halves(jnp.concatenate([middle_part, late], axis=1), first_half)
    cut_late = middle_part.shape[1]

    def gather_plane(shard):
        return lax.all_gather(shard, "dp", axis=0, tiled=True, axis_index_groups=PLANE)

    middle_part = gather_plane(pairs[:, :cut_late])
    late = gather_plane(pairs[:, cut_late:])
    two_hidden = 2 * hidden_cols
    all_weights = (
        (
            early[:, :three_cols],
            early[:, three_cols:],
            middle_part[:, :hidden_cols],
            middle_part[:, hidden_cols:two_hidden],
        ),
        (
            middle_part[:, two_hidden : two_hidden + three_cols],
            middle_part[:, two_hidden + three_cols :],
            late[:, :hidden_cols],
            late[:, hidden_cols:],
        ),
    )
    proj_bias = mix_features(proj_bias)
    ln_gain = mix_features(ln_gain)
    ln_shift = mix_features(ln_shift)

    current = mix_features(hidden_in)
    stored = []
    for layer_index in range(LAYERS):
        mat_qkv, mat_out, mat_up, mat_down = all_weights[layer_index]
        rows_all = gather_rows(current.astype(bfloat))
        mixed_rows = jnp.dot(
            rows_all, mat_qkv, preferred_element_type=single
        )
        bias_here = lax.dynamic_slice_in_dim(
            qv_bias[layer_index], tensor_pos * head_cols, head_cols, 1
        )
        bias_three = jnp.concatenate(
            [bias_here[0], jnp.zeros((head_cols,), single), bias_here[1]]
        )
        qkv_bf = (mixed_rows + bias_three).astype(bfloat)
        context_rows = attend(qkv_bf, seg_row, seg_col)
        resid_one = (
            current + sum_rows(right_product(context_rows, mat_out)) + proj_bias[layer_index, 0]
        )
        middle, normed_one, inv_one = layer_norm(
            resid_one, ln_gain[layer_index, 0], ln_shift[layer_index, 0]
        )
        middle_all = gather_rows(middle.astype(bfloat))
        up_here = lax.dynamic_slice_in_dim(
            up_bias[layer_index], tensor_pos * hidden_cols, hidden_cols, 0
        )
        hidden_pre = jnp.dot(middle_all, mat_up, preferred_element_type=single) + up_here
        hidden_bf = (hidden_pre * normal_cdf(hidden_pre)).astype(bfloat)
        resid_two = (
            middle + sum_rows(right_product(hidden_bf, mat_down)) + proj_bias[layer_index, 1]
        )
        output_rows, normed_two, inv_two = layer_norm(
            resid_two, ln_gain[layer_index, 1], ln_shift[layer_index, 1]
        )
        stored.append(
            (
                rows_all,
                qkv_bf,
                context_rows,
                normed_one,
                inv_one,
                middle_all,
                hidden_pre,
                hidden_bf,
                normed_two,
                inv_two,
            )
        )
        current = output_rows
    upstream = mix_features(cotangent)
    sums_ffn = []
    both_axes = ("dp", "tensor")
    grads_qv, grads_proj, grads_upb, grads_gain, grads_shift = ([], [], [], [], [])
    for layer_index in reversed(range(LAYERS)):
        (
            rows_all,
            qkv_bf,
            context_rows,
            normed_one,
            inv_one,
            middle_all,
            hidden_pre,
            hidden_bf,
            normed_two,
            inv_two,
        ) = stored[layer_index]
        mat_qkv, mat_out, mat_up, mat_down = all_weights[layer_index]
        gain_two = jnp.sum(upstream * normed_two, axis=0)
        shift_two = jnp.sum(upstream, axis=0)
        grad_two = norm_back(upstream, normed_two, inv_two, ln_gain[layer_index, 1])
        bias_two = jnp.sum(grad_two, axis=0)
        grad_ffn_all = gather_rows(grad_two.astype(bfloat))
        grad_hidden = jnp.dot(grad_ffn_all, mat_down, preferred_element_type=single)
        grad_pre = grad_hidden * gelu_slope(hidden_pre)
        grad_pre_bf = grad_pre.astype(bfloat)
        up_term = jnp.sum(grad_pre, axis=0)
        grad_mid = grad_two + sum_rows(right_product(grad_pre_bf, mat_up))
        gain_one = jnp.sum(grad_mid * normed_one, axis=0)
        shift_one = jnp.sum(grad_mid, axis=0)
        grad_one = norm_back(grad_mid, normed_one, inv_one, ln_gain[layer_index, 0])
        bias_one = jnp.sum(grad_one, axis=0)
        grad_attn_all = gather_rows(grad_one.astype(bfloat))
        block_ffn = weight_grads(
            (middle_all, grad_pre_bf), (grad_ffn_all, hidden_bf), (grad_attn_all, context_rows)
        )
        grads_proj.append(jnp.stack([bias_one, bias_two]))
        grads_upb.append(
            lax.dynamic_update_slice(
                jnp.zeros((up_bias.shape[1],), single), up_term, (tensor_pos * hidden_cols,)
            )
        )
        grads_gain.append(jnp.stack([gain_one, gain_two]))
        grads_shift.append(jnp.stack([shift_one, shift_two]))
        if layer_index:
            grad_attn_all, block_ffn = lax.optimization_barrier((grad_attn_all, block_ffn))
        else:
            small_parts = [
                jnp.stack(part)
                for part in (
                    [jnp.zeros((2, model_width), single)] + grads_qv,
                    grads_proj[::-1],
                    grads_upb[::-1],
                    grads_gain[::-1],
                    grads_shift[::-1],
                )
            ]
            flat = jnp.concatenate([part.reshape(-1) for part in small_parts])
            pieces = flat.reshape(lax.axis_size(both_axes), -1)
            grad_attn_all, block_ffn, pieces, qkv_last = lax.optimization_barrier(
                (grad_attn_all, block_ffn, pieces, qkv_last)
            )
            small_owned = sum_owned(pieces, both_axes)
        sums_ffn.append(
            lax.psum_scatter(
                block_ffn, "dp", scatter_dimension=0, tiled=True, axis_index_groups=PLANE
            )
        )
        grad_context = jnp.dot(grad_attn_all, mat_out, preferred_element_type=single).astype(bfloat)
        grad_mixed_bf, total = attend_back(qkv_bf, seg_row, seg_col, grad_context)
        bias_qv = jnp.stack([total[0, :head_cols], total[0, 2 * head_cols :]])
        block_qkv = weight_grads((rows_all, grad_mixed_bf))
        if layer_index:
            grads_qv.append(
                lax.dynamic_update_slice(
                    jnp.zeros((2, model_width), single), bias_qv, (0, tensor_pos * head_cols)
                )
            )
        else:
            grad_mixed_bf, small_owned = lax.optimization_barrier((grad_mixed_bf, small_owned))
        input_part = right_product(grad_mixed_bf, mat_qkv)
        input_part, block_qkv = lax.optimization_barrier((input_part, block_qkv))
        qkv_sum = sum_owned(block_qkv, "dp", PLANE)
        if layer_index:
            qkv_last = qkv_sum
        upstream = grad_one + sum_rows(input_part)
    qkv_sum, small_owned, bias_qv = lax.optimization_barrier((qkv_sum, small_owned, bias_qv))
    flat = spread(jnp.concatenate([small_owned, bias_qv.reshape(1, -1)], axis=1), both_axes)
    first_qv = flat[:, small_owned.shape[1] :].reshape(-1, tensor_count, 2, head_cols)
    first_qv = jnp.swapaxes(jnp.sum(first_qv, axis=0), 0, 1).reshape(2, model_width)
    flat = flat[:, : small_owned.shape[1]].reshape(-1)
    small_totals = []
    for part in small_parts:
        small_totals.append(flat[: part.size].reshape(part.shape))
        flat = flat[part.size :]
    small_totals[0] = small_totals[0].at[0].set(first_qv)
    sums_last = sum_halves(
        jnp.concatenate([sums_ffn[0].astype(single), qkv_last], axis=1), first_half
    )
    sums_first = sum_halves(
        jnp.concatenate([sums_ffn[1].astype(single), qkv_sum], axis=1), first_half
    )
    cut_out = two_hidden + head_cols
    grad_weights = []
    for sums in (sums_first, sums_last):
        grad_weights.append(
            (
                sums[:, cut_out:].reshape(owner_rows, 3, head_cols),
                sums[:, two_hidden:cut_out],
                sums[:, :hidden_cols],
                sums[:, hidden_cols:two_hidden],
            )
        )
    return (
        unmix_features(current),
        unmix_features(upstream),
        jnp.stack([part[0] for part in grad_weights]),
        jnp.stack([part[1] for part in grad_weights]),
        jnp.stack([part[2] for part in grad_weights]),
        jnp.stack([part[3] for part in grad_weights]),
        small_totals[0],
        unmix_features(small_totals[1]),
        small_totals[2],
        unmix_features(small_totals[3]),
        unmix_features(small_totals[4]),
    )


def solution(mesh):
    placed = (
        P(("dp", "tensor"), None),
        P("dp", None),
        P(None, "dp", None, "tensor"),
        P(None, "dp", "tensor"),
        P(None, "dp", "tensor"),
        P(None, "dp", "tensor"),
        P(),
        P(),
        P(),
        P(),
        P(),
        P(("dp", "tensor"), None),
    )
    return jax.shard_map(
        shards,
        mesh=mesh,
        in_specs=placed,
        out_specs=(
            P(("dp", "tensor"), None),
            P(("dp", "tensor"), None),
            P(None, "dp", None, "tensor"),
            P(None, "dp", "tensor"),
            P(None, "dp", "tensor"),
            P(None, "dp", "tensor"),
            P(),
            P(),
            P(),
            P(),
            P(),
        ),
        check_vma=False,
    )
```

```python
import jax
import jax.numpy as jnp
from jax import lax
from jax.experimental import pallas as pl
from jax.experimental.pallas import tpu as pltpu
from jax.sharding import PartitionSpec as P

HEADS = 16
HEAD_DIM = 64
LAYERS = 2


NORM_EPS = 1e-12
HALF_ROOT = 0.7071067811865476
DENSITY = 0.3989422804014327


def normal_cdf(values):
    return 0.5 * (1.0 + lax.erf(values * HALF_ROOT))


def gelu_slope(values):
    return normal_cdf(values) + values * jnp.exp(-0.5 * values * values) * DENSITY


def layer_norm(activations, gain_row, shift_row):
    center = activations - jnp.mean(activations, axis=-1, keepdims=True)
    inv_std = lax.rsqrt(jnp.mean(center * center, axis=-1, keepdims=True) + NORM_EPS)
    normed = center * inv_std
    return (normed * gain_row + shift_row, normed, inv_std)


def norm_back(upstream, normed, inv_std, gain_row):
    scaled = upstream * gain_row
    return inv_std * (
        scaled
        - jnp.mean(scaled, axis=-1, keepdims=True)
        - normed * jnp.mean(scaled * normed, axis=-1, keepdims=True)
    )


def attention_weights(qkv_ref, seg_row, seg_col, head):
    width = HEADS // 4 * HEAD_DIM
    cols = [slice(third * width + head * HEAD_DIM, third * width + (head + 1) * HEAD_DIM) for third in range(3)]
    query = qkv_ref[:, cols[0]] * jnp.bfloat16(HEAD_DIM**-0.5)
    key = qkv_ref[:, cols[1]]
    value = qkv_ref[:, cols[2]]
    scores = right_product(key, query)
    scores = jnp.where(seg_col[...] == seg_row[...], scores, -1e30)
    raised = jnp.exp(scores - jnp.max(scores, axis=0, keepdims=True))
    probs = raised * (1.0 / jnp.sum(raised, axis=0, keepdims=True))
    return query, key, value, probs, cols


def attend_kernel(qkv_ref, seg_row, seg_col, context_ref):
    for head in range(context_ref.shape[1] // HEAD_DIM):
        _, _, value, probs, cols = attention_weights(qkv_ref, seg_row, seg_col, head)
        context = outer_sum(value, probs.astype(jnp.bfloat16))
        context_ref[:, cols[0]] = context.T.astype(jnp.bfloat16)


def attend_back_kernel(qkv_ref, seg_row, seg_col, grad_ref, mixed_ref, total_ref):
    total_ref[...] = jnp.zeros_like(total_ref)
    for head in range(grad_ref.shape[1] // HEAD_DIM):
        query, key, value, probs, cols = attention_weights(qkv_ref, seg_row, seg_col, head)
        grad = grad_ref[:, cols[0]]
        grad_probs = right_product(value, grad)
        row_dot = jnp.sum(probs * grad_probs, axis=0, keepdims=True)
        grad_scores = (probs * (grad_probs - row_dot)).astype(jnp.bfloat16)
        grad_query = outer_sum(key, grad_scores).T * (HEAD_DIM**-0.5)
        grad_key = jnp.dot(grad_scores, query, preferred_element_type=jnp.float32)
        grad_value = jnp.dot(
            probs.astype(jnp.bfloat16), grad, preferred_element_type=jnp.float32
        )
        for col, part in zip(cols, (grad_query, grad_key, grad_value)):
            mixed_ref[:, col] = part.astype(jnp.bfloat16)
            total_ref[0:1, col] = jnp.sum(part, axis=0, keepdims=True)


def attention_cost(rows, cols, products, moved):
    return pl.CostEstimate(
        flops=2 * products * rows * rows * (cols // 3),
        transcendentals=rows * rows * (cols // 3 // HEAD_DIM),
        bytes_accessed=2 * rows * moved,
    )


def attend(qkv_bf, seg_row, seg_col):
    rows, cols = qkv_bf.shape
    return pl.pallas_call(
        attend_kernel,
        out_shape=jax.ShapeDtypeStruct((rows, cols // 3), jnp.bfloat16),
        cost_estimate=attention_cost(rows, cols, 2, cols + cols // 3),
    )(qkv_bf, seg_row, seg_col)


def attend_back(qkv_bf, seg_row, seg_col, grad_context):
    rows, cols = qkv_bf.shape
    return pl.pallas_call(
        attend_back_kernel,
        out_shape=(
            jax.ShapeDtypeStruct((rows, cols), jnp.bfloat16),
            jax.ShapeDtypeStruct((8, cols), jnp.float32),
        ),
        cost_estimate=attention_cost(rows, cols, 5, 2 * cols + cols // 3),
    )(qkv_bf, seg_row, seg_col, grad_context)


def right_product(left_side, right_side):
    return lax.dot_general(
        left_side, right_side, (((1,), (1,)), ((), ())), preferred_element_type=jnp.float32
    )


def outer_sum(left_side, right_side):
    return lax.dot_general(
        left_side, right_side, (((0,), (0,)), ((), ())), preferred_element_type=jnp.float32
    )


def weight_grads_kernel(*refs):
    result = refs[-1]
    first = 0
    left_over = len(refs) % 3
    if left_over == 2:
        extra_ref = refs[-2]
        result[:, result.shape[1] - extra_ref.shape[1] :] = extra_ref[...]
        refs = refs[:-2] + refs[-1:]
    for near_ref, far_ref, right_ref in zip(refs[0:-1:3], refs[1:-1:3], refs[2:-1:3]):
        last = first + right_ref.shape[1]
        half = near_ref.shape[0]
        block = outer_sum(near_ref[...], right_ref[:half, :])
        block = block + outer_sum(far_ref[...], right_ref[half:, :])
        result[:, first:last] = block.astype(jnp.bfloat16)
        first = last


def weight_grads(*pairs, extra=None):
    tile = 256
    half, width = pairs[0][0][0].shape
    total = sum(right.shape[1] for _, right in pairs)
    specs, operands = [], []
    for left, right in pairs:
        specs += [pl.BlockSpec((half, tile), lambda i: (0, i))] * 2
        specs.append(pl.BlockSpec(right.shape, lambda i: (0, 0)))
        operands += [left[0], left[1], right]
    flops = 4 * half * width * total
    moved = sum(2 * operand.size for operand in operands) + 2 * width * total
    if extra is not None:
        specs.append(pl.BlockSpec((tile, extra.shape[1]), lambda i: (i, 0)))
        operands.append(extra)
        total += extra.shape[1]
    return pl.pallas_call(
        weight_grads_kernel,
        grid=(width // tile,),
        in_specs=specs,
        out_specs=pl.BlockSpec((tile, total), lambda i: (i, 0)),
        out_shape=jax.ShapeDtypeStruct((width, total), jnp.bfloat16),
        cost_estimate=pl.CostEstimate(flops=flops, transcendentals=0, bytes_accessed=moved),
    )(*operands)


def swap(values, bit):
    return lax.ppermute(values, "tensor", [(i, i ^ bit) for i in range(4)])


def with_neighbour(own):
    return jnp.concatenate([own, swap(own, 2)], axis=0)


def gather_rows(pair):
    return pair, swap(pair, 1)


def sum_rows(partial_sum, held=None):
    half = partial_sum.shape[0] // 2
    quarter = half // 2
    part = partial_sum.astype(jnp.bfloat16)
    both = part[:half].astype(jnp.float32) + swap(part[half:], 1).astype(jnp.float32)
    across = swap(both.astype(jnp.bfloat16), 2)
    if held is not None:
        across, held = lax.optimization_barrier((across, held))
    across = jnp.concatenate([across[quarter:], across[:quarter]], axis=0)
    total = both + across.astype(jnp.float32)
    return total if held is None else (total, held)


PLANE = [[half * 16 + place for place in range(16)] for half in range(2)]


def swap_half(values):
    return lax.ppermute(values, "dp", [(i, i ^ 16) for i in range(32)])


def mix_features(values):
    lead = values.shape[:-1]
    values = values.reshape(lead + (2, 16, 32))
    return jnp.swapaxes(values, -3, -2).reshape(lead + (1024,))


def unmix_features(values):
    lead = values.shape[:-1]
    values = values.reshape(lead + (16, 2, 32))
    return jnp.swapaxes(values, -3, -2).reshape(lead + (1024,))


def pair_halves(shard, first_half):
    other = swap_half(shard)
    return jnp.where(
        first_half, jnp.concatenate([shard, other]), jnp.concatenate([other, shard])
    )


def spread(shard, axes, groups=None):
    count = lax.axis_size(axes) if groups is None else len(groups[0])
    copies = jnp.broadcast_to(shard[None], (count,) + shard.shape)
    copies = copies.reshape((count * shard.shape[0],) + shard.shape[1:])
    return lax.all_to_all(copies, axes, 0, 0, tiled=True, axis_index_groups=groups)


def sum_owned(partial_sum, axes, groups=None):
    count = lax.axis_size(axes) if groups is None else len(groups[0])
    pieces = lax.all_to_all(partial_sum, axes, 0, 0, tiled=True, axis_index_groups=groups)
    pieces = pieces.reshape((count, -1) + partial_sum.shape[1:])
    return jnp.sum(pieces.astype(jnp.float32), axis=0)


def sum_halves(pair, first_half):
    rows = pair.shape[0] // 2
    own = jnp.where(first_half, pair[:rows], pair[rows:])
    other = jnp.where(first_half, pair[rows:], pair[:rows])
    return own.astype(jnp.float32) + swap_half(other.astype(jnp.bfloat16)).astype(jnp.float32)


def shards(
    hidden_in,
    segments,
    w_qkv,
    w_out,
    w_up,
    w_down,
    qv_bias,
    proj_bias,
    up_bias,
    ln_gain,
    ln_shift,
    cotangent,
):
    single = jnp.float32
    bfloat = jnp.bfloat16
    model_width = hidden_in.shape[1]
    tensor_count = lax.axis_size("tensor")
    tensor_pos = lax.axis_index("tensor")
    head_count = HEADS // tensor_count
    head_cols = head_count * HEAD_DIM
    hidden_cols = w_up.shape[2]
    seq_count, seq_length = segments.shape
    all_rows = seq_count * seq_length
    owner_rows = model_width // lax.axis_size("dp")
    own_rows = hidden_in.shape[0]
    three_cols = 3 * head_cols
    seg_local = jnp.concatenate(
        [
            lax.dynamic_slice_in_dim(segments, (tensor_pos ^ bit) * own_rows, own_rows, 1)
            for bit in (0, 2, 1, 3)
        ],
        axis=1,
    )

    seg_row, seg_col = seg_local, seg_local.reshape(-1, 1)

    def shard_of(layer_index):
        return (
            w_qkv[layer_index].reshape(owner_rows, three_cols),
            w_out[layer_index],
            w_up[layer_index],
            w_down[layer_index],
        )

    first_half = lax.axis_index("dp") < 16
    first, second = shard_of(0), shard_of(1)
    early = jnp.concatenate(first[:2], axis=1)
    middle_part = jnp.concatenate(first[2:] + second[:2], axis=1)
    late = jnp.concatenate(second[2:], axis=1)
    early = spread(early, "dp").reshape(2, 16, owner_rows, -1)
    early = jnp.swapaxes(early, 0, 1).reshape(model_width, -1)

    def gather_plane(shard):
        return lax.all_gather(shard, "dp", axis=0, tiled=True, axis_index_groups=PLANE)

    middle_part = gather_plane(pair_halves(middle_part, first_half))
    late = gather_plane(pair_halves(late, first_half))
    two_hidden = 2 * hidden_cols
    all_weights = (
        (
            early[:, :three_cols],
            early[:, three_cols:],
            middle_part[:, :hidden_cols],
            middle_part[:, hidden_cols:two_hidden],
        ),
        (
            middle_part[:, two_hidden : two_hidden + three_cols],
            middle_part[:, two_hidden + three_cols :],
            late[:, :hidden_cols],
            late[:, hidden_cols:],
        ),
    )
    proj_bias = mix_features(proj_bias)
    ln_gain = mix_features(ln_gain)
    ln_shift = mix_features(ln_shift)

    current = with_neighbour(mix_features(hidden_in))
    stored = []
    for layer_index in range(LAYERS):
        mat_qkv, mat_out, mat_up, mat_down = all_weights[layer_index]
        rows_all = gather_rows(current.astype(bfloat))
        mixed_rows = jnp.dot(
            jnp.concatenate(rows_all), mat_qkv, preferred_element_type=single
        )
        bias_here = lax.dynamic_slice_in_dim(
            qv_bias[layer_index], tensor_pos * head_cols, head_cols, 1
        )
        bias_three = jnp.concatenate(
            [bias_here[0], jnp.zeros((head_cols,), single), bias_here[1]]
        )
        qkv_bf = (mixed_rows + bias_three).astype(bfloat)
        context_rows = attend(qkv_bf, seg_row, seg_col)
        resid_one = (
            current + sum_rows(right_product(context_rows, mat_out)) + proj_bias[layer_index, 0]
        )
        middle, normed_one, inv_one = layer_norm(
            resid_one, ln_gain[layer_index, 0], ln_shift[layer_index, 0]
        )
        middle_all = gather_rows(middle.astype(bfloat))
        up_here = lax.dynamic_slice_in_dim(
            up_bias[layer_index], tensor_pos * hidden_cols, hidden_cols, 0
        )
        hidden_pre = jnp.dot(jnp.concatenate(middle_all), mat_up, preferred_element_type=single) + up_here
        hidden_bf = (hidden_pre * normal_cdf(hidden_pre)).astype(bfloat)
        resid_two = (
            middle + sum_rows(right_product(hidden_bf, mat_down)) + proj_bias[layer_index, 1]
        )
        output_rows, normed_two, inv_two = layer_norm(
            resid_two, ln_gain[layer_index, 1], ln_shift[layer_index, 1]
        )
        stored.append(
            (
                rows_all,
                qkv_bf,
                context_rows,
                normed_one,
                inv_one,
                middle_all,
                hidden_pre,
                hidden_bf,
                normed_two,
                inv_two,
            )
        )
        current = output_rows
    upstream = with_neighbour(mix_features(cotangent))
    sums_ffn = []
    both_axes = ("dp", "tensor")
    all_tokens, own_columns = [None] * LAYERS, [None] * LAYERS
    for layer_index in reversed(range(LAYERS)):
        (
            rows_all,
            qkv_bf,
            context_rows,
            normed_one,
            inv_one,
            middle_all,
            hidden_pre,
            hidden_bf,
            normed_two,
            inv_two,
        ) = stored[layer_index]
        mat_qkv, mat_out, mat_up, mat_down = all_weights[layer_index]
        gain_two = jnp.sum((upstream * normed_two)[:own_rows], axis=0)
        shift_two = jnp.sum(upstream[:own_rows], axis=0)
        grad_two = norm_back(upstream, normed_two, inv_two, ln_gain[layer_index, 1])
        bias_two = jnp.sum(grad_two[:own_rows], axis=0)
        grad_ffn_all = gather_rows(grad_two.astype(bfloat))
        grad_hidden = jnp.dot(jnp.concatenate(grad_ffn_all), mat_down, preferred_element_type=single)
        grad_pre = grad_hidden * gelu_slope(hidden_pre)
        grad_pre_bf = grad_pre.astype(bfloat)
        up_term = jnp.sum(grad_pre, axis=0)
        block_ffn = weight_grads((middle_all, grad_pre_bf), (grad_ffn_all, hidden_bf))
        part_sum, block_ffn = sum_rows(right_product(grad_pre_bf, mat_up), block_ffn)
        sums_ffn.append(
            lax.psum_scatter(
                block_ffn, "dp", scatter_dimension=0, tiled=True, axis_index_groups=PLANE
            )
        )
        grad_mid = grad_two + part_sum
        gain_one = jnp.sum((grad_mid * normed_one)[:own_rows], axis=0)
        shift_one = jnp.sum(grad_mid[:own_rows], axis=0)
        grad_one = norm_back(grad_mid, normed_one, inv_one, ln_gain[layer_index, 0])
        bias_one = jnp.sum(grad_one[:own_rows], axis=0)
        grad_attn_all = gather_rows(grad_one.astype(bfloat))
        grad_context = jnp.dot(
            jnp.concatenate(grad_attn_all), mat_out, preferred_element_type=single
        ).astype(bfloat)
        if not layer_index:
            grad_context, sums_attn = lax.optimization_barrier((grad_context, sums_attn))
        grad_mixed_bf, total = attend_back(qkv_bf, seg_row, seg_col, grad_context)
        all_tokens[layer_index] = [gain_one, gain_two, shift_one, shift_two, bias_one, bias_two]
        all_tokens[layer_index] = jnp.concatenate(all_tokens[layer_index])
        own_columns[layer_index] = jnp.concatenate(
            [total[0, :head_cols], total[0, 2 * head_cols :], up_term]
        )
        pairs = ((rows_all, grad_mixed_bf), (grad_attn_all, context_rows))
        if layer_index:
            input_part = right_product(grad_mixed_bf, mat_qkv)
            part_sum, block = sum_rows(input_part, weight_grads(*pairs))
            sums_attn = sum_owned(block, "dp", PLANE)
        else:
            small = jnp.concatenate(all_tokens + own_columns).reshape(model_width, -1)
            high = small.astype(bfloat)
            low = (small - high.astype(single)).astype(bfloat)
            count = small.shape[1]
            rest = jnp.zeros((model_width, 128 - 2 * count), bfloat)
            sums_last = jnp.concatenate([sums_ffn[0].astype(single), sums_attn], axis=1)
            extra = jnp.concatenate([high, low, rest], axis=1)
            sums_attn = sum_owned(weight_grads(*pairs, extra=extra), "dp", PLANE)
            sums_last = sum_halves(sums_last, first_half)
            sums_attn, sums_last, grad_mixed_bf = lax.optimization_barrier(
                (sums_attn, sums_last, grad_mixed_bf)
            )
            block_cols = three_cols + head_cols
            small = sums_attn[:, block_cols : block_cols + count]
            small = small + sums_attn[:, block_cols + count : block_cols + 2 * count]
            sums_attn = sums_attn[:, :block_cols]
            small = spread(small.reshape(1, -1), both_axes)
            part_sum, small = sum_rows(right_product(grad_mixed_bf, mat_qkv), small)
        upstream = grad_one + part_sum
    small = small.reshape(2, 16, tensor_count, -1)
    small = jnp.swapaxes(jnp.sum(small, axis=0), 0, 1).reshape(tensor_count, -1)
    token_count = LAYERS * 6 * model_width
    over_tokens = jnp.sum(small[:, :token_count], axis=0).reshape(LAYERS, 3, 2, model_width)
    over_tokens = unmix_features(over_tokens)
    over_columns = jnp.swapaxes(small[:, token_count:].reshape(tensor_count, LAYERS, -1), 0, 1)
    total_qv = over_columns[:, :, : 2 * head_cols].reshape(LAYERS, tensor_count, 2, head_cols)
    total_qv = jnp.swapaxes(total_qv, 1, 2).reshape(LAYERS, 2, model_width)
    total_up = over_columns[:, :, 2 * head_cols :].reshape(LAYERS, -1)
    sums_first = sum_halves(
        jnp.concatenate([sums_ffn[1].astype(single), sums_attn], axis=1), first_half
    )
    cut_out = two_hidden + three_cols
    grad_weights = []
    for sums in (sums_first, sums_last):
        grad_weights.append(
            (
                sums[:, two_hidden:cut_out].reshape(owner_rows, 3, head_cols),
                sums[:, cut_out:],
                sums[:, :hidden_cols],
                sums[:, hidden_cols:two_hidden],
            )
        )
    return (
        unmix_features(current[:own_rows]),
        unmix_features(upstream[:own_rows]),
        jnp.stack([part[0] for part in grad_weights]),
        jnp.stack([part[1] for part in grad_weights]),
        jnp.stack([part[2] for part in grad_weights]),
        jnp.stack([part[3] for part in grad_weights]),
        total_qv,
        over_tokens[:, 2],
        total_up,
        over_tokens[:, 0],
        over_tokens[:, 1],
    )


def solution(mesh):
    placed = (
        P(("dp", "tensor"), None),
        P("dp", None),
        P(None, "dp", None, "tensor"),
        P(None, "dp", "tensor"),
        P(None, "dp", "tensor"),
        P(None, "dp", "tensor"),
        P(),
        P(),
        P(),
        P(),
        P(),
        P(("dp", "tensor"), None),
    )
    return jax.shard_map(
        shards,
        mesh=mesh,
        in_specs=placed,
        out_specs=(
            P(("dp", "tensor"), None),
            P(("dp", "tensor"), None),
            P(None, "dp", None, "tensor"),
            P(None, "dp", "tensor"),
            P(None, "dp", "tensor"),
            P(None, "dp", "tensor"),
            P(),
            P(),
            P(),
            P(),
            P(),
        ),
        check_vma=False,
    )
```

```python
import jax
import jax.numpy as jnp
from jax import lax
from jax.experimental import pallas as pl
from jax.experimental.pallas import tpu as pltpu
from jax.sharding import PartitionSpec as P

HEADS = 16
HEAD_DIM = 64
LAYERS = 2


NORM_EPS = 1e-12
HALF_ROOT = 0.7071067811865476
DENSITY = 0.3989422804014327


def normal_cdf(values):
    return 0.5 * (1.0 + lax.erf(values * HALF_ROOT))


def gelu_slope(values):
    return normal_cdf(values) + values * jnp.exp(-0.5 * values * values) * DENSITY


def layer_norm(activations, gain_row, shift_row):
    center = activations - jnp.mean(activations, axis=-1, keepdims=True)
    inv_std = lax.rsqrt(jnp.mean(center * center, axis=-1, keepdims=True) + NORM_EPS)
    normed = center * inv_std
    return (normed * gain_row + shift_row, normed, inv_std)


def norm_back(upstream, normed, inv_std, gain_row):
    scaled = upstream * gain_row
    return inv_std * (
        scaled
        - jnp.mean(scaled, axis=-1, keepdims=True)
        - normed * jnp.mean(scaled * normed, axis=-1, keepdims=True)
    )


def attention_weights(qkv_ref, seg_row, seg_col, head):
    width = HEADS // 4 * HEAD_DIM
    cols = [slice(third * width + head * HEAD_DIM, third * width + (head + 1) * HEAD_DIM) for third in range(3)]
    query = qkv_ref[:, cols[0]] * jnp.bfloat16(HEAD_DIM**-0.5)
    key = qkv_ref[:, cols[1]]
    value = qkv_ref[:, cols[2]]
    scores = right_product(key, query)
    scores = jnp.where(seg_col[...] == seg_row[...], scores, -1e30)
    raised = jnp.exp(scores - jnp.max(scores, axis=0, keepdims=True))
    probs = raised * (1.0 / jnp.sum(raised, axis=0, keepdims=True))
    return query, key, value, probs, cols


def attend_kernel(qkv_ref, seg_row, seg_col, context_ref):
    for head in range(context_ref.shape[1] // HEAD_DIM):
        _, _, value, probs, cols = attention_weights(qkv_ref, seg_row, seg_col, head)
        context = outer_sum(value, probs.astype(jnp.bfloat16))
        context_ref[:, cols[0]] = context.T.astype(jnp.bfloat16)


def attend_back_kernel(qkv_ref, seg_row, seg_col, grad_ref, mixed_ref, total_ref):
    total_ref[...] = jnp.zeros_like(total_ref)
    for head in range(grad_ref.shape[1] // HEAD_DIM):
        query, key, value, probs, cols = attention_weights(qkv_ref, seg_row, seg_col, head)
        grad = grad_ref[:, cols[0]]
        grad_probs = right_product(value, grad)
        row_dot = jnp.sum(probs * grad_probs, axis=0, keepdims=True)
        grad_scores = (probs * (grad_probs - row_dot)).astype(jnp.bfloat16)
        grad_query = outer_sum(key, grad_scores).T * (HEAD_DIM**-0.5)
        grad_key = jnp.dot(grad_scores, query, preferred_element_type=jnp.float32)
        grad_value = jnp.dot(
            probs.astype(jnp.bfloat16), grad, preferred_element_type=jnp.float32
        )
        for col, part in zip(cols, (grad_query, grad_key, grad_value)):
            mixed_ref[:, col] = part.astype(jnp.bfloat16)
            total_ref[0:1, col] = jnp.sum(part, axis=0, keepdims=True)


def attention_cost(rows, cols, products, moved):
    return pl.CostEstimate(
        flops=2 * products * rows * rows * (cols // 3),
        transcendentals=rows * rows * (cols // 3 // HEAD_DIM),
        bytes_accessed=2 * rows * moved,
    )


def attend(qkv_bf, seg_row, seg_col):
    rows, cols = qkv_bf.shape
    return pl.pallas_call(
        attend_kernel,
        out_shape=jax.ShapeDtypeStruct((rows, cols // 3), jnp.bfloat16),
        cost_estimate=attention_cost(rows, cols, 2, cols + cols // 3),
    )(qkv_bf, seg_row, seg_col)


def attend_back(qkv_bf, seg_row, seg_col, grad_context):
    rows, cols = qkv_bf.shape
    return pl.pallas_call(
        attend_back_kernel,
        out_shape=(
            jax.ShapeDtypeStruct((rows, cols), jnp.bfloat16),
            jax.ShapeDtypeStruct((8, cols), jnp.float32),
        ),
        cost_estimate=attention_cost(rows, cols, 5, 2 * cols + cols // 3),
    )(qkv_bf, seg_row, seg_col, grad_context)


def right_product(left_side, right_side):
    return lax.dot_general(
        left_side, right_side, (((1,), (1,)), ((), ())), preferred_element_type=jnp.float32
    )


def outer_sum(left_side, right_side):
    return lax.dot_general(
        left_side, right_side, (((0,), (0,)), ((), ())), preferred_element_type=jnp.float32
    )


def weight_grads_kernel(*refs):
    result = refs[-1]
    first = 0
    left_over = len(refs) % 3
    if left_over == 2:
        extra_ref = refs[-2]
        result[:, result.shape[1] - extra_ref.shape[1] :] = extra_ref[...]
        refs = refs[:-2] + refs[-1:]
    for near_ref, far_ref, right_ref in zip(refs[0:-1:3], refs[1:-1:3], refs[2:-1:3]):
        last = first + right_ref.shape[1]
        half = near_ref.shape[0]
        block = outer_sum(near_ref[...], right_ref[:half, :])
        block = block + outer_sum(far_ref[...], right_ref[half:, :])
        result[:, first:last] = block.astype(jnp.bfloat16)
        first = last


def weight_grads(*pairs, extra=None):
    tile = 256
    half, width = pairs[0][0][0].shape
    total = sum(right.shape[1] for _, right in pairs)
    specs, operands = [], []
    for left, right in pairs:
        specs += [pl.BlockSpec((half, tile), lambda i: (0, i))] * 2
        specs.append(pl.BlockSpec(right.shape, lambda i: (0, 0)))
        operands += [left[0], left[1], right]
    flops = 4 * half * width * total
    moved = sum(2 * operand.size for operand in operands) + 2 * width * total
    if extra is not None:
        specs.append(pl.BlockSpec((tile, extra.shape[1]), lambda i: (i, 0)))
        operands.append(extra)
        total += extra.shape[1]
    return pl.pallas_call(
        weight_grads_kernel,
        grid=(width // tile,),
        in_specs=specs,
        out_specs=pl.BlockSpec((tile, total), lambda i: (i, 0)),
        out_shape=jax.ShapeDtypeStruct((width, total), jnp.bfloat16),
        cost_estimate=pl.CostEstimate(flops=flops, transcendentals=0, bytes_accessed=moved),
    )(*operands)


def swap(values, bit):
    return lax.ppermute(values, "tensor", [(i, i ^ bit) for i in range(4)])


def with_neighbour(own):
    return jnp.concatenate([own, swap(own, 2)], axis=0)


def gather_rows(pair):
    return pair, swap(pair, 1)


def sum_rows(partial_sum, held=None):
    half = partial_sum.shape[0] // 2
    quarter = half // 2
    part = partial_sum.astype(jnp.bfloat16)
    both = part[:half].astype(jnp.float32) + swap(part[half:], 1).astype(jnp.float32)
    across = swap(both.astype(jnp.bfloat16), 2)
    if held is not None:
        across, held = lax.optimization_barrier((across, held))
    across = jnp.concatenate([across[quarter:], across[:quarter]], axis=0)
    total = both + across.astype(jnp.float32)
    return total if held is None else (total, held)


PLANE = [[half * 16 + place for place in range(16)] for half in range(2)]


def swap_half(values):
    return lax.ppermute(values, "dp", [(i, i ^ 16) for i in range(32)])


def mix_features(values):
    lead = values.shape[:-1]
    values = values.reshape(lead + (2, 16, 32))
    return jnp.swapaxes(values, -3, -2).reshape(lead + (1024,))


def unmix_features(values):
    lead = values.shape[:-1]
    values = values.reshape(lead + (16, 2, 32))
    return jnp.swapaxes(values, -3, -2).reshape(lead + (1024,))


def pair_halves(shard, first_half):
    other = swap_half(shard)
    return jnp.where(
        first_half, jnp.concatenate([shard, other]), jnp.concatenate([other, shard])
    )


def spread(shard, axes, groups=None):
    count = lax.axis_size(axes) if groups is None else len(groups[0])
    copies = jnp.broadcast_to(shard[None], (count,) + shard.shape)
    copies = copies.reshape((count * shard.shape[0],) + shard.shape[1:])
    return lax.all_to_all(copies, axes, 0, 0, tiled=True, axis_index_groups=groups)


def sum_owned(partial_sum, axes, groups=None):
    count = lax.axis_size(axes) if groups is None else len(groups[0])
    pieces = lax.all_to_all(partial_sum, axes, 0, 0, tiled=True, axis_index_groups=groups)
    pieces = pieces.reshape((count, -1) + partial_sum.shape[1:])
    return jnp.sum(pieces.astype(jnp.float32), axis=0)


def sum_halves(pair, first_half):
    rows = pair.shape[0] // 2
    own = jnp.where(first_half, pair[:rows], pair[rows:])
    other = jnp.where(first_half, pair[rows:], pair[:rows])
    return own.astype(jnp.float32) + swap_half(other.astype(jnp.bfloat16)).astype(jnp.float32)


def shards(
    hidden_in,
    segments,
    w_qkv,
    w_out,
    w_up,
    w_down,
    qv_bias,
    proj_bias,
    up_bias,
    ln_gain,
    ln_shift,
    cotangent,
):
    single = jnp.float32
    bfloat = jnp.bfloat16
    model_width = hidden_in.shape[1]
    tensor_count = lax.axis_size("tensor")
    tensor_pos = lax.axis_index("tensor")
    head_count = HEADS // tensor_count
    head_cols = head_count * HEAD_DIM
    hidden_cols = w_up.shape[2]
    seq_count, seq_length = segments.shape
    all_rows = seq_count * seq_length
    owner_rows = model_width // lax.axis_size("dp")
    own_rows = hidden_in.shape[0]
    three_cols = 3 * head_cols
    seg_local = jnp.concatenate(
        [
            lax.dynamic_slice_in_dim(segments, (tensor_pos ^ bit) * own_rows, own_rows, 1)
            for bit in (0, 2, 1, 3)
        ],
        axis=1,
    )

    seg_row, seg_col = seg_local, seg_local.reshape(-1, 1)

    def shard_of(layer_index):
        return (
            w_qkv[layer_index].reshape(owner_rows, three_cols),
            w_out[layer_index],
            w_up[layer_index],
            w_down[layer_index],
        )

    first_half = lax.axis_index("dp") < 16
    first, second = shard_of(0), shard_of(1)
    early = jnp.concatenate(first[:2], axis=1)
    middle_part = jnp.concatenate(first[2:] + second[:2], axis=1)
    late = jnp.concatenate(second[2:], axis=1)
    early = spread(early, "dp").reshape(2, 16, owner_rows, -1)
    early = jnp.swapaxes(early, 0, 1).reshape(model_width, -1)

    def gather_plane(shard):
        return lax.all_gather(shard, "dp", axis=0, tiled=True, axis_index_groups=PLANE)

    middle_part = gather_plane(pair_halves(middle_part, first_half))
    late = gather_plane(pair_halves(late, first_half))
    two_hidden = 2 * hidden_cols
    all_weights = (
        (
            early[:, :three_cols],
            early[:, three_cols:],
            middle_part[:, :hidden_cols],
            middle_part[:, hidden_cols:two_hidden],
        ),
        (
            middle_part[:, two_hidden : two_hidden + three_cols],
            middle_part[:, two_hidden + three_cols :],
            late[:, :hidden_cols],
            late[:, hidden_cols:],
        ),
    )
    proj_bias = mix_features(proj_bias)
    ln_gain = mix_features(ln_gain)
    ln_shift = mix_features(ln_shift)

    current = with_neighbour(mix_features(hidden_in))
    stored = []
    for layer_index in range(LAYERS):
        mat_qkv, mat_out, mat_up, mat_down = all_weights[layer_index]
        rows_all = gather_rows(current.astype(bfloat))
        mixed_rows = jnp.dot(
            jnp.concatenate(rows_all), mat_qkv, preferred_element_type=single
        )
        bias_here = lax.dynamic_slice_in_dim(
            qv_bias[layer_index], tensor_pos * head_cols, head_cols, 1
        )
        bias_three = jnp.concatenate(
            [bias_here[0], jnp.zeros((head_cols,), single), bias_here[1]]
        )
        qkv_bf = (mixed_rows + bias_three).astype(bfloat)
        context_rows = attend(qkv_bf, seg_row, seg_col)
        resid_one = (
            current + sum_rows(right_product(context_rows, mat_out)) + proj_bias[layer_index, 0]
        )
        middle, normed_one, inv_one = layer_norm(
            resid_one, ln_gain[layer_index, 0], ln_shift[layer_index, 0]
        )
        middle_all = gather_rows(middle.astype(bfloat))
        up_here = lax.dynamic_slice_in_dim(
            up_bias[layer_index], tensor_pos * hidden_cols, hidden_cols, 0
        )
        hidden_pre = jnp.dot(jnp.concatenate(middle_all), mat_up, preferred_element_type=single) + up_here
        hidden_bf = (hidden_pre * normal_cdf(hidden_pre)).astype(bfloat)
        resid_two = (
            middle + sum_rows(right_product(hidden_bf, mat_down)) + proj_bias[layer_index, 1]
        )
        output_rows, normed_two, inv_two = layer_norm(
            resid_two, ln_gain[layer_index, 1], ln_shift[layer_index, 1]
        )
        stored.append(
            (
                rows_all,
                qkv_bf,
                context_rows,
                normed_one,
                inv_one,
                middle_all,
                hidden_pre,
                hidden_bf,
                normed_two,
                inv_two,
            )
        )
        current = output_rows
    def scatter_plane(block):
        return lax.psum_scatter(
            block, "dp", scatter_dimension=0, tiled=True, axis_index_groups=PLANE
        )

    upstream = with_neighbour(mix_features(cotangent))
    sums_ffn = []
    both_axes = ("dp", "tensor")
    all_tokens, own_columns = [None] * LAYERS, [None] * LAYERS
    for layer_index in reversed(range(LAYERS)):
        (
            rows_all,
            qkv_bf,
            context_rows,
            normed_one,
            inv_one,
            middle_all,
            hidden_pre,
            hidden_bf,
            normed_two,
            inv_two,
        ) = stored[layer_index]
        mat_qkv, mat_out, mat_up, mat_down = all_weights[layer_index]
        gain_two = jnp.sum((upstream * normed_two)[:own_rows], axis=0)
        shift_two = jnp.sum(upstream[:own_rows], axis=0)
        grad_two = norm_back(upstream, normed_two, inv_two, ln_gain[layer_index, 1])
        bias_two = jnp.sum(grad_two[:own_rows], axis=0)
        grad_ffn_all = gather_rows(grad_two.astype(bfloat))
        grad_hidden = jnp.dot(jnp.concatenate(grad_ffn_all), mat_down, preferred_element_type=single)
        grad_pre = grad_hidden * gelu_slope(hidden_pre)
        grad_pre_bf = grad_pre.astype(bfloat)
        up_term = jnp.sum(grad_pre, axis=0)
        block_ffn = weight_grads((middle_all, grad_pre_bf), (grad_ffn_all, hidden_bf))
        part_sum, block_ffn = sum_rows(right_product(grad_pre_bf, mat_up), block_ffn)
        sums_ffn.append(scatter_plane(block_ffn) if layer_index else sum_owned(block_ffn, "dp", PLANE))
        grad_mid = grad_two + part_sum
        gain_one = jnp.sum((grad_mid * normed_one)[:own_rows], axis=0)
        shift_one = jnp.sum(grad_mid[:own_rows], axis=0)
        grad_one = norm_back(grad_mid, normed_one, inv_one, ln_gain[layer_index, 0])
        bias_one = jnp.sum(grad_one[:own_rows], axis=0)
        grad_attn_all = gather_rows(grad_one.astype(bfloat))
        grad_context = jnp.dot(
            jnp.concatenate(grad_attn_all), mat_out, preferred_element_type=single
        ).astype(bfloat)
        grad_mixed_bf, total = attend_back(qkv_bf, seg_row, seg_col, grad_context)
        if not layer_index:
            grad_mixed_bf, sums_ffn[1] = lax.optimization_barrier((grad_mixed_bf, sums_ffn[1]))
        all_tokens[layer_index] = [gain_one, gain_two, shift_one, shift_two, bias_one, bias_two]
        all_tokens[layer_index] = jnp.concatenate(all_tokens[layer_index])
        own_columns[layer_index] = jnp.concatenate(
            [total[0, :head_cols], total[0, 2 * head_cols :], up_term]
        )
        pairs = ((rows_all, grad_mixed_bf), (grad_attn_all, context_rows))
        if layer_index:
            input_part = right_product(grad_mixed_bf, mat_qkv)
            part_sum, block = sum_rows(input_part, weight_grads(*pairs))
            sums_attn = scatter_plane(block)
        else:
            small = jnp.concatenate(all_tokens + own_columns).reshape(model_width, -1)
            high = small.astype(bfloat)
            low = (small - high.astype(single)).astype(bfloat)
            count = small.shape[1]
            rest = jnp.zeros((model_width, 128 - 2 * count), bfloat)
            sums_last = jnp.concatenate([sums_ffn[0], sums_attn], axis=1)
            extra = jnp.concatenate([high, low, rest], axis=1)
            sums_attn = sum_owned(weight_grads(*pairs, extra=extra), "dp", PLANE)
            sums_last = sum_halves(sums_last, first_half)
            sums_attn, sums_last, grad_mixed_bf = lax.optimization_barrier(
                (sums_attn, sums_last, grad_mixed_bf)
            )
            block_cols = three_cols + head_cols
            small = sums_attn[:, block_cols : block_cols + count]
            small = small + sums_attn[:, block_cols + count : block_cols + 2 * count]
            sums_attn = sums_attn[:, :block_cols]
            small = spread(small.reshape(1, -1), both_axes)
            part_sum, small = sum_rows(right_product(grad_mixed_bf, mat_qkv), small)
        upstream = grad_one + part_sum
    small = small.reshape(2, 16, tensor_count, -1)
    small = jnp.swapaxes(jnp.sum(small, axis=0), 0, 1).reshape(tensor_count, -1)
    token_count = LAYERS * 6 * model_width
    over_tokens = jnp.sum(small[:, :token_count], axis=0).reshape(LAYERS, 3, 2, model_width)
    over_tokens = unmix_features(over_tokens)
    over_columns = jnp.swapaxes(small[:, token_count:].reshape(tensor_count, LAYERS, -1), 0, 1)
    total_qv = over_columns[:, :, : 2 * head_cols].reshape(LAYERS, tensor_count, 2, head_cols)
    total_qv = jnp.swapaxes(total_qv, 1, 2).reshape(LAYERS, 2, model_width)
    total_up = over_columns[:, :, 2 * head_cols :].reshape(LAYERS, -1)
    sums_first = sum_halves(
        jnp.concatenate([sums_ffn[1], sums_attn], axis=1), first_half
    )
    cut_out = two_hidden + three_cols
    grad_weights = []
    for sums in (sums_first, sums_last):
        grad_weights.append(
            (
                sums[:, two_hidden:cut_out].reshape(owner_rows, 3, head_cols),
                sums[:, cut_out:],
                sums[:, :hidden_cols],
                sums[:, hidden_cols:two_hidden],
            )
        )
    return (
        unmix_features(current[:own_rows]),
        unmix_features(upstream[:own_rows]),
        jnp.stack([part[0] for part in grad_weights]),
        jnp.stack([part[1] for part in grad_weights]),
        jnp.stack([part[2] for part in grad_weights]),
        jnp.stack([part[3] for part in grad_weights]),
        total_qv,
        over_tokens[:, 2],
        total_up,
        over_tokens[:, 0],
        over_tokens[:, 1],
    )


def solution(mesh):
    placed = (
        P(("dp", "tensor"), None),
        P("dp", None),
        P(None, "dp", None, "tensor"),
        P(None, "dp", "tensor"),
        P(None, "dp", "tensor"),
        P(None, "dp", "tensor"),
        P(),
        P(),
        P(),
        P(),
        P(),
        P(("dp", "tensor"), None),
    )
    return jax.shard_map(
        shards,
        mesh=mesh,
        in_specs=placed,
        out_specs=(
            P(("dp", "tensor"), None),
            P(("dp", "tensor"), None),
            P(None, "dp", None, "tensor"),
            P(None, "dp", "tensor"),
            P(None, "dp", "tensor"),
            P(None, "dp", "tensor"),
            P(),
            P(),
            P(),
            P(),
            P(),
        ),
        check_vma=False,
    )
```

```python
import jax
import jax.numpy as jnp
from jax import lax
from jax.experimental import pallas as pl
from jax.experimental.pallas import tpu as pltpu
from jax.sharding import PartitionSpec as P

HEADS = 16
HEAD_DIM = 64
LAYERS = 2


NORM_EPS = 1e-12
HALF_ROOT = 0.7071067811865476
DENSITY = 0.3989422804014327


def normal_cdf(values):
    return 0.5 * (1.0 + lax.erf(values * HALF_ROOT))


def gelu_slope(values):
    return normal_cdf(values) + values * jnp.exp(-0.5 * values * values) * DENSITY


def layer_norm(activations, gain_row, shift_row):
    center = activations - jnp.mean(activations, axis=-1, keepdims=True)
    inv_std = lax.rsqrt(jnp.mean(center * center, axis=-1, keepdims=True) + NORM_EPS)
    normed = center * inv_std
    return (normed * gain_row + shift_row, normed, inv_std)


def norm_back(upstream, normed, inv_std, gain_row):
    scaled = upstream * gain_row
    return inv_std * (
        scaled
        - jnp.mean(scaled, axis=-1, keepdims=True)
        - normed * jnp.mean(scaled * normed, axis=-1, keepdims=True)
    )


def attention_weights(qkv_ref, seg_row, seg_col, head):
    width = HEADS // 4 * HEAD_DIM
    cols = [slice(third * width + head * HEAD_DIM, third * width + (head + 1) * HEAD_DIM) for third in range(3)]
    query = qkv_ref[:, cols[0]] * jnp.bfloat16(HEAD_DIM**-0.5)
    key = qkv_ref[:, cols[1]]
    value = qkv_ref[:, cols[2]]
    scores = right_product(key, query)
    scores = jnp.where(seg_col[...] == seg_row[...], scores, -1e30)
    raised = jnp.exp(scores - jnp.max(scores, axis=0, keepdims=True))
    probs = raised * (1.0 / jnp.sum(raised, axis=0, keepdims=True))
    return query, key, value, probs, cols


def attend_kernel(qkv_ref, seg_row, seg_col, context_ref):
    for head in range(context_ref.shape[1] // HEAD_DIM):
        _, _, value, probs, cols = attention_weights(qkv_ref, seg_row, seg_col, head)
        context = outer_sum(value, probs.astype(jnp.bfloat16))
        context_ref[:, cols[0]] = context.T.astype(jnp.bfloat16)


def attend_back_kernel(qkv_ref, seg_row, seg_col, grad_ref, mixed_ref, total_ref):
    total_ref[...] = jnp.zeros_like(total_ref)
    for head in range(grad_ref.shape[1] // HEAD_DIM):
        query, key, value, probs, cols = attention_weights(qkv_ref, seg_row, seg_col, head)
        grad = grad_ref[:, cols[0]]
        grad_probs = right_product(value, grad)
        row_dot = jnp.sum(probs * grad_probs, axis=0, keepdims=True)
        grad_scores = (probs * (grad_probs - row_dot)).astype(jnp.bfloat16)
        grad_query = outer_sum(key, grad_scores).T * (HEAD_DIM**-0.5)
        grad_key = jnp.dot(grad_scores, query, preferred_element_type=jnp.float32)
        grad_value = jnp.dot(
            probs.astype(jnp.bfloat16), grad, preferred_element_type=jnp.float32
        )
        for col, part in zip(cols, (grad_query, grad_key, grad_value)):
            mixed_ref[:, col] = part.astype(jnp.bfloat16)
            total_ref[0:1, col] = jnp.sum(part, axis=0, keepdims=True)


def attention_cost(rows, cols, products, moved):
    return pl.CostEstimate(
        flops=2 * products * rows * rows * (cols // 3),
        transcendentals=rows * rows * (cols // 3 // HEAD_DIM),
        bytes_accessed=2 * rows * moved,
    )


def attend(qkv_bf, seg_row, seg_col):
    rows, cols = qkv_bf.shape
    return pl.pallas_call(
        attend_kernel,
        out_shape=jax.ShapeDtypeStruct((rows, cols // 3), jnp.bfloat16),
        cost_estimate=attention_cost(rows, cols, 2, cols + cols // 3),
    )(qkv_bf, seg_row, seg_col)


def attend_back(qkv_bf, seg_row, seg_col, grad_context):
    rows, cols = qkv_bf.shape
    return pl.pallas_call(
        attend_back_kernel,
        out_shape=(
            jax.ShapeDtypeStruct((rows, cols), jnp.bfloat16),
            jax.ShapeDtypeStruct((8, cols), jnp.float32),
        ),
        cost_estimate=attention_cost(rows, cols, 5, 2 * cols + cols // 3),
    )(qkv_bf, seg_row, seg_col, grad_context)


def right_product(left_side, right_side):
    return lax.dot_general(
        left_side, right_side, (((1,), (1,)), ((), ())), preferred_element_type=jnp.float32
    )


def outer_sum(left_side, right_side):
    return lax.dot_general(
        left_side, right_side, (((0,), (0,)), ((), ())), preferred_element_type=jnp.float32
    )


def weight_grads_kernel(*refs):
    result = refs[-1]
    first = 0
    left_over = len(refs) % 3
    if left_over == 2:
        extra_ref = refs[-2]
        result[:, result.shape[1] - extra_ref.shape[1] :] = extra_ref[...]
        refs = refs[:-2] + refs[-1:]
    for near_ref, far_ref, right_ref in zip(refs[0:-1:3], refs[1:-1:3], refs[2:-1:3]):
        last = first + right_ref.shape[1]
        half = near_ref.shape[0]
        block = outer_sum(near_ref[...], right_ref[:half, :])
        block = block + outer_sum(far_ref[...], right_ref[half:, :])
        result[:, first:last] = block.astype(jnp.bfloat16)
        first = last


def weight_grads(*pairs, extra=None):
    tile = 256
    half, width = pairs[0][0][0].shape
    total = sum(right.shape[1] for _, right in pairs)
    specs, operands = [], []
    for left, right in pairs:
        specs += [pl.BlockSpec((half, tile), lambda i: (0, i))] * 2
        specs.append(pl.BlockSpec(right.shape, lambda i: (0, 0)))
        operands += [left[0], left[1], right]
    flops = 4 * half * width * total
    moved = sum(2 * operand.size for operand in operands) + 2 * width * total
    if extra is not None:
        specs.append(pl.BlockSpec((tile, extra.shape[1]), lambda i: (i, 0)))
        operands.append(extra)
        total += extra.shape[1]
    return pl.pallas_call(
        weight_grads_kernel,
        grid=(width // tile,),
        in_specs=specs,
        out_specs=pl.BlockSpec((tile, total), lambda i: (i, 0)),
        out_shape=jax.ShapeDtypeStruct((width, total), jnp.bfloat16),
        cost_estimate=pl.CostEstimate(flops=flops, transcendentals=0, bytes_accessed=moved),
    )(*operands)


def swap(values, bit):
    return lax.ppermute(values, "tensor", [(i, i ^ bit) for i in range(4)])


def with_neighbour(own):
    return jnp.concatenate([own, swap(own, 2)], axis=0)


def gather_rows(pair):
    return pair, swap(pair, 1)


def sum_rows(partial_sum, held=None):
    half = partial_sum.shape[0] // 2
    quarter = half // 2
    part = partial_sum.astype(jnp.bfloat16)
    both = part[:half].astype(jnp.float32) + swap(part[half:], 1).astype(jnp.float32)
    across = swap(both.astype(jnp.bfloat16), 2)
    if held is not None:
        across, held = lax.optimization_barrier((across, held))
    across = jnp.concatenate([across[quarter:], across[:quarter]], axis=0)
    total = both + across.astype(jnp.float32)
    return total if held is None else (total, held)


PLANE = [[half * 16 + place for place in range(16)] for half in range(2)]


def swap_half(values):
    return lax.ppermute(values, "dp", [(i, i ^ 16) for i in range(32)])


def mix_features(values):
    lead = values.shape[:-1]
    values = values.reshape(lead + (2, 16, 32))
    return jnp.swapaxes(values, -3, -2).reshape(lead + (1024,))


def unmix_features(values):
    lead = values.shape[:-1]
    values = values.reshape(lead + (16, 2, 32))
    return jnp.swapaxes(values, -3, -2).reshape(lead + (1024,))


def pair_halves(shard, first_half):
    other = swap_half(shard)
    return jnp.where(
        first_half, jnp.concatenate([shard, other]), jnp.concatenate([other, shard])
    )


def spread(shard, axes, groups=None):
    count = lax.axis_size(axes) if groups is None else len(groups[0])
    copies = jnp.broadcast_to(shard[None], (count,) + shard.shape)
    copies = copies.reshape((count * shard.shape[0],) + shard.shape[1:])
    return lax.all_to_all(copies, axes, 0, 0, tiled=True, axis_index_groups=groups)


def sum_owned(partial_sum, axes, groups=None):
    count = lax.axis_size(axes) if groups is None else len(groups[0])
    pieces = lax.all_to_all(partial_sum, axes, 0, 0, tiled=True, axis_index_groups=groups)
    pieces = pieces.reshape((count, -1) + partial_sum.shape[1:])
    return jnp.sum(pieces.astype(jnp.float32), axis=0)


def sum_halves(pair, first_half):
    rows = pair.shape[0] // 2
    own = jnp.where(first_half, pair[:rows], pair[rows:])
    other = jnp.where(first_half, pair[rows:], pair[:rows])
    return own.astype(jnp.float32) + swap_half(other.astype(jnp.bfloat16)).astype(jnp.float32)


def shards(
    hidden_in,
    segments,
    w_qkv,
    w_out,
    w_up,
    w_down,
    qv_bias,
    proj_bias,
    up_bias,
    ln_gain,
    ln_shift,
    cotangent,
):
    single = jnp.float32
    bfloat = jnp.bfloat16
    model_width = hidden_in.shape[1]
    tensor_count = lax.axis_size("tensor")
    tensor_pos = lax.axis_index("tensor")
    head_count = HEADS // tensor_count
    head_cols = head_count * HEAD_DIM
    hidden_cols = w_up.shape[2]
    seq_count, seq_length = segments.shape
    all_rows = seq_count * seq_length
    owner_rows = model_width // lax.axis_size("dp")
    own_rows = hidden_in.shape[0]
    three_cols = 3 * head_cols
    seg_local = jnp.concatenate(
        [
            lax.dynamic_slice_in_dim(segments, (tensor_pos ^ bit) * own_rows, own_rows, 1)
            for bit in (0, 2, 1, 3)
        ],
        axis=1,
    )

    seg_row, seg_col = seg_local, seg_local.reshape(-1, 1)

    def shard_of(layer_index):
        return (
            w_qkv[layer_index].reshape(owner_rows, three_cols),
            w_out[layer_index],
            w_up[layer_index],
            w_down[layer_index],
        )

    first_half = lax.axis_index("dp") < 16
    first, second = shard_of(0), shard_of(1)
    early = jnp.concatenate(first[:2], axis=1)
    middle_part = jnp.concatenate(first[2:] + second[:2], axis=1)
    late = jnp.concatenate(second[2:], axis=1)
    early = spread(early, "dp").reshape(2, 16, owner_rows, -1)
    early = jnp.swapaxes(early, 0, 1).reshape(model_width, -1)

    def gather_plane(shard):
        return lax.all_gather(shard, "dp", axis=0, tiled=True, axis_index_groups=PLANE)

    middle_part = gather_plane(pair_halves(middle_part, first_half))
    late = gather_plane(pair_halves(late, first_half))
    two_hidden = 2 * hidden_cols
    all_weights = (
        (
            early[:, :three_cols],
            early[:, three_cols:],
            middle_part[:, :hidden_cols],
            middle_part[:, hidden_cols:two_hidden],
        ),
        (
            middle_part[:, two_hidden : two_hidden + three_cols],
            middle_part[:, two_hidden + three_cols :],
            late[:, :hidden_cols],
            late[:, hidden_cols:],
        ),
    )
    proj_bias = mix_features(proj_bias)
    ln_gain = mix_features(ln_gain)
    ln_shift = mix_features(ln_shift)

    current = with_neighbour(mix_features(hidden_in))
    stored = []
    for layer_index in range(LAYERS):
        mat_qkv, mat_out, mat_up, mat_down = all_weights[layer_index]
        rows_all = gather_rows(current.astype(bfloat))
        mixed_rows = jnp.dot(
            jnp.concatenate(rows_all), mat_qkv, preferred_element_type=single
        )
        bias_here = lax.dynamic_slice_in_dim(
            qv_bias[layer_index], tensor_pos * head_cols, head_cols, 1
        )
        bias_three = jnp.concatenate(
            [bias_here[0], jnp.zeros((head_cols,), single), bias_here[1]]
        )
        qkv_bf = (mixed_rows + bias_three).astype(bfloat)
        context_rows = attend(qkv_bf, seg_row, seg_col)
        resid_one = (
            current + sum_rows(right_product(context_rows, mat_out)) + proj_bias[layer_index, 0]
        )
        middle, normed_one, inv_one = layer_norm(
            resid_one, ln_gain[layer_index, 0], ln_shift[layer_index, 0]
        )
        middle_all = gather_rows(middle.astype(bfloat))
        up_here = lax.dynamic_slice_in_dim(
            up_bias[layer_index], tensor_pos * hidden_cols, hidden_cols, 0
        )
        hidden_pre = jnp.dot(jnp.concatenate(middle_all), mat_up, preferred_element_type=single) + up_here
        hidden_bf = (hidden_pre * normal_cdf(hidden_pre)).astype(bfloat)
        resid_two = (
            middle + sum_rows(right_product(hidden_bf, mat_down)) + proj_bias[layer_index, 1]
        )
        output_rows, normed_two, inv_two = layer_norm(
            resid_two, ln_gain[layer_index, 1], ln_shift[layer_index, 1]
        )
        stored.append(
            (
                rows_all,
                qkv_bf,
                context_rows,
                normed_one,
                inv_one,
                middle_all,
                hidden_pre,
                hidden_bf,
                normed_two,
                inv_two,
            )
        )
        current = output_rows
    upstream = with_neighbour(mix_features(cotangent))
    sums_ffn = []
    both_axes = ("dp", "tensor")
    all_tokens, own_columns = [None] * LAYERS, [None] * LAYERS
    for layer_index in reversed(range(LAYERS)):
        (
            rows_all,
            qkv_bf,
            context_rows,
            normed_one,
            inv_one,
            middle_all,
            hidden_pre,
            hidden_bf,
            normed_two,
            inv_two,
        ) = stored[layer_index]
        mat_qkv, mat_out, mat_up, mat_down = all_weights[layer_index]
        gain_two = jnp.sum((upstream * normed_two)[:own_rows], axis=0)
        shift_two = jnp.sum(upstream[:own_rows], axis=0)
        grad_two = norm_back(upstream, normed_two, inv_two, ln_gain[layer_index, 1])
        bias_two = jnp.sum(grad_two[:own_rows], axis=0)
        grad_ffn_all = gather_rows(grad_two.astype(bfloat))
        grad_hidden = jnp.dot(jnp.concatenate(grad_ffn_all), mat_down, preferred_element_type=single)
        grad_pre = grad_hidden * gelu_slope(hidden_pre)
        grad_pre_bf = grad_pre.astype(bfloat)
        up_term = jnp.sum(grad_pre, axis=0)
        block_ffn = weight_grads(
            (middle_all, grad_pre_bf),
            (grad_ffn_all, hidden_bf),
            extra=None if layer_index else block_last,
        )
        part_sum, block_ffn = sum_rows(right_product(grad_pre_bf, mat_up), block_ffn)
        sums_ffn.append(
            lax.psum_scatter(
                block_ffn, "dp", scatter_dimension=0, tiled=True, axis_index_groups=PLANE
            )
        )
        grad_mid = grad_two + part_sum
        gain_one = jnp.sum((grad_mid * normed_one)[:own_rows], axis=0)
        shift_one = jnp.sum(grad_mid[:own_rows], axis=0)
        grad_one = norm_back(grad_mid, normed_one, inv_one, ln_gain[layer_index, 0])
        bias_one = jnp.sum(grad_one[:own_rows], axis=0)
        grad_attn_all = gather_rows(grad_one.astype(bfloat))
        grad_context = jnp.dot(
            jnp.concatenate(grad_attn_all), mat_out, preferred_element_type=single
        ).astype(bfloat)
        grad_mixed_bf, total = attend_back(qkv_bf, seg_row, seg_col, grad_context)
        all_tokens[layer_index] = [gain_one, gain_two, shift_one, shift_two, bias_one, bias_two]
        all_tokens[layer_index] = jnp.concatenate(all_tokens[layer_index])
        own_columns[layer_index] = jnp.concatenate(
            [total[0, :head_cols], total[0, 2 * head_cols :], up_term]
        )
        pairs = ((rows_all, grad_mixed_bf), (grad_attn_all, context_rows))
        if layer_index:
            input_part = right_product(grad_mixed_bf, mat_qkv)
            part_sum, block_last = sum_rows(input_part, weight_grads(*pairs))
        else:
            small = jnp.concatenate(all_tokens + own_columns).reshape(model_width, -1)
            high = small.astype(bfloat)
            low = (small - high.astype(single)).astype(bfloat)
            count = small.shape[1]
            rest = jnp.zeros((model_width, 128 - 2 * count), bfloat)
            extra = jnp.concatenate([high, low, rest], axis=1)
            sums_attn = sum_owned(weight_grads(*pairs, extra=extra), "dp", PLANE)
            sums_attn, grad_mixed_bf = lax.optimization_barrier((sums_attn, grad_mixed_bf))
            block_cols = three_cols + head_cols
            small = sums_attn[:, block_cols : block_cols + count]
            small = small + sums_attn[:, block_cols + count : block_cols + 2 * count]
            sums_attn = sums_attn[:, :block_cols]
            small = spread(small.reshape(1, -1), both_axes)
            part_sum, small = sum_rows(right_product(grad_mixed_bf, mat_qkv), small)
        upstream = grad_one + part_sum
    small = small.reshape(2, 16, tensor_count, -1)
    small = jnp.swapaxes(jnp.sum(small, axis=0), 0, 1).reshape(tensor_count, -1)
    token_count = LAYERS * 6 * model_width
    over_tokens = jnp.sum(small[:, :token_count], axis=0).reshape(LAYERS, 3, 2, model_width)
    over_tokens = unmix_features(over_tokens)
    over_columns = jnp.swapaxes(small[:, token_count:].reshape(tensor_count, LAYERS, -1), 0, 1)
    total_qv = over_columns[:, :, : 2 * head_cols].reshape(LAYERS, tensor_count, 2, head_cols)
    total_qv = jnp.swapaxes(total_qv, 1, 2).reshape(LAYERS, 2, model_width)
    total_up = over_columns[:, :, 2 * head_cols :].reshape(LAYERS, -1)
    early = sum_halves(
        jnp.concatenate([sums_ffn[0].astype(single), sums_attn], axis=1), first_half
    )
    late = sum_halves(sums_ffn[1], first_half)
    sums_first = jnp.concatenate([late[:, :two_hidden], early[:, two_hidden:]], axis=1)
    sums_last = jnp.concatenate([early[:, :two_hidden], late[:, two_hidden:]], axis=1)
    cut_out = two_hidden + three_cols
    grad_weights = []
    for sums in (sums_first, sums_last):
        grad_weights.append(
            (
                sums[:, two_hidden:cut_out].reshape(owner_rows, 3, head_cols),
                sums[:, cut_out:],
                sums[:, :hidden_cols],
                sums[:, hidden_cols:two_hidden],
            )
        )
    return (
        unmix_features(current[:own_rows]),
        unmix_features(upstream[:own_rows]),
        jnp.stack([part[0] for part in grad_weights]),
        jnp.stack([part[1] for part in grad_weights]),
        jnp.stack([part[2] for part in grad_weights]),
        jnp.stack([part[3] for part in grad_weights]),
        total_qv,
        over_tokens[:, 2],
        total_up,
        over_tokens[:, 0],
        over_tokens[:, 1],
    )


def solution(mesh):
    placed = (
        P(("dp", "tensor"), None),
        P("dp", None),
        P(None, "dp", None, "tensor"),
        P(None, "dp", "tensor"),
        P(None, "dp", "tensor"),
        P(None, "dp", "tensor"),
        P(),
        P(),
        P(),
        P(),
        P(),
        P(("dp", "tensor"), None),
    )
    return jax.shard_map(
        shards,
        mesh=mesh,
        in_specs=placed,
        out_specs=(
            P(("dp", "tensor"), None),
            P(("dp", "tensor"), None),
            P(None, "dp", None, "tensor"),
            P(None, "dp", "tensor"),
            P(None, "dp", "tensor"),
            P(None, "dp", "tensor"),
            P(),
            P(),
            P(),
            P(),
            P(),
        ),
        check_vma=False,
    )
```

```python
import jax
import jax.numpy as jnp
from jax import lax
from jax.experimental import pallas as pl
from jax.experimental.pallas import tpu as pltpu
from jax.sharding import PartitionSpec as P

HEADS = 16
HEAD_DIM = 64
LAYERS = 2


NORM_EPS = 1e-12
HALF_ROOT = 0.7071067811865476
DENSITY = 0.3989422804014327


def normal_cdf(values):
    return 0.5 * (1.0 + lax.erf(values * HALF_ROOT))


def gelu_slope(values):
    return normal_cdf(values) + values * jnp.exp(-0.5 * values * values) * DENSITY


def layer_norm(activations, gain_row, shift_row):
    center = activations - jnp.mean(activations, axis=-1, keepdims=True)
    inv_std = lax.rsqrt(jnp.mean(center * center, axis=-1, keepdims=True) + NORM_EPS)
    normed = center * inv_std
    return (normed * gain_row + shift_row, normed, inv_std)


def norm_back(upstream, normed, inv_std, gain_row):
    scaled = upstream * gain_row
    return inv_std * (
        scaled
        - jnp.mean(scaled, axis=-1, keepdims=True)
        - normed * jnp.mean(scaled * normed, axis=-1, keepdims=True)
    )


def attention_weights(qkv_ref, seg_row, seg_col, head):
    width = HEADS // 4 * HEAD_DIM
    cols = [slice(third * width + head * HEAD_DIM, third * width + (head + 1) * HEAD_DIM) for third in range(3)]
    query = qkv_ref[:, cols[0]] * jnp.bfloat16(HEAD_DIM**-0.5)
    key = qkv_ref[:, cols[1]]
    value = qkv_ref[:, cols[2]]
    scores = right_product(key, query)
    scores = jnp.where(seg_col[...] == seg_row[...], scores, -1e30)
    raised = jnp.exp(scores - jnp.max(scores, axis=0, keepdims=True))
    probs = raised * (1.0 / jnp.sum(raised, axis=0, keepdims=True))
    return query, key, value, probs, cols


def attend_kernel(qkv_ref, seg_row, seg_col, context_ref):
    for head in range(context_ref.shape[1] // HEAD_DIM):
        _, _, value, probs, cols = attention_weights(qkv_ref, seg_row, seg_col, head)
        context = outer_sum(value, probs.astype(jnp.bfloat16))
        context_ref[:, cols[0]] = context.T.astype(jnp.bfloat16)


def attend_back_kernel(qkv_ref, seg_row, seg_col, grad_ref, mixed_ref, total_ref):
    total_ref[...] = jnp.zeros_like(total_ref)
    for head in range(grad_ref.shape[1] // HEAD_DIM):
        query, key, value, probs, cols = attention_weights(qkv_ref, seg_row, seg_col, head)
        grad = grad_ref[:, cols[0]]
        grad_probs = right_product(value, grad)
        row_dot = jnp.sum(probs * grad_probs, axis=0, keepdims=True)
        grad_scores = (probs * (grad_probs - row_dot)).astype(jnp.bfloat16)
        grad_query = outer_sum(key, grad_scores).T * (HEAD_DIM**-0.5)
        grad_key = jnp.dot(grad_scores, query, preferred_element_type=jnp.float32)
        grad_value = jnp.dot(
            probs.astype(jnp.bfloat16), grad, preferred_element_type=jnp.float32
        )
        for col, part in zip(cols, (grad_query, grad_key, grad_value)):
            mixed_ref[:, col] = part.astype(jnp.bfloat16)
            total_ref[0:1, col] = jnp.sum(part, axis=0, keepdims=True)


def attention_cost(rows, cols, products, moved):
    return pl.CostEstimate(
        flops=2 * products * rows * rows * (cols // 3),
        transcendentals=rows * rows * (cols // 3 // HEAD_DIM),
        bytes_accessed=2 * rows * moved,
    )


def attend(qkv_bf, seg_row, seg_col):
    rows, cols = qkv_bf.shape
    return pl.pallas_call(
        attend_kernel,
        out_shape=jax.ShapeDtypeStruct((rows, cols // 3), jnp.bfloat16),
        cost_estimate=attention_cost(rows, cols, 2, cols + cols // 3),
    )(qkv_bf, seg_row, seg_col)


def attend_back(qkv_bf, seg_row, seg_col, grad_context):
    rows, cols = qkv_bf.shape
    return pl.pallas_call(
        attend_back_kernel,
        out_shape=(
            jax.ShapeDtypeStruct((rows, cols), jnp.bfloat16),
            jax.ShapeDtypeStruct((8, cols), jnp.float32),
        ),
        cost_estimate=attention_cost(rows, cols, 5, 2 * cols + cols // 3),
    )(qkv_bf, seg_row, seg_col, grad_context)


def right_product(left_side, right_side):
    return lax.dot_general(
        left_side, right_side, (((1,), (1,)), ((), ())), preferred_element_type=jnp.float32
    )


def outer_sum(left_side, right_side):
    return lax.dot_general(
        left_side, right_side, (((0,), (0,)), ((), ())), preferred_element_type=jnp.float32
    )


def weight_grads_kernel(*refs):
    result = refs[-1]
    first = 0
    left_over = len(refs) % 3
    if left_over == 2:
        extra_ref = refs[-2]
        result[:, result.shape[1] - extra_ref.shape[1] :] = extra_ref[...]
        refs = refs[:-2] + refs[-1:]
    for near_ref, far_ref, right_ref in zip(refs[0:-1:3], refs[1:-1:3], refs[2:-1:3]):
        last = first + right_ref.shape[1]
        half = near_ref.shape[0]
        block = outer_sum(near_ref[...], right_ref[:half, :])
        block = block + outer_sum(far_ref[...], right_ref[half:, :])
        result[:, first:last] = block.astype(jnp.bfloat16)
        first = last


def weight_grads(*pairs, extra=None):
    tile = 256
    half, width = pairs[0][0][0].shape
    total = sum(right.shape[1] for _, right in pairs)
    specs, operands = [], []
    for left, right in pairs:
        specs += [pl.BlockSpec((half, tile), lambda i: (0, i))] * 2
        specs.append(pl.BlockSpec(right.shape, lambda i: (0, 0)))
        operands += [left[0], left[1], right]
    flops = 4 * half * width * total
    moved = sum(2 * operand.size for operand in operands) + 2 * width * total
    if extra is not None:
        specs.append(pl.BlockSpec((tile, extra.shape[1]), lambda i: (i, 0)))
        operands.append(extra)
        total += extra.shape[1]
    return pl.pallas_call(
        weight_grads_kernel,
        grid=(width // tile,),
        in_specs=specs,
        out_specs=pl.BlockSpec((tile, total), lambda i: (i, 0)),
        out_shape=jax.ShapeDtypeStruct((width, total), jnp.bfloat16),
        cost_estimate=pl.CostEstimate(flops=flops, transcendentals=0, bytes_accessed=moved),
    )(*operands)


def swap(values, bit):
    return lax.ppermute(values, "tensor", [(i, i ^ bit) for i in range(4)])


def with_neighbour(own):
    return jnp.concatenate([own, swap(own, 2)], axis=0)


def gather_rows(pair):
    return pair, swap(pair, 1)


def half_sums(partial_sum, held=None):
    half = partial_sum.shape[0] // 2
    part = partial_sum.astype(jnp.bfloat16)
    both = part[:half].astype(jnp.float32) + swap(part[half:], 1).astype(jnp.float32)
    both = both.astype(jnp.bfloat16)
    across = swap(both, 2)
    if held is not None:
        across, held = lax.optimization_barrier((across, held))
    return both, across, held


def add_halves(both, across):
    quarter = both.shape[0] // 2
    across = jnp.concatenate([across[quarter:], across[:quarter]], axis=0)
    return both.astype(jnp.float32) + across.astype(jnp.float32)


def sum_rows(partial_sum):
    both, across, _ = half_sums(partial_sum)
    return add_halves(both, across)


def norm_back_kernel(
    before_ref, both_ref, across_ref, normed_ref, inv_ref, gain_ref, grad_ref, short_ref, total_ref
):
    rows, width = before_ref.shape
    quarter = rows // 2
    total_ref[...] = jnp.zeros_like(total_ref)
    for half in range(2):
        here = slice(half * quarter, (half + 1) * quarter)
        there = slice((1 - half) * quarter, (2 - half) * quarter)
        upstream = both_ref[here, :].astype(jnp.float32) + across_ref[there, :].astype(jnp.float32)
        upstream = before_ref[here, :] + upstream
        normed = normed_ref[here, :]
        scaled = upstream * gain_ref[...]
        mean = jnp.sum(scaled, axis=1, keepdims=True) * (1.0 / width)
        slope = jnp.sum(scaled * normed, axis=1, keepdims=True) * (1.0 / width)
        grad = inv_ref[here, :] * (scaled - mean - normed * slope)
        grad_ref[here, :] = grad
        short_ref[here, :] = grad.astype(jnp.bfloat16)
        if not half:
            total_ref[0:1, :] = jnp.sum(upstream * normed, axis=0, keepdims=True)
            total_ref[1:2, :] = jnp.sum(upstream, axis=0, keepdims=True)
            total_ref[2:3, :] = jnp.sum(grad, axis=0, keepdims=True)


def norm_back_sum(before, both, across, normed, inv_std, gain_row):
    rows, width = before.shape
    return pl.pallas_call(
        norm_back_kernel,
        out_shape=(
            jax.ShapeDtypeStruct((rows, width), jnp.float32),
            jax.ShapeDtypeStruct((rows, width), jnp.bfloat16),
            jax.ShapeDtypeStruct((8, width), jnp.float32),
        ),
        cost_estimate=pl.CostEstimate(
            flops=16 * rows * width, transcendentals=0, bytes_accessed=18 * rows * width
        ),
    )(before, both, across, normed, inv_std, gain_row.reshape(1, width))


PLANE = [[half * 16 + place for place in range(16)] for half in range(2)]


def swap_half(values):
    return lax.ppermute(values, "dp", [(i, i ^ 16) for i in range(32)])


def mix_features(values):
    lead = values.shape[:-1]
    values = values.reshape(lead + (2, 16, 32))
    return jnp.swapaxes(values, -3, -2).reshape(lead + (1024,))


def unmix_features(values):
    lead = values.shape[:-1]
    values = values.reshape(lead + (16, 2, 32))
    return jnp.swapaxes(values, -3, -2).reshape(lead + (1024,))


def pair_halves(shard, first_half):
    other = swap_half(shard)
    return jnp.where(
        first_half, jnp.concatenate([shard, other]), jnp.concatenate([other, shard])
    )


def spread(shard, axes, groups=None):
    count = lax.axis_size(axes) if groups is None else len(groups[0])
    copies = jnp.broadcast_to(shard[None], (count,) + shard.shape)
    copies = copies.reshape((count * shard.shape[0],) + shard.shape[1:])
    return lax.all_to_all(copies, axes, 0, 0, tiled=True, axis_index_groups=groups)


def sum_owned(partial_sum, axes, groups=None):
    count = lax.axis_size(axes) if groups is None else len(groups[0])
    pieces = lax.all_to_all(partial_sum, axes, 0, 0, tiled=True, axis_index_groups=groups)
    pieces = pieces.reshape((count, -1) + partial_sum.shape[1:])
    return jnp.sum(pieces.astype(jnp.float32), axis=0)


def sum_halves(pair, first_half):
    rows = pair.shape[0] // 2
    own = jnp.where(first_half, pair[:rows], pair[rows:])
    other = jnp.where(first_half, pair[rows:], pair[:rows])
    return own.astype(jnp.float32) + swap_half(other.astype(jnp.bfloat16)).astype(jnp.float32)


def shards(
    hidden_in,
    segments,
    w_qkv,
    w_out,
    w_up,
    w_down,
    qv_bias,
    proj_bias,
    up_bias,
    ln_gain,
    ln_shift,
    cotangent,
):
    single = jnp.float32
    bfloat = jnp.bfloat16
    model_width = hidden_in.shape[1]
    tensor_count = lax.axis_size("tensor")
    tensor_pos = lax.axis_index("tensor")
    head_count = HEADS // tensor_count
    head_cols = head_count * HEAD_DIM
    hidden_cols = w_up.shape[2]
    seq_count, seq_length = segments.shape
    all_rows = seq_count * seq_length
    owner_rows = model_width // lax.axis_size("dp")
    own_rows = hidden_in.shape[0]
    three_cols = 3 * head_cols
    seg_local = jnp.concatenate(
        [
            lax.dynamic_slice_in_dim(segments, (tensor_pos ^ bit) * own_rows, own_rows, 1)
            for bit in (0, 2, 1, 3)
        ],
        axis=1,
    )

    seg_row, seg_col = seg_local, seg_local.reshape(-1, 1)

    def shard_of(layer_index):
        return (
            w_qkv[layer_index].reshape(owner_rows, three_cols),
            w_out[layer_index],
            w_up[layer_index],
            w_down[layer_index],
        )

    first_half = lax.axis_index("dp") < 16
    first, second = shard_of(0), shard_of(1)
    early = jnp.concatenate(first[:2], axis=1)
    middle_part = jnp.concatenate(first[2:] + second[:2], axis=1)
    late = jnp.concatenate(second[2:], axis=1)
    early = spread(early, "dp").reshape(2, 16, owner_rows, -1)
    early = jnp.swapaxes(early, 0, 1).reshape(model_width, -1)

    def gather_plane(shard):
        return lax.all_gather(shard, "dp", axis=0, tiled=True, axis_index_groups=PLANE)

    middle_part = gather_plane(pair_halves(middle_part, first_half))
    late = gather_plane(pair_halves(late, first_half))
    two_hidden = 2 * hidden_cols
    all_weights = (
        (
            early[:, :three_cols],
            early[:, three_cols:],
            middle_part[:, :hidden_cols],
            middle_part[:, hidden_cols:two_hidden],
        ),
        (
            middle_part[:, two_hidden : two_hidden + three_cols],
            middle_part[:, two_hidden + three_cols :],
            late[:, :hidden_cols],
            late[:, hidden_cols:],
        ),
    )
    proj_bias = mix_features(proj_bias)
    ln_gain = mix_features(ln_gain)
    ln_shift = mix_features(ln_shift)

    current = with_neighbour(mix_features(hidden_in))
    stored = []
    for layer_index in range(LAYERS):
        mat_qkv, mat_out, mat_up, mat_down = all_weights[layer_index]
        rows_all = gather_rows(current.astype(bfloat))
        mixed_rows = jnp.dot(
            jnp.concatenate(rows_all), mat_qkv, preferred_element_type=single
        )
        bias_here = lax.dynamic_slice_in_dim(
            qv_bias[layer_index], tensor_pos * head_cols, head_cols, 1
        )
        bias_three = jnp.concatenate(
            [bias_here[0], jnp.zeros((head_cols,), single), bias_here[1]]
        )
        qkv_bf = (mixed_rows + bias_three).astype(bfloat)
        context_rows = attend(qkv_bf, seg_row, seg_col)
        resid_one = (
            current + sum_rows(right_product(context_rows, mat_out)) + proj_bias[layer_index, 0]
        )
        middle, normed_one, inv_one = layer_norm(
            resid_one, ln_gain[layer_index, 0], ln_shift[layer_index, 0]
        )
        middle_all = gather_rows(middle.astype(bfloat))
        up_here = lax.dynamic_slice_in_dim(
            up_bias[layer_index], tensor_pos * hidden_cols, hidden_cols, 0
        )
        hidden_pre = jnp.dot(jnp.concatenate(middle_all), mat_up, preferred_element_type=single) + up_here
        hidden_bf = (hidden_pre * normal_cdf(hidden_pre)).astype(bfloat)
        resid_two = (
            middle + sum_rows(right_product(hidden_bf, mat_down)) + proj_bias[layer_index, 1]
        )
        output_rows, normed_two, inv_two = layer_norm(
            resid_two, ln_gain[layer_index, 1], ln_shift[layer_index, 1]
        )
        stored.append(
            (
                rows_all,
                qkv_bf,
                context_rows,
                normed_one,
                inv_one,
                middle_all,
                hidden_pre,
                hidden_bf,
                normed_two,
                inv_two,
            )
        )
        current = output_rows
    upstream = with_neighbour(mix_features(cotangent))
    sums_ffn = []
    both_axes = ("dp", "tensor")
    all_tokens, own_columns = [None] * LAYERS, [None] * LAYERS
    for layer_index in reversed(range(LAYERS)):
        (
            rows_all,
            qkv_bf,
            context_rows,
            normed_one,
            inv_one,
            middle_all,
            hidden_pre,
            hidden_bf,
            normed_two,
            inv_two,
        ) = stored[layer_index]
        mat_qkv, mat_out, mat_up, mat_down = all_weights[layer_index]
        gain_two = ln_gain[layer_index, 1]
        if layer_index:
            grad_two = norm_back(upstream, normed_two, inv_two, gain_two)
            short_two = grad_two.astype(bfloat)
            own_up = upstream[:own_rows]
            totals_two = [own_up * normed_two[:own_rows], own_up, grad_two[:own_rows]]
            totals_two = jnp.stack([jnp.sum(part, axis=0) for part in totals_two])
        else:
            grad_two, short_two, totals_two = norm_back_sum(
                grad_one, both, across, normed_two, inv_two, gain_two
            )
        grad_ffn_all = gather_rows(short_two)
        grad_hidden = jnp.dot(jnp.concatenate(grad_ffn_all), mat_down, preferred_element_type=single)
        grad_pre = grad_hidden * gelu_slope(hidden_pre)
        grad_pre_bf = grad_pre.astype(bfloat)
        up_term = jnp.sum(grad_pre, axis=0)
        block_ffn = weight_grads(
            (middle_all, grad_pre_bf),
            (grad_ffn_all, hidden_bf),
            extra=None if layer_index else block_last,
        )
        both, across, block_ffn = half_sums(right_product(grad_pre_bf, mat_up), block_ffn)
        sums_ffn.append(
            lax.psum_scatter(
                block_ffn, "dp", scatter_dimension=0, tiled=True, axis_index_groups=PLANE
            )
        )
        grad_one, short_one, totals_one = norm_back_sum(
            grad_two, both, across, normed_one, inv_one, ln_gain[layer_index, 0]
        )
        grad_attn_all = gather_rows(short_one)
        grad_context = jnp.dot(
            jnp.concatenate(grad_attn_all), mat_out, preferred_element_type=single
        ).astype(bfloat)
        grad_mixed_bf, total = attend_back(qkv_bf, seg_row, seg_col, grad_context)
        all_tokens[layer_index] = jnp.stack([totals_one[:3], totals_two[:3]], axis=1).reshape(-1)
        own_columns[layer_index] = jnp.concatenate(
            [total[0, :head_cols], total[0, 2 * head_cols :], up_term]
        )
        pairs = ((rows_all, grad_mixed_bf), (grad_attn_all, context_rows))
        if layer_index:
            input_part = right_product(grad_mixed_bf, mat_qkv)
            both, across, block_last = half_sums(input_part, weight_grads(*pairs))
        else:
            small = jnp.concatenate(all_tokens + own_columns).reshape(model_width, -1)
            high = small.astype(bfloat)
            low = (small - high.astype(single)).astype(bfloat)
            count = small.shape[1]
            rest = jnp.zeros((model_width, 128 - 2 * count), bfloat)
            extra = jnp.concatenate([high, low, rest], axis=1)
            sums_attn = sum_owned(weight_grads(*pairs, extra=extra), "dp", PLANE)
            sums_attn, grad_mixed_bf = lax.optimization_barrier((sums_attn, grad_mixed_bf))
            block_cols = three_cols + head_cols
            small = sums_attn[:, block_cols : block_cols + count]
            small = small + sums_attn[:, block_cols + count : block_cols + 2 * count]
            sums_attn = sums_attn[:, :block_cols]
            small = spread(small.reshape(1, -1), both_axes)
            early = sum_halves(
                jnp.concatenate([sums_ffn[0].astype(single), sums_attn], axis=1), first_half
            )
            both, across, (small, early) = half_sums(
                right_product(grad_mixed_bf, mat_qkv), (small, early)
            )
            upstream = grad_one + add_halves(both, across)
    small = small.reshape(2, 16, tensor_count, -1)
    small = jnp.swapaxes(jnp.sum(small, axis=0), 0, 1).reshape(tensor_count, -1)
    token_count = LAYERS * 6 * model_width
    over_tokens = jnp.sum(small[:, :token_count], axis=0).reshape(LAYERS, 3, 2, model_width)
    over_tokens = unmix_features(over_tokens)
    over_columns = jnp.swapaxes(small[:, token_count:].reshape(tensor_count, LAYERS, -1), 0, 1)
    total_qv = over_columns[:, :, : 2 * head_cols].reshape(LAYERS, tensor_count, 2, head_cols)
    total_qv = jnp.swapaxes(total_qv, 1, 2).reshape(LAYERS, 2, model_width)
    total_up = over_columns[:, :, 2 * head_cols :].reshape(LAYERS, -1)
    late = sum_halves(sums_ffn[1], first_half)
    sums_first = jnp.concatenate([late[:, :two_hidden], early[:, two_hidden:]], axis=1)
    sums_last = jnp.concatenate([early[:, :two_hidden], late[:, two_hidden:]], axis=1)
    cut_out = two_hidden + three_cols
    grad_weights = []
    for sums in (sums_first, sums_last):
        grad_weights.append(
            (
                sums[:, two_hidden:cut_out].reshape(owner_rows, 3, head_cols),
                sums[:, cut_out:],
                sums[:, :hidden_cols],
                sums[:, hidden_cols:two_hidden],
            )
        )
    return (
        unmix_features(current[:own_rows]),
        unmix_features(upstream[:own_rows]),
        jnp.stack([part[0] for part in grad_weights]),
        jnp.stack([part[1] for part in grad_weights]),
        jnp.stack([part[2] for part in grad_weights]),
        jnp.stack([part[3] for part in grad_weights]),
        total_qv,
        over_tokens[:, 2],
        total_up,
        over_tokens[:, 0],
        over_tokens[:, 1],
    )


def solution(mesh):
    placed = (
        P(("dp", "tensor"), None),
        P("dp", None),
        P(None, "dp", None, "tensor"),
        P(None, "dp", "tensor"),
        P(None, "dp", "tensor"),
        P(None, "dp", "tensor"),
        P(),
        P(),
        P(),
        P(),
        P(),
        P(("dp", "tensor"), None),
    )
    return jax.shard_map(
        shards,
        mesh=mesh,
        in_specs=placed,
        out_specs=(
            P(("dp", "tensor"), None),
            P(("dp", "tensor"), None),
            P(None, "dp", None, "tensor"),
            P(None, "dp", "tensor"),
            P(None, "dp", "tensor"),
            P(None, "dp", "tensor"),
            P(),
            P(),
            P(),
            P(),
            P(),
        ),
        check_vma=False,
    )
```

```python
import jax
import jax.numpy as jnp
from jax import lax
from jax.experimental import pallas as pl
from jax.experimental.pallas import tpu as pltpu
from jax.sharding import PartitionSpec as P

HEADS = 16
HEAD_DIM = 64
LAYERS = 2


NORM_EPS = 1e-12
HALF_ROOT = 0.7071067811865476
DENSITY = 0.3989422804014327


def normal_cdf(values):
    return 0.5 * (1.0 + lax.erf(values * HALF_ROOT))


def gelu_slope(values):
    return normal_cdf(values) + values * jnp.exp(-0.5 * values * values) * DENSITY


def layer_norm(activations, gain_row, shift_row):
    center = activations - jnp.mean(activations, axis=-1, keepdims=True)
    inv_std = lax.rsqrt(jnp.mean(center * center, axis=-1, keepdims=True) + NORM_EPS)
    normed = center * inv_std
    return (normed * gain_row + shift_row, normed, inv_std)


def norm_back(upstream, normed, inv_std, gain_row):
    scaled = upstream * gain_row
    return inv_std * (
        scaled
        - jnp.mean(scaled, axis=-1, keepdims=True)
        - normed * jnp.mean(scaled * normed, axis=-1, keepdims=True)
    )


def attention_weights(qkv_ref, seg_row, seg_col, head):
    width = HEADS // 4 * HEAD_DIM
    cols = [slice(third * width + head * HEAD_DIM, third * width + (head + 1) * HEAD_DIM) for third in range(3)]
    query = qkv_ref[:, cols[0]] * jnp.bfloat16(HEAD_DIM**-0.5)
    key = qkv_ref[:, cols[1]]
    value = qkv_ref[:, cols[2]]
    scores = right_product(key, query)
    scores = jnp.where(seg_col[...] == seg_row[...], scores, -1e30)
    raised = jnp.exp(scores - jnp.max(scores, axis=0, keepdims=True))
    probs = raised * (1.0 / jnp.sum(raised, axis=0, keepdims=True))
    return query, key, value, probs, cols


def attend_kernel(qkv_ref, seg_row, seg_col, context_ref):
    for head in range(context_ref.shape[1] // HEAD_DIM):
        _, _, value, probs, cols = attention_weights(qkv_ref, seg_row, seg_col, head)
        context = outer_sum(value, probs.astype(jnp.bfloat16))
        context_ref[:, cols[0]] = context.T.astype(jnp.bfloat16)


def attend_back_kernel(qkv_ref, seg_row, seg_col, grad_ref, mixed_ref, total_ref):
    total_ref[...] = jnp.zeros_like(total_ref)
    for head in range(grad_ref.shape[1] // HEAD_DIM):
        query, key, value, probs, cols = attention_weights(qkv_ref, seg_row, seg_col, head)
        grad = grad_ref[:, cols[0]]
        grad_probs = right_product(value, grad)
        row_dot = jnp.sum(probs * grad_probs, axis=0, keepdims=True)
        grad_scores = (probs * (grad_probs - row_dot)).astype(jnp.bfloat16)
        grad_query = outer_sum(key, grad_scores).T * (HEAD_DIM**-0.5)
        grad_key = jnp.dot(grad_scores, query, preferred_element_type=jnp.float32)
        grad_value = jnp.dot(
            probs.astype(jnp.bfloat16), grad, preferred_element_type=jnp.float32
        )
        for col, part in zip(cols, (grad_query, grad_key, grad_value)):
            mixed_ref[:, col] = part.astype(jnp.bfloat16)
            total_ref[0:1, col] = jnp.sum(part, axis=0, keepdims=True)


def attention_cost(rows, cols, products, moved):
    return pl.CostEstimate(
        flops=2 * products * rows * rows * (cols // 3),
        transcendentals=rows * rows * (cols // 3 // HEAD_DIM),
        bytes_accessed=2 * rows * moved,
    )


def attend(qkv_bf, seg_row, seg_col):
    rows, cols = qkv_bf.shape
    return pl.pallas_call(
        attend_kernel,
        out_shape=jax.ShapeDtypeStruct((rows, cols // 3), jnp.bfloat16),
        cost_estimate=attention_cost(rows, cols, 2, cols + cols // 3),
    )(qkv_bf, seg_row, seg_col)


def attend_back(qkv_bf, seg_row, seg_col, grad_context):
    rows, cols = qkv_bf.shape
    return pl.pallas_call(
        attend_back_kernel,
        out_shape=(
            jax.ShapeDtypeStruct((rows, cols), jnp.bfloat16),
            jax.ShapeDtypeStruct((8, cols), jnp.float32),
        ),
        cost_estimate=attention_cost(rows, cols, 5, 2 * cols + cols // 3),
    )(qkv_bf, seg_row, seg_col, grad_context)


def right_product(left_side, right_side):
    return lax.dot_general(
        left_side, right_side, (((1,), (1,)), ((), ())), preferred_element_type=jnp.float32
    )


def outer_sum(left_side, right_side):
    return lax.dot_general(
        left_side, right_side, (((0,), (0,)), ((), ())), preferred_element_type=jnp.float32
    )


def weight_grads_kernel(*refs):
    result = refs[-1]
    first = 0
    left_over = len(refs) % 3
    if left_over == 2:
        extra_ref = refs[-2]
        result[:, result.shape[1] - extra_ref.shape[1] :] = extra_ref[...]
        refs = refs[:-2] + refs[-1:]
    for near_ref, far_ref, right_ref in zip(refs[0:-1:3], refs[1:-1:3], refs[2:-1:3]):
        last = first + right_ref.shape[1]
        half = near_ref.shape[0]
        block = outer_sum(near_ref[...], right_ref[:half, :])
        block = block + outer_sum(far_ref[...], right_ref[half:, :])
        result[:, first:last] = block.astype(jnp.bfloat16)
        first = last


def weight_grads(*pairs, extra=None):
    tile = 256
    half, width = pairs[0][0][0].shape
    total = sum(right.shape[1] for _, right in pairs)
    specs, operands = [], []
    for left, right in pairs:
        specs += [pl.BlockSpec((half, tile), lambda i: (0, i))] * 2
        specs.append(pl.BlockSpec(right.shape, lambda i: (0, 0)))
        operands += [left[0], left[1], right]
    flops = 4 * half * width * total
    moved = sum(2 * operand.size for operand in operands) + 2 * width * total
    if extra is not None:
        specs.append(pl.BlockSpec((tile, extra.shape[1]), lambda i: (i, 0)))
        operands.append(extra)
        total += extra.shape[1]
    return pl.pallas_call(
        weight_grads_kernel,
        grid=(width // tile,),
        in_specs=specs,
        out_specs=pl.BlockSpec((tile, total), lambda i: (i, 0)),
        out_shape=jax.ShapeDtypeStruct((width, total), jnp.bfloat16),
        cost_estimate=pl.CostEstimate(flops=flops, transcendentals=0, bytes_accessed=moved),
    )(*operands)


def swap(values, bit):
    return lax.ppermute(values, "tensor", [(i, i ^ bit) for i in range(4)])


def with_neighbour(own):
    return jnp.concatenate([own, swap(own, 2)], axis=0)


def gather_rows(pair):
    return pair, swap(pair, 1)


def half_sums(partial_sum, held=None):
    half = partial_sum.shape[0] // 2
    part = partial_sum.astype(jnp.bfloat16)
    both = part[:half].astype(jnp.float32) + swap(part[half:], 1).astype(jnp.float32)
    both = both.astype(jnp.bfloat16)
    across = swap(both, 2)
    if held is not None:
        across, held = lax.optimization_barrier((across, held))
    return both, across, held


def add_halves(both, across):
    quarter = both.shape[0] // 2
    across = jnp.concatenate([across[quarter:], across[:quarter]], axis=0)
    return both.astype(jnp.float32) + across.astype(jnp.float32)


def sum_rows(partial_sum):
    both, across, _ = half_sums(partial_sum)
    return add_halves(both, across)


def norm_back_kernel(
    before_ref, both_ref, across_ref, normed_ref, inv_ref, gain_ref, grad_ref, short_ref, total_ref
):
    rows, width = before_ref.shape
    quarter = rows // 2
    total_ref[...] = jnp.zeros_like(total_ref)
    for half in range(2):
        here = slice(half * quarter, (half + 1) * quarter)
        there = slice((1 - half) * quarter, (2 - half) * quarter)
        upstream = both_ref[here, :].astype(jnp.float32) + across_ref[there, :].astype(jnp.float32)
        upstream = before_ref[here, :] + upstream
        normed = normed_ref[here, :]
        scaled = upstream * gain_ref[...]
        mean = jnp.sum(scaled, axis=1, keepdims=True) * (1.0 / width)
        slope = jnp.sum(scaled * normed, axis=1, keepdims=True) * (1.0 / width)
        grad = inv_ref[here, :] * (scaled - mean - normed * slope)
        grad_ref[here, :] = grad
        short_ref[here, :] = grad.astype(jnp.bfloat16)
        if not half:
            total_ref[0:1, :] = jnp.sum(upstream * normed, axis=0, keepdims=True)
            total_ref[1:2, :] = jnp.sum(upstream, axis=0, keepdims=True)
            total_ref[2:3, :] = jnp.sum(grad, axis=0, keepdims=True)


def norm_back_sum(before, both, across, normed, inv_std, gain_row):
    rows, width = before.shape
    return pl.pallas_call(
        norm_back_kernel,
        out_shape=(
            jax.ShapeDtypeStruct((rows, width), jnp.float32),
            jax.ShapeDtypeStruct((rows, width), jnp.bfloat16),
            jax.ShapeDtypeStruct((8, width), jnp.float32),
        ),
        cost_estimate=pl.CostEstimate(
            flops=16 * rows * width, transcendentals=0, bytes_accessed=18 * rows * width
        ),
    )(before, both, across, normed, inv_std, gain_row.reshape(1, width))


PLANE = [[half * 16 + place for place in range(16)] for half in range(2)]


def swap_half(values):
    return lax.ppermute(values, "dp", [(i, i ^ 16) for i in range(32)])


def mix_features(values):
    lead = values.shape[:-1]
    values = values.reshape(lead + (2, 16, 32))
    return jnp.swapaxes(values, -3, -2).reshape(lead + (1024,))


def unmix_features(values):
    lead = values.shape[:-1]
    values = values.reshape(lead + (16, 2, 32))
    return jnp.swapaxes(values, -3, -2).reshape(lead + (1024,))


def pair_halves(shard, first_half):
    other = swap_half(shard)
    return jnp.where(
        first_half, jnp.concatenate([shard, other]), jnp.concatenate([other, shard])
    )


def spread(shard, axes, groups=None):
    count = lax.axis_size(axes) if groups is None else len(groups[0])
    copies = jnp.broadcast_to(shard[None], (count,) + shard.shape)
    copies = copies.reshape((count * shard.shape[0],) + shard.shape[1:])
    return lax.all_to_all(copies, axes, 0, 0, tiled=True, axis_index_groups=groups)


def sum_owned(partial_sum, axes, groups=None):
    count = lax.axis_size(axes) if groups is None else len(groups[0])
    pieces = lax.all_to_all(partial_sum, axes, 0, 0, tiled=True, axis_index_groups=groups)
    pieces = pieces.reshape((count, -1) + partial_sum.shape[1:])
    return jnp.sum(pieces.astype(jnp.float32), axis=0)


def sum_halves(pair, first_half):
    rows = pair.shape[0] // 2
    own = jnp.where(first_half, pair[:rows], pair[rows:])
    other = jnp.where(first_half, pair[rows:], pair[:rows])
    return own.astype(jnp.float32) + swap_half(other.astype(jnp.bfloat16)).astype(jnp.float32)


def shards(
    hidden_in,
    segments,
    w_qkv,
    w_out,
    w_up,
    w_down,
    qv_bias,
    proj_bias,
    up_bias,
    ln_gain,
    ln_shift,
    cotangent,
):
    single = jnp.float32
    bfloat = jnp.bfloat16
    model_width = hidden_in.shape[1]
    tensor_count = lax.axis_size("tensor")
    tensor_pos = lax.axis_index("tensor")
    head_count = HEADS // tensor_count
    head_cols = head_count * HEAD_DIM
    hidden_cols = w_up.shape[2]
    seq_count, seq_length = segments.shape
    all_rows = seq_count * seq_length
    owner_rows = model_width // lax.axis_size("dp")
    own_rows = hidden_in.shape[0]
    three_cols = 3 * head_cols
    seg_local = jnp.concatenate(
        [
            lax.dynamic_slice_in_dim(segments, (tensor_pos ^ bit) * own_rows, own_rows, 1)
            for bit in (0, 2, 1, 3)
        ],
        axis=1,
    )

    seg_row, seg_col = seg_local, seg_local.reshape(-1, 1)

    def shard_of(layer_index):
        return (
            w_qkv[layer_index].reshape(owner_rows, three_cols),
            w_out[layer_index],
            w_up[layer_index],
            w_down[layer_index],
        )

    first_half = lax.axis_index("dp") < 16
    first, second = shard_of(0), shard_of(1)
    early = jnp.concatenate(first[:2], axis=1)
    middle_part = jnp.concatenate(first[2:] + second[:2], axis=1)
    late = jnp.concatenate(second[2:], axis=1)
    early = spread(early, "dp").reshape(2, 16, owner_rows, -1)
    early = jnp.swapaxes(early, 0, 1).reshape(model_width, -1)

    def gather_plane(shard):
        return lax.all_gather(shard, "dp", axis=0, tiled=True, axis_index_groups=PLANE)

    middle_part = gather_plane(pair_halves(middle_part, first_half))
    late = gather_plane(pair_halves(late, first_half))
    two_hidden = 2 * hidden_cols
    all_weights = (
        (
            early[:, :three_cols],
            early[:, three_cols:],
            middle_part[:, :hidden_cols],
            middle_part[:, hidden_cols:two_hidden],
        ),
        (
            middle_part[:, two_hidden : two_hidden + three_cols],
            middle_part[:, two_hidden + three_cols :],
            late[:, :hidden_cols],
            late[:, hidden_cols:],
        ),
    )
    proj_bias = mix_features(proj_bias)
    ln_gain = mix_features(ln_gain)
    ln_shift = mix_features(ln_shift)

    current = with_neighbour(mix_features(hidden_in))
    stored = []
    for layer_index in range(LAYERS):
        mat_qkv, mat_out, mat_up, mat_down = all_weights[layer_index]
        rows_all = gather_rows(current.astype(bfloat))
        mixed_rows = jnp.dot(
            jnp.concatenate(rows_all), mat_qkv, preferred_element_type=single
        )
        bias_here = lax.dynamic_slice_in_dim(
            qv_bias[layer_index], tensor_pos * head_cols, head_cols, 1
        )
        bias_three = jnp.concatenate(
            [bias_here[0], jnp.zeros((head_cols,), single), bias_here[1]]
        )
        qkv_bf = (mixed_rows + bias_three).astype(bfloat)
        context_rows = attend(qkv_bf, seg_row, seg_col)
        resid_one = (
            current + sum_rows(right_product(context_rows, mat_out)) + proj_bias[layer_index, 0]
        )
        middle, normed_one, inv_one = layer_norm(
            resid_one, ln_gain[layer_index, 0], ln_shift[layer_index, 0]
        )
        middle_all = gather_rows(middle.astype(bfloat))
        up_here = lax.dynamic_slice_in_dim(
            up_bias[layer_index], tensor_pos * hidden_cols, hidden_cols, 0
        )
        hidden_pre = jnp.dot(jnp.concatenate(middle_all), mat_up, preferred_element_type=single) + up_here
        hidden_bf = (hidden_pre * normal_cdf(hidden_pre)).astype(bfloat)
        resid_two = (
            middle + sum_rows(right_product(hidden_bf, mat_down)) + proj_bias[layer_index, 1]
        )
        output_rows, normed_two, inv_two = layer_norm(
            resid_two, ln_gain[layer_index, 1], ln_shift[layer_index, 1]
        )
        stored.append(
            (
                rows_all,
                qkv_bf,
                context_rows,
                normed_one,
                inv_one,
                middle_all,
                hidden_pre,
                hidden_bf,
                normed_two,
                inv_two,
            )
        )
        current = output_rows
    upstream = with_neighbour(mix_features(cotangent))
    sums_ffn = []
    both_axes = ("dp", "tensor")
    all_tokens, own_columns = [None] * LAYERS, [None] * LAYERS
    for layer_index in reversed(range(LAYERS)):
        (
            rows_all,
            qkv_bf,
            context_rows,
            normed_one,
            inv_one,
            middle_all,
            hidden_pre,
            hidden_bf,
            normed_two,
            inv_two,
        ) = stored[layer_index]
        mat_qkv, mat_out, mat_up, mat_down = all_weights[layer_index]
        gain_two = ln_gain[layer_index, 1]
        if layer_index:
            grad_two = norm_back(upstream, normed_two, inv_two, gain_two)
            short_two = grad_two.astype(bfloat)
            own_up = upstream[:own_rows]
            totals_two = [own_up * normed_two[:own_rows], own_up, grad_two[:own_rows]]
            totals_two = jnp.stack([jnp.sum(part, axis=0) for part in totals_two])
        else:
            grad_two, short_two, totals_two = norm_back_sum(
                grad_one, both, across, normed_two, inv_two, gain_two
            )
        grad_ffn_all = gather_rows(short_two)
        grad_hidden = jnp.dot(jnp.concatenate(grad_ffn_all), mat_down, preferred_element_type=single)
        grad_pre = grad_hidden * gelu_slope(hidden_pre)
        grad_pre_bf = grad_pre.astype(bfloat)
        up_term = jnp.sum(grad_pre, axis=0)
        block_ffn = weight_grads(
            (middle_all, grad_pre_bf),
            (grad_ffn_all, hidden_bf),
            extra=None if layer_index else block_last,
        )
        both, across, _ = half_sums(right_product(grad_pre_bf, mat_up), block_ffn)
        sums_ffn.append(
            lax.psum_scatter(
                block_ffn, "dp", scatter_dimension=0, tiled=True, axis_index_groups=PLANE
            )
        )
        grad_one, short_one, totals_one = norm_back_sum(
            grad_two, both, across, normed_one, inv_one, ln_gain[layer_index, 0]
        )
        grad_attn_all = gather_rows(short_one)
        grad_context = jnp.dot(
            jnp.concatenate(grad_attn_all), mat_out, preferred_element_type=single
        ).astype(bfloat)
        grad_mixed_bf, total = attend_back(qkv_bf, seg_row, seg_col, grad_context)
        all_tokens[layer_index] = jnp.stack([totals_one[:3], totals_two[:3]], axis=1).reshape(-1)
        own_columns[layer_index] = jnp.concatenate(
            [total[0, :head_cols], total[0, 2 * head_cols :], up_term]
        )
        pairs = ((rows_all, grad_mixed_bf), (grad_attn_all, context_rows))
        if layer_index:
            input_part = right_product(grad_mixed_bf, mat_qkv)
            both, across, block_last = half_sums(input_part, weight_grads(*pairs))
        else:
            small = jnp.concatenate(all_tokens + own_columns).reshape(model_width, -1)
            high = small.astype(bfloat)
            low = (small - high.astype(single)).astype(bfloat)
            count = small.shape[1]
            rest = jnp.zeros((model_width, 128 - 2 * count), bfloat)
            extra = jnp.concatenate([high, low, rest], axis=1)
            sums_attn = sum_owned(weight_grads(*pairs, extra=extra), "dp", PLANE)
            block_cols = three_cols + head_cols
            small = sums_attn[:, block_cols : block_cols + count]
            small = small + sums_attn[:, block_cols + count : block_cols + 2 * count]
            sums_attn = sums_attn[:, :block_cols]
            both, across, small = half_sums(right_product(grad_mixed_bf, mat_qkv), small)
            small = spread(small.reshape(1, -1), both_axes)
            early = sum_halves(
                jnp.concatenate([sums_ffn[0].astype(single), sums_attn], axis=1), first_half
            )
            small, early = lax.optimization_barrier((small, early))
            upstream = grad_one + add_halves(both, across)
    small = small.reshape(2, 16, tensor_count, -1)
    small = jnp.swapaxes(jnp.sum(small, axis=0), 0, 1).reshape(tensor_count, -1)
    token_count = LAYERS * 6 * model_width
    over_tokens = jnp.sum(small[:, :token_count], axis=0).reshape(LAYERS, 3, 2, model_width)
    over_tokens = unmix_features(over_tokens)
    over_columns = jnp.swapaxes(small[:, token_count:].reshape(tensor_count, LAYERS, -1), 0, 1)
    total_qv = over_columns[:, :, : 2 * head_cols].reshape(LAYERS, tensor_count, 2, head_cols)
    total_qv = jnp.swapaxes(total_qv, 1, 2).reshape(LAYERS, 2, model_width)
    total_up = over_columns[:, :, 2 * head_cols :].reshape(LAYERS, -1)
    late = sum_halves(sums_ffn[1], first_half)
    sums_first = jnp.concatenate([late[:, :two_hidden], early[:, two_hidden:]], axis=1)
    sums_last = jnp.concatenate([early[:, :two_hidden], late[:, two_hidden:]], axis=1)
    cut_out = two_hidden + three_cols
    grad_weights = []
    for sums in (sums_first, sums_last):
        grad_weights.append(
            (
                sums[:, two_hidden:cut_out].reshape(owner_rows, 3, head_cols),
                sums[:, cut_out:],
                sums[:, :hidden_cols],
                sums[:, hidden_cols:two_hidden],
            )
        )
    return (
        unmix_features(current[:own_rows]),
        unmix_features(upstream[:own_rows]),
        jnp.stack([part[0] for part in grad_weights]),
        jnp.stack([part[1] for part in grad_weights]),
        jnp.stack([part[2] for part in grad_weights]),
        jnp.stack([part[3] for part in grad_weights]),
        total_qv,
        over_tokens[:, 2],
        total_up,
        over_tokens[:, 0],
        over_tokens[:, 1],
    )


def solution(mesh):
    placed = (
        P(("dp", "tensor"), None),
        P("dp", None),
        P(None, "dp", None, "tensor"),
        P(None, "dp", "tensor"),
        P(None, "dp", "tensor"),
        P(None, "dp", "tensor"),
        P(),
        P(),
        P(),
        P(),
        P(),
        P(("dp", "tensor"), None),
    )
    return jax.shard_map(
        shards,
        mesh=mesh,
        in_specs=placed,
        out_specs=(
            P(("dp", "tensor"), None),
            P(("dp", "tensor"), None),
            P(None, "dp", None, "tensor"),
            P(None, "dp", "tensor"),
            P(None, "dp", "tensor"),
            P(None, "dp", "tensor"),
            P(),
            P(),
            P(),
            P(),
            P(),
        ),
        check_vma=False,
    )
```

```python
import jax
import jax.numpy as jnp
from jax import lax
from jax.experimental import pallas as pl
from jax.experimental.pallas import tpu as pltpu
from jax.sharding import PartitionSpec as P

HEADS = 16
HEAD_DIM = 64
LAYERS = 2


NORM_EPS = 1e-12
HALF_ROOT = 0.7071067811865476
DENSITY = 0.3989422804014327


def normal_cdf(values):
    return 0.5 * (1.0 + lax.erf(values * HALF_ROOT))


def gelu_slope(values):
    return normal_cdf(values) + values * jnp.exp(-0.5 * values * values) * DENSITY


def layer_norm(activations, gain_row, shift_row):
    center = activations - jnp.mean(activations, axis=-1, keepdims=True)
    inv_std = lax.rsqrt(jnp.mean(center * center, axis=-1, keepdims=True) + NORM_EPS)
    normed = center * inv_std
    return (normed * gain_row + shift_row, normed, inv_std)


def norm_back(upstream, normed, inv_std, gain_row):
    scaled = upstream * gain_row
    return inv_std * (
        scaled
        - jnp.mean(scaled, axis=-1, keepdims=True)
        - normed * jnp.mean(scaled * normed, axis=-1, keepdims=True)
    )


def attention_weights(qkv_ref, seg_row, seg_col, head):
    width = HEADS // 4 * HEAD_DIM
    cols = [slice(third * width + head * HEAD_DIM, third * width + (head + 1) * HEAD_DIM) for third in range(3)]
    query = qkv_ref[:, cols[0]] * jnp.bfloat16(HEAD_DIM**-0.5)
    key = qkv_ref[:, cols[1]]
    value = qkv_ref[:, cols[2]]
    scores = right_product(key, query)
    scores = jnp.where(seg_col[...] == seg_row[...], scores, -1e30)
    raised = jnp.exp(scores - jnp.max(scores, axis=0, keepdims=True))
    probs = raised * (1.0 / jnp.sum(raised, axis=0, keepdims=True))
    return query, key, value, probs, cols


def attend_kernel(qkv_ref, seg_row, seg_col, context_ref):
    for head in range(context_ref.shape[1] // HEAD_DIM):
        _, _, value, probs, cols = attention_weights(qkv_ref, seg_row, seg_col, head)
        context = outer_sum(value, probs.astype(jnp.bfloat16))
        context_ref[:, cols[0]] = context.T.astype(jnp.bfloat16)


def attend_back_kernel(qkv_ref, seg_row, seg_col, grad_ref, mixed_ref, total_ref):
    total_ref[...] = jnp.zeros_like(total_ref)
    for head in range(grad_ref.shape[1] // HEAD_DIM):
        query, key, value, probs, cols = attention_weights(qkv_ref, seg_row, seg_col, head)
        grad = grad_ref[:, cols[0]]
        grad_probs = right_product(value, grad)
        row_dot = jnp.sum(probs * grad_probs, axis=0, keepdims=True)
        grad_scores = (probs * (grad_probs - row_dot)).astype(jnp.bfloat16)
        grad_query = outer_sum(key, grad_scores).T * (HEAD_DIM**-0.5)
        grad_key = jnp.dot(grad_scores, query, preferred_element_type=jnp.float32)
        grad_value = jnp.dot(
            probs.astype(jnp.bfloat16), grad, preferred_element_type=jnp.float32
        )
        for col, part in zip(cols, (grad_query, grad_key, grad_value)):
            mixed_ref[:, col] = part.astype(jnp.bfloat16)
            total_ref[0:1, col] = jnp.sum(part, axis=0, keepdims=True)


def attention_cost(rows, cols, products, moved):
    return pl.CostEstimate(
        flops=2 * products * rows * rows * (cols // 3),
        transcendentals=rows * rows * (cols // 3 // HEAD_DIM),
        bytes_accessed=2 * rows * moved,
    )


def attend(qkv_bf, seg_row, seg_col):
    rows, cols = qkv_bf.shape
    return pl.pallas_call(
        attend_kernel,
        out_shape=jax.ShapeDtypeStruct((rows, cols // 3), jnp.bfloat16),
        cost_estimate=attention_cost(rows, cols, 2, cols + cols // 3),
    )(qkv_bf, seg_row, seg_col)


def attend_back(qkv_bf, seg_row, seg_col, grad_context):
    rows, cols = qkv_bf.shape
    return pl.pallas_call(
        attend_back_kernel,
        out_shape=(
            jax.ShapeDtypeStruct((rows, cols), jnp.bfloat16),
            jax.ShapeDtypeStruct((8, cols), jnp.float32),
        ),
        cost_estimate=attention_cost(rows, cols, 5, 2 * cols + cols // 3),
    )(qkv_bf, seg_row, seg_col, grad_context)


def right_product(left_side, right_side):
    return lax.dot_general(
        left_side, right_side, (((1,), (1,)), ((), ())), preferred_element_type=jnp.float32
    )


def outer_sum(left_side, right_side):
    return lax.dot_general(
        left_side, right_side, (((0,), (0,)), ((), ())), preferred_element_type=jnp.float32
    )


def weight_grads_kernel(*refs):
    result = refs[-1]
    first = 0
    left_over = len(refs) % 3
    if left_over == 2:
        extra_ref = refs[-2]
        result[:, result.shape[1] - extra_ref.shape[1] :] = extra_ref[...]
        refs = refs[:-2] + refs[-1:]
    for near_ref, far_ref, right_ref in zip(refs[0:-1:3], refs[1:-1:3], refs[2:-1:3]):
        last = first + right_ref.shape[1]
        half = near_ref.shape[0]
        block = outer_sum(near_ref[...], right_ref[:half, :])
        block = block + outer_sum(far_ref[...], right_ref[half:, :])
        result[:, first:last] = block.astype(jnp.bfloat16)
        first = last


def weight_grads(*pairs, extra=None):
    tile = 256
    half, width = pairs[0][0][0].shape
    total = sum(right.shape[1] for _, right in pairs)
    specs, operands = [], []
    for left, right in pairs:
        specs += [pl.BlockSpec((half, tile), lambda i: (0, i))] * 2
        specs.append(pl.BlockSpec(right.shape, lambda i: (0, 0)))
        operands += [left[0], left[1], right]
    flops = 4 * half * width * total
    moved = sum(2 * operand.size for operand in operands) + 2 * width * total
    if extra is not None:
        specs.append(pl.BlockSpec((tile, extra.shape[1]), lambda i: (i, 0)))
        operands.append(extra)
        total += extra.shape[1]
    return pl.pallas_call(
        weight_grads_kernel,
        grid=(width // tile,),
        in_specs=specs,
        out_specs=pl.BlockSpec((tile, total), lambda i: (i, 0)),
        out_shape=jax.ShapeDtypeStruct((width, total), jnp.bfloat16),
        cost_estimate=pl.CostEstimate(flops=flops, transcendentals=0, bytes_accessed=moved),
    )(*operands)


def swap(values, bit):
    return lax.ppermute(values, "tensor", [(i, i ^ bit) for i in range(4)])


def with_neighbour(own):
    return jnp.concatenate([own, swap(own, 2)], axis=0)


def gather_rows(pair):
    return pair, swap(pair, 1)


def half_sums(partial_sum, held=None):
    half = partial_sum.shape[0] // 2
    part = partial_sum.astype(jnp.bfloat16)
    both = part[:half].astype(jnp.float32) + swap(part[half:], 1).astype(jnp.float32)
    both = both.astype(jnp.bfloat16)
    across = swap(both, 2)
    if held is not None:
        across, held = lax.optimization_barrier((across, held))
    return both, across, held


def add_halves(both, across):
    quarter = both.shape[0] // 2
    across = jnp.concatenate([across[quarter:], across[:quarter]], axis=0)
    return both.astype(jnp.float32) + across.astype(jnp.float32)


def sum_rows(partial_sum):
    both, across, _ = half_sums(partial_sum)
    return add_halves(both, across)


def norm_back_kernel(
    before_ref, both_ref, across_ref, normed_ref, inv_ref, gain_ref, grad_ref, short_ref, total_ref
):
    rows, width = before_ref.shape
    quarter = rows // 2
    total_ref[...] = jnp.zeros_like(total_ref)
    for half in range(2):
        here = slice(half * quarter, (half + 1) * quarter)
        there = slice((1 - half) * quarter, (2 - half) * quarter)
        upstream = both_ref[here, :].astype(jnp.float32) + across_ref[there, :].astype(jnp.float32)
        upstream = before_ref[here, :] + upstream
        normed = normed_ref[here, :]
        scaled = upstream * gain_ref[...]
        mean = jnp.sum(scaled, axis=1, keepdims=True) * (1.0 / width)
        slope = jnp.sum(scaled * normed, axis=1, keepdims=True) * (1.0 / width)
        grad = inv_ref[here, :] * (scaled - mean - normed * slope)
        grad_ref[here, :] = grad
        short_ref[here, :] = grad.astype(jnp.bfloat16)
        if not half:
            total_ref[0:1, :] = jnp.sum(upstream * normed, axis=0, keepdims=True)
            total_ref[1:2, :] = jnp.sum(upstream, axis=0, keepdims=True)
            total_ref[2:3, :] = jnp.sum(grad, axis=0, keepdims=True)


def norm_back_sum(before, both, across, normed, inv_std, gain_row):
    rows, width = before.shape
    return pl.pallas_call(
        norm_back_kernel,
        out_shape=(
            jax.ShapeDtypeStruct((rows, width), jnp.float32),
            jax.ShapeDtypeStruct((rows, width), jnp.bfloat16),
            jax.ShapeDtypeStruct((8, width), jnp.float32),
        ),
        cost_estimate=pl.CostEstimate(
            flops=16 * rows * width, transcendentals=0, bytes_accessed=18 * rows * width
        ),
    )(before, both, across, normed, inv_std, gain_row.reshape(1, width))


PLANE = [[half * 16 + place for place in range(16)] for half in range(2)]


def swap_half(values):
    return lax.ppermute(values, "dp", [(i, i ^ 16) for i in range(32)])


def mix_features(values):
    lead = values.shape[:-1]
    values = values.reshape(lead + (2, 16, 32))
    return jnp.swapaxes(values, -3, -2).reshape(lead + (1024,))


def unmix_features(values):
    lead = values.shape[:-1]
    values = values.reshape(lead + (16, 2, 32))
    return jnp.swapaxes(values, -3, -2).reshape(lead + (1024,))


def pair_halves(shard, first_half):
    other = swap_half(shard)
    return jnp.where(
        first_half, jnp.concatenate([shard, other]), jnp.concatenate([other, shard])
    )


def spread(shard, axes, groups=None):
    count = lax.axis_size(axes) if groups is None else len(groups[0])
    copies = jnp.broadcast_to(shard[None], (count,) + shard.shape)
    copies = copies.reshape((count * shard.shape[0],) + shard.shape[1:])
    return lax.all_to_all(copies, axes, 0, 0, tiled=True, axis_index_groups=groups)


def sum_owned(partial_sum, axes, groups=None):
    count = lax.axis_size(axes) if groups is None else len(groups[0])
    pieces = lax.all_to_all(partial_sum, axes, 0, 0, tiled=True, axis_index_groups=groups)
    pieces = pieces.reshape((count, -1) + partial_sum.shape[1:])
    return jnp.sum(pieces.astype(jnp.float32), axis=0)


def sum_halves(pair, first_half):
    rows = pair.shape[0] // 2
    own = jnp.where(first_half, pair[:rows], pair[rows:])
    other = jnp.where(first_half, pair[rows:], pair[:rows])
    return own.astype(jnp.float32) + swap_half(other.astype(jnp.bfloat16)).astype(jnp.float32)


def shards(
    hidden_in,
    segments,
    w_qkv,
    w_out,
    w_up,
    w_down,
    qv_bias,
    proj_bias,
    up_bias,
    ln_gain,
    ln_shift,
    cotangent,
):
    single = jnp.float32
    bfloat = jnp.bfloat16
    model_width = hidden_in.shape[1]
    tensor_count = lax.axis_size("tensor")
    tensor_pos = lax.axis_index("tensor")
    head_count = HEADS // tensor_count
    head_cols = head_count * HEAD_DIM
    hidden_cols = w_up.shape[2]
    seq_count, seq_length = segments.shape
    all_rows = seq_count * seq_length
    owner_rows = model_width // lax.axis_size("dp")
    own_rows = hidden_in.shape[0]
    three_cols = 3 * head_cols
    seg_local = jnp.concatenate(
        [
            lax.dynamic_slice_in_dim(segments, (tensor_pos ^ bit) * own_rows, own_rows, 1)
            for bit in (0, 2, 1, 3)
        ],
        axis=1,
    )

    seg_row, seg_col = seg_local, seg_local.reshape(-1, 1)

    def shard_of(layer_index):
        return (
            w_qkv[layer_index].reshape(owner_rows, three_cols),
            w_out[layer_index],
            w_up[layer_index],
            w_down[layer_index],
        )

    first_half = lax.axis_index("dp") < 16
    first, second = shard_of(0), shard_of(1)
    early = jnp.concatenate(first[:2], axis=1)
    middle_part = jnp.concatenate(first[2:] + second[:2], axis=1)
    late = jnp.concatenate(second[2:], axis=1)
    early = spread(early, "dp").reshape(2, 16, owner_rows, -1)
    early = jnp.swapaxes(early, 0, 1).reshape(model_width, -1)

    def gather_plane(shard):
        return lax.all_gather(shard, "dp", axis=0, tiled=True, axis_index_groups=PLANE)

    middle_part = gather_plane(pair_halves(middle_part, first_half))
    late = gather_plane(pair_halves(late, first_half))
    two_hidden = 2 * hidden_cols
    all_weights = (
        (
            early[:, :three_cols],
            early[:, three_cols:],
            middle_part[:, :hidden_cols],
            middle_part[:, hidden_cols:two_hidden],
        ),
        (
            middle_part[:, two_hidden : two_hidden + three_cols],
            middle_part[:, two_hidden + three_cols :],
            late[:, :hidden_cols],
            late[:, hidden_cols:],
        ),
    )
    proj_bias = mix_features(proj_bias)
    ln_gain = mix_features(ln_gain)
    ln_shift = mix_features(ln_shift)

    current = with_neighbour(mix_features(hidden_in))
    cotangent = mix_features(cotangent)
    cotangent_across = swap(cotangent, 2)
    stored = []
    for layer_index in range(LAYERS):
        mat_qkv, mat_out, mat_up, mat_down = all_weights[layer_index]
        rows_all = gather_rows(current.astype(bfloat))
        mixed_rows = jnp.dot(
            jnp.concatenate(rows_all), mat_qkv, preferred_element_type=single
        )
        bias_here = lax.dynamic_slice_in_dim(
            qv_bias[layer_index], tensor_pos * head_cols, head_cols, 1
        )
        bias_three = jnp.concatenate(
            [bias_here[0], jnp.zeros((head_cols,), single), bias_here[1]]
        )
        qkv_bf = (mixed_rows + bias_three).astype(bfloat)
        context_rows = attend(qkv_bf, seg_row, seg_col)
        if not layer_index:
            context_rows, cotangent_across = lax.optimization_barrier(
                (context_rows, cotangent_across)
            )
        resid_one = (
            current + sum_rows(right_product(context_rows, mat_out)) + proj_bias[layer_index, 0]
        )
        middle, normed_one, inv_one = layer_norm(
            resid_one, ln_gain[layer_index, 0], ln_shift[layer_index, 0]
        )
        middle_all = gather_rows(middle.astype(bfloat))
        up_here = lax.dynamic_slice_in_dim(
            up_bias[layer_index], tensor_pos * hidden_cols, hidden_cols, 0
        )
        hidden_pre = jnp.dot(jnp.concatenate(middle_all), mat_up, preferred_element_type=single) + up_here
        hidden_bf = (hidden_pre * normal_cdf(hidden_pre)).astype(bfloat)
        resid_two = (
            middle + sum_rows(right_product(hidden_bf, mat_down)) + proj_bias[layer_index, 1]
        )
        output_rows, normed_two, inv_two = layer_norm(
            resid_two, ln_gain[layer_index, 1], ln_shift[layer_index, 1]
        )
        stored.append(
            (
                rows_all,
                qkv_bf,
                context_rows,
                normed_one,
                inv_one,
                middle_all,
                hidden_pre,
                hidden_bf,
                normed_two,
                inv_two,
            )
        )
        current = output_rows
    upstream = jnp.concatenate([cotangent, cotangent_across])
    sums_ffn = []
    both_axes = ("dp", "tensor")
    all_tokens, own_columns = [None] * LAYERS, [None] * LAYERS
    for layer_index in reversed(range(LAYERS)):
        (
            rows_all,
            qkv_bf,
            context_rows,
            normed_one,
            inv_one,
            middle_all,
            hidden_pre,
            hidden_bf,
            normed_two,
            inv_two,
        ) = stored[layer_index]
        mat_qkv, mat_out, mat_up, mat_down = all_weights[layer_index]
        gain_two = ln_gain[layer_index, 1]
        if layer_index:
            grad_two = norm_back(upstream, normed_two, inv_two, gain_two)
            short_two = grad_two.astype(bfloat)
            own_up = upstream[:own_rows]
            totals_two = [own_up * normed_two[:own_rows], own_up, grad_two[:own_rows]]
            totals_two = jnp.stack([jnp.sum(part, axis=0) for part in totals_two])
        else:
            grad_two, short_two, totals_two = norm_back_sum(
                grad_one, both, across, normed_two, inv_two, gain_two
            )
        grad_ffn_all = gather_rows(short_two)
        grad_hidden = jnp.dot(jnp.concatenate(grad_ffn_all), mat_down, preferred_element_type=single)
        grad_pre = grad_hidden * gelu_slope(hidden_pre)
        grad_pre_bf = grad_pre.astype(bfloat)
        up_term = jnp.sum(grad_pre, axis=0)
        block_ffn = weight_grads(
            (middle_all, grad_pre_bf),
            (grad_ffn_all, hidden_bf),
            extra=None if layer_index else block_last,
        )
        both, across, _ = half_sums(right_product(grad_pre_bf, mat_up), block_ffn)
        sums_ffn.append(
            lax.psum_scatter(
                block_ffn, "dp", scatter_dimension=0, tiled=True, axis_index_groups=PLANE
            )
        )
        grad_one, short_one, totals_one = norm_back_sum(
            grad_two, both, across, normed_one, inv_one, ln_gain[layer_index, 0]
        )
        grad_attn_all = gather_rows(short_one)
        grad_context = jnp.dot(
            jnp.concatenate(grad_attn_all), mat_out, preferred_element_type=single
        ).astype(bfloat)
        grad_mixed_bf, total = attend_back(qkv_bf, seg_row, seg_col, grad_context)
        all_tokens[layer_index] = jnp.stack([totals_one[:3], totals_two[:3]], axis=1).reshape(-1)
        own_columns[layer_index] = jnp.concatenate(
            [total[0, :head_cols], total[0, 2 * head_cols :], up_term]
        )
        pairs = ((rows_all, grad_mixed_bf), (grad_attn_all, context_rows))
        if layer_index:
            input_part = right_product(grad_mixed_bf, mat_qkv)
            both, across, block_last = half_sums(input_part, weight_grads(*pairs))
        else:
            small = jnp.concatenate(all_tokens + own_columns).reshape(model_width, -1)
            high = small.astype(bfloat)
            low = (small - high.astype(single)).astype(bfloat)
            count = small.shape[1]
            rest = jnp.zeros((model_width, 128 - 2 * count), bfloat)
            extra = jnp.concatenate([high, low, rest], axis=1)
            sums_attn = sum_owned(weight_grads(*pairs, extra=extra), "dp", PLANE)
            block_cols = three_cols + head_cols
            small = sums_attn[:, block_cols : block_cols + count]
            small = small + sums_attn[:, block_cols + count : block_cols + 2 * count]
            sums_attn = sums_attn[:, :block_cols]
            both, across, small = half_sums(right_product(grad_mixed_bf, mat_qkv), small)
            small = spread(small.reshape(1, -1), both_axes)
            early = sum_halves(
                jnp.concatenate([sums_ffn[0].astype(single), sums_attn], axis=1), first_half
            )
            small, early = lax.optimization_barrier((small, early))
            upstream = grad_one + add_halves(both, across)
    small = small.reshape(2, 16, tensor_count, -1)
    small = jnp.swapaxes(jnp.sum(small, axis=0), 0, 1).reshape(tensor_count, -1)
    token_count = LAYERS * 6 * model_width
    over_tokens = jnp.sum(small[:, :token_count], axis=0).reshape(LAYERS, 3, 2, model_width)
    over_tokens = unmix_features(over_tokens)
    over_columns = jnp.swapaxes(small[:, token_count:].reshape(tensor_count, LAYERS, -1), 0, 1)
    total_qv = over_columns[:, :, : 2 * head_cols].reshape(LAYERS, tensor_count, 2, head_cols)
    total_qv = jnp.swapaxes(total_qv, 1, 2).reshape(LAYERS, 2, model_width)
    total_up = over_columns[:, :, 2 * head_cols :].reshape(LAYERS, -1)
    late = sum_halves(sums_ffn[1], first_half)
    sums_first = jnp.concatenate([late[:, :two_hidden], early[:, two_hidden:]], axis=1)
    sums_last = jnp.concatenate([early[:, :two_hidden], late[:, two_hidden:]], axis=1)
    cut_out = two_hidden + three_cols
    grad_weights = []
    for sums in (sums_first, sums_last):
        grad_weights.append(
            (
                sums[:, two_hidden:cut_out].reshape(owner_rows, 3, head_cols),
                sums[:, cut_out:],
                sums[:, :hidden_cols],
                sums[:, hidden_cols:two_hidden],
            )
        )
    return (
        unmix_features(current[:own_rows]),
        unmix_features(upstream[:own_rows]),
        jnp.stack([part[0] for part in grad_weights]),
        jnp.stack([part[1] for part in grad_weights]),
        jnp.stack([part[2] for part in grad_weights]),
        jnp.stack([part[3] for part in grad_weights]),
        total_qv,
        over_tokens[:, 2],
        total_up,
        over_tokens[:, 0],
        over_tokens[:, 1],
    )


def solution(mesh):
    placed = (
        P(("dp", "tensor"), None),
        P("dp", None),
        P(None, "dp", None, "tensor"),
        P(None, "dp", "tensor"),
        P(None, "dp", "tensor"),
        P(None, "dp", "tensor"),
        P(),
        P(),
        P(),
        P(),
        P(),
        P(("dp", "tensor"), None),
    )
    return jax.shard_map(
        shards,
        mesh=mesh,
        in_specs=placed,
        out_specs=(
            P(("dp", "tensor"), None),
            P(("dp", "tensor"), None),
            P(None, "dp", None, "tensor"),
            P(None, "dp", "tensor"),
            P(None, "dp", "tensor"),
            P(None, "dp", "tensor"),
            P(),
            P(),
            P(),
            P(),
            P(),
        ),
        check_vma=False,
    )
```

```python
import jax
import jax.numpy as jnp
from jax import lax
from jax.experimental import pallas as pl
from jax.experimental.pallas import tpu as pltpu
from jax.sharding import PartitionSpec as P

HEADS = 16
HEAD_DIM = 64
LAYERS = 2


NORM_EPS = 1e-12
HALF_ROOT = 0.7071067811865476
DENSITY = 0.3989422804014327


def normal_cdf(values):
    return 0.5 * (1.0 + lax.erf(values * HALF_ROOT))


def gelu_slope(values):
    return normal_cdf(values) + values * jnp.exp(-0.5 * values * values) * DENSITY


def layer_norm(activations, gain_row, shift_row):
    center = activations - jnp.mean(activations, axis=-1, keepdims=True)
    inv_std = lax.rsqrt(jnp.mean(center * center, axis=-1, keepdims=True) + NORM_EPS)
    normed = center * inv_std
    return (normed * gain_row + shift_row, normed, inv_std)


def norm_back(upstream, normed, inv_std, gain_row):
    scaled = upstream * gain_row
    return inv_std * (
        scaled
        - jnp.mean(scaled, axis=-1, keepdims=True)
        - normed * jnp.mean(scaled * normed, axis=-1, keepdims=True)
    )


def attention_weights(qkv_ref, seg_row, seg_col, head):
    width = HEADS // 4 * HEAD_DIM
    cols = [slice(third * width + head * HEAD_DIM, third * width + (head + 1) * HEAD_DIM) for third in range(3)]
    query = qkv_ref[:, cols[0]] * jnp.bfloat16(HEAD_DIM**-0.5)
    key = qkv_ref[:, cols[1]]
    value = qkv_ref[:, cols[2]]
    scores = right_product(key, query)
    scores = jnp.where(seg_col[...] == seg_row[...], scores, -1e30)
    raised = jnp.exp(scores - jnp.max(scores, axis=0, keepdims=True))
    probs = raised * (1.0 / jnp.sum(raised, axis=0, keepdims=True))
    return query, key, value, probs, cols


def attend_kernel(qkv_ref, seg_row, seg_col, context_ref):
    for head in range(context_ref.shape[1] // HEAD_DIM):
        _, _, value, probs, cols = attention_weights(qkv_ref, seg_row, seg_col, head)
        context = outer_sum(value, probs.astype(jnp.bfloat16))
        context_ref[:, cols[0]] = context.T.astype(jnp.bfloat16)


def attend_back_kernel(qkv_ref, seg_row, seg_col, grad_ref, mixed_ref, total_ref):
    total_ref[...] = jnp.zeros_like(total_ref)
    for head in range(grad_ref.shape[1] // HEAD_DIM):
        query, key, value, probs, cols = attention_weights(qkv_ref, seg_row, seg_col, head)
        grad = grad_ref[:, cols[0]]
        grad_probs = right_product(value, grad)
        row_dot = jnp.sum(probs * grad_probs, axis=0, keepdims=True)
        grad_scores = (probs * (grad_probs - row_dot)).astype(jnp.bfloat16)
        grad_query = outer_sum(key, grad_scores).T * (HEAD_DIM**-0.5)
        grad_key = jnp.dot(grad_scores, query, preferred_element_type=jnp.float32)
        grad_value = jnp.dot(
            probs.astype(jnp.bfloat16), grad, preferred_element_type=jnp.float32
        )
        for col, part in zip(cols, (grad_query, grad_key, grad_value)):
            mixed_ref[:, col] = part.astype(jnp.bfloat16)
            total_ref[0:1, col] = jnp.sum(part, axis=0, keepdims=True)


def attention_cost(rows, cols, products, moved):
    return pl.CostEstimate(
        flops=2 * products * rows * rows * (cols // 3),
        transcendentals=rows * rows * (cols // 3 // HEAD_DIM),
        bytes_accessed=2 * rows * moved,
    )


def attend(qkv_bf, seg_row, seg_col):
    rows, cols = qkv_bf.shape
    return pl.pallas_call(
        attend_kernel,
        out_shape=jax.ShapeDtypeStruct((rows, cols // 3), jnp.bfloat16),
        cost_estimate=attention_cost(rows, cols, 2, cols + cols // 3),
    )(qkv_bf, seg_row, seg_col)


def attend_back(qkv_bf, seg_row, seg_col, grad_context):
    rows, cols = qkv_bf.shape
    return pl.pallas_call(
        attend_back_kernel,
        out_shape=(
            jax.ShapeDtypeStruct((rows, cols), jnp.bfloat16),
            jax.ShapeDtypeStruct((8, cols), jnp.float32),
        ),
        cost_estimate=attention_cost(rows, cols, 5, 2 * cols + cols // 3),
    )(qkv_bf, seg_row, seg_col, grad_context)


def right_product(left_side, right_side):
    return lax.dot_general(
        left_side, right_side, (((1,), (1,)), ((), ())), preferred_element_type=jnp.float32
    )


def outer_sum(left_side, right_side):
    return lax.dot_general(
        left_side, right_side, (((0,), (0,)), ((), ())), preferred_element_type=jnp.float32
    )


def weight_grads_kernel(*refs):
    result = refs[-1]
    first = 0
    left_over = len(refs) % 3
    if left_over == 2:
        extra_ref = refs[-2]
        result[:, result.shape[1] - extra_ref.shape[1] :] = extra_ref[...]
        refs = refs[:-2] + refs[-1:]
    for near_ref, far_ref, right_ref in zip(refs[0:-1:3], refs[1:-1:3], refs[2:-1:3]):
        last = first + right_ref.shape[1]
        half = near_ref.shape[0]
        block = outer_sum(near_ref[...], right_ref[:half, :])
        block = block + outer_sum(far_ref[...], right_ref[half:, :])
        result[:, first:last] = block.astype(jnp.bfloat16)
        first = last


def weight_grads(*pairs, extra=None):
    tile = 256
    half, width = pairs[0][0][0].shape
    total = sum(right.shape[1] for _, right in pairs)
    specs, operands = [], []
    for left, right in pairs:
        specs += [pl.BlockSpec((half, tile), lambda i: (0, i))] * 2
        specs.append(pl.BlockSpec(right.shape, lambda i: (0, 0)))
        operands += [left[0], left[1], right]
    flops = 4 * half * width * total
    moved = sum(2 * operand.size for operand in operands) + 2 * width * total
    if extra is not None:
        specs.append(pl.BlockSpec((tile, extra.shape[1]), lambda i: (i, 0)))
        operands.append(extra)
        total += extra.shape[1]
    return pl.pallas_call(
        weight_grads_kernel,
        grid=(width // tile,),
        in_specs=specs,
        out_specs=pl.BlockSpec((tile, total), lambda i: (i, 0)),
        out_shape=jax.ShapeDtypeStruct((width, total), jnp.bfloat16),
        cost_estimate=pl.CostEstimate(flops=flops, transcendentals=0, bytes_accessed=moved),
    )(*operands)


def swap(values, bit):
    return lax.ppermute(values, "tensor", [(i, i ^ bit) for i in range(4)])


def with_neighbour(own):
    return jnp.concatenate([own, swap(own, 2)], axis=0)


def gather_rows(pair):
    return pair, swap(pair, 1)


def half_sums(partial_sum, held=None):
    half = partial_sum.shape[0] // 2
    part = partial_sum.astype(jnp.bfloat16)
    both = part[:half].astype(jnp.float32) + swap(part[half:], 1).astype(jnp.float32)
    both = both.astype(jnp.bfloat16)
    across = swap(both, 2)
    if held is not None:
        across, held = lax.optimization_barrier((across, held))
    return both, across, held


def add_halves(both, across):
    quarter = both.shape[0] // 2
    across = jnp.concatenate([across[quarter:], across[:quarter]], axis=0)
    return both.astype(jnp.float32) + across.astype(jnp.float32)


def sum_rows(partial_sum):
    both, across, _ = half_sums(partial_sum)
    return add_halves(both, across)


def norm_back_kernel(
    before_ref, both_ref, across_ref, normed_ref, inv_ref, gain_ref, grad_ref, short_ref, total_ref
):
    rows, width = before_ref.shape
    quarter = rows // 2
    total_ref[...] = jnp.zeros_like(total_ref)
    for half in range(2):
        here = slice(half * quarter, (half + 1) * quarter)
        there = slice((1 - half) * quarter, (2 - half) * quarter)
        upstream = both_ref[here, :].astype(jnp.float32) + across_ref[there, :].astype(jnp.float32)
        upstream = before_ref[here, :] + upstream
        normed = normed_ref[here, :]
        scaled = upstream * gain_ref[...]
        mean = jnp.sum(scaled, axis=1, keepdims=True) * (1.0 / width)
        slope = jnp.sum(scaled * normed, axis=1, keepdims=True) * (1.0 / width)
        grad = inv_ref[here, :] * (scaled - mean - normed * slope)
        grad_ref[here, :] = grad
        short_ref[here, :] = grad.astype(jnp.bfloat16)
        if not half:
            total_ref[0:1, :] = jnp.sum(upstream * normed, axis=0, keepdims=True)
            total_ref[1:2, :] = jnp.sum(upstream, axis=0, keepdims=True)
            total_ref[2:3, :] = jnp.sum(grad, axis=0, keepdims=True)


def norm_back_sum(before, both, across, normed, inv_std, gain_row):
    rows, width = before.shape
    return pl.pallas_call(
        norm_back_kernel,
        out_shape=(
            jax.ShapeDtypeStruct((rows, width), jnp.float32),
            jax.ShapeDtypeStruct((rows, width), jnp.bfloat16),
            jax.ShapeDtypeStruct((8, width), jnp.float32),
        ),
        cost_estimate=pl.CostEstimate(
            flops=16 * rows * width, transcendentals=0, bytes_accessed=18 * rows * width
        ),
    )(before, both, across, normed, inv_std, gain_row.reshape(1, width))


PLANE = [[half * 16 + place for place in range(16)] for half in range(2)]


def swap_half(values):
    return lax.ppermute(values, "dp", [(i, i ^ 16) for i in range(32)])


def mix_features(values):
    lead = values.shape[:-1]
    values = values.reshape(lead + (2, 16, 32))
    return jnp.swapaxes(values, -3, -2).reshape(lead + (1024,))


def unmix_features(values):
    lead = values.shape[:-1]
    values = values.reshape(lead + (16, 2, 32))
    return jnp.swapaxes(values, -3, -2).reshape(lead + (1024,))


def pair_halves(shard, first_half):
    other = swap_half(shard)
    return jnp.where(
        first_half, jnp.concatenate([shard, other]), jnp.concatenate([other, shard])
    )


def spread(shard, axes, groups=None):
    count = lax.axis_size(axes) if groups is None else len(groups[0])
    copies = jnp.broadcast_to(shard[None], (count,) + shard.shape)
    copies = copies.reshape((count * shard.shape[0],) + shard.shape[1:])
    return lax.all_to_all(copies, axes, 0, 0, tiled=True, axis_index_groups=groups)


def sum_owned(partial_sum, axes, groups=None):
    count = lax.axis_size(axes) if groups is None else len(groups[0])
    pieces = lax.all_to_all(partial_sum, axes, 0, 0, tiled=True, axis_index_groups=groups)
    pieces = pieces.reshape((count, -1) + partial_sum.shape[1:])
    return jnp.sum(pieces.astype(jnp.float32), axis=0)


def sum_halves(pair, first_half):
    rows = pair.shape[0] // 2
    own = jnp.where(first_half, pair[:rows], pair[rows:])
    other = jnp.where(first_half, pair[rows:], pair[:rows])
    return own.astype(jnp.float32) + swap_half(other.astype(jnp.bfloat16)).astype(jnp.float32)


def shards(
    hidden_in,
    segments,
    w_qkv,
    w_out,
    w_up,
    w_down,
    qv_bias,
    proj_bias,
    up_bias,
    ln_gain,
    ln_shift,
    cotangent,
):
    single = jnp.float32
    bfloat = jnp.bfloat16
    model_width = hidden_in.shape[1]
    tensor_count = lax.axis_size("tensor")
    tensor_pos = lax.axis_index("tensor")
    head_count = HEADS // tensor_count
    head_cols = head_count * HEAD_DIM
    hidden_cols = w_up.shape[2]
    seq_count, seq_length = segments.shape
    all_rows = seq_count * seq_length
    owner_rows = model_width // lax.axis_size("dp")
    own_rows = hidden_in.shape[0]
    three_cols = 3 * head_cols
    seg_local = jnp.concatenate(
        [
            lax.dynamic_slice_in_dim(segments, (tensor_pos ^ bit) * own_rows, own_rows, 1)
            for bit in (0, 2, 1, 3)
        ],
        axis=1,
    )

    seg_row, seg_col = seg_local, seg_local.reshape(-1, 1)

    def shard_of(layer_index):
        return (
            w_qkv[layer_index].reshape(owner_rows, three_cols),
            w_out[layer_index],
            w_up[layer_index],
            w_down[layer_index],
        )

    first_half = lax.axis_index("dp") < 16
    first, second = shard_of(0), shard_of(1)
    early = jnp.concatenate(first[:2], axis=1)
    middle_part = jnp.concatenate(first[2:] + second[:2], axis=1)
    late = jnp.concatenate(second[2:], axis=1)
    early = spread(early, "dp").reshape(2, 16, owner_rows, -1)
    early = jnp.swapaxes(early, 0, 1).reshape(model_width, -1)

    def gather_plane(shard):
        return lax.all_gather(shard, "dp", axis=0, tiled=True, axis_index_groups=PLANE)

    middle_part = gather_plane(pair_halves(middle_part, first_half))
    late_pair = pair_halves(late, first_half)
    two_hidden = 2 * hidden_cols
    all_weights = [
        (
            early[:, :three_cols],
            early[:, three_cols:],
            middle_part[:, :hidden_cols],
            middle_part[:, hidden_cols:two_hidden],
        ),
        (
            middle_part[:, two_hidden : two_hidden + three_cols],
            middle_part[:, two_hidden + three_cols :],
        ),
    ]
    proj_bias = mix_features(proj_bias)
    ln_gain = mix_features(ln_gain)
    ln_shift = mix_features(ln_shift)

    current = with_neighbour(mix_features(hidden_in))
    cotangent = mix_features(cotangent)
    cotangent_across = swap(cotangent, 2)
    stored = []
    for layer_index in range(LAYERS):
        mat_qkv, mat_out, mat_up, mat_down = all_weights[layer_index]
        rows_all = gather_rows(current.astype(bfloat))
        mixed_rows = jnp.dot(
            jnp.concatenate(rows_all), mat_qkv, preferred_element_type=single
        )
        bias_here = lax.dynamic_slice_in_dim(
            qv_bias[layer_index], tensor_pos * head_cols, head_cols, 1
        )
        bias_three = jnp.concatenate(
            [bias_here[0], jnp.zeros((head_cols,), single), bias_here[1]]
        )
        qkv_bf = (mixed_rows + bias_three).astype(bfloat)
        if not layer_index:
            qkv_bf, late_pair = lax.optimization_barrier((qkv_bf, late_pair))
            late = gather_plane(late_pair)
            all_weights[1] = all_weights[1] + (late[:, :hidden_cols], late[:, hidden_cols:])
        context_rows = attend(qkv_bf, seg_row, seg_col)
        if not layer_index:
            context_rows, cotangent_across = lax.optimization_barrier(
                (context_rows, cotangent_across)
            )
        resid_one = (
            current + sum_rows(right_product(context_rows, mat_out)) + proj_bias[layer_index, 0]
        )
        middle, normed_one, inv_one = layer_norm(
            resid_one, ln_gain[layer_index, 0], ln_shift[layer_index, 0]
        )
        middle_all = gather_rows(middle.astype(bfloat))
        up_here = lax.dynamic_slice_in_dim(
            up_bias[layer_index], tensor_pos * hidden_cols, hidden_cols, 0
        )
        hidden_pre = jnp.dot(jnp.concatenate(middle_all), mat_up, preferred_element_type=single) + up_here
        hidden_bf = (hidden_pre * normal_cdf(hidden_pre)).astype(bfloat)
        resid_two = (
            middle + sum_rows(right_product(hidden_bf, mat_down)) + proj_bias[layer_index, 1]
        )
        output_rows, normed_two, inv_two = layer_norm(
            resid_two, ln_gain[layer_index, 1], ln_shift[layer_index, 1]
        )
        stored.append(
            (
                rows_all,
                qkv_bf,
                context_rows,
                normed_one,
                inv_one,
                middle_all,
                hidden_pre,
                hidden_bf,
                normed_two,
                inv_two,
            )
        )
        current = output_rows
    upstream = jnp.concatenate([cotangent, cotangent_across])
    sums_ffn = []
    both_axes = ("dp", "tensor")
    all_tokens, own_columns = [None] * LAYERS, [None] * LAYERS
    for layer_index in reversed(range(LAYERS)):
        (
            rows_all,
            qkv_bf,
            context_rows,
            normed_one,
            inv_one,
            middle_all,
            hidden_pre,
            hidden_bf,
            normed_two,
            inv_two,
        ) = stored[layer_index]
        mat_qkv, mat_out, mat_up, mat_down = all_weights[layer_index]
        gain_two = ln_gain[layer_index, 1]
        if layer_index:
            grad_two = norm_back(upstream, normed_two, inv_two, gain_two)
            short_two = grad_two.astype(bfloat)
            own_up = upstream[:own_rows]
            totals_two = [own_up * normed_two[:own_rows], own_up, grad_two[:own_rows]]
            totals_two = jnp.stack([jnp.sum(part, axis=0) for part in totals_two])
        else:
            grad_two, short_two, totals_two = norm_back_sum(
                grad_one, both, across, normed_two, inv_two, gain_two
            )
        grad_ffn_all = gather_rows(short_two)
        grad_hidden = jnp.dot(jnp.concatenate(grad_ffn_all), mat_down, preferred_element_type=single)
        grad_pre = grad_hidden * gelu_slope(hidden_pre)
        grad_pre_bf = grad_pre.astype(bfloat)
        up_term = jnp.sum(grad_pre, axis=0)
        block_ffn = weight_grads(
            (middle_all, grad_pre_bf),
            (grad_ffn_all, hidden_bf),
            extra=None if layer_index else block_last,
        )
        both, across, _ = half_sums(right_product(grad_pre_bf, mat_up), block_ffn)
        sums_ffn.append(
            lax.psum_scatter(
                block_ffn, "dp", scatter_dimension=0, tiled=True, axis_index_groups=PLANE
            )
        )
        grad_one, short_one, totals_one = norm_back_sum(
            grad_two, both, across, normed_one, inv_one, ln_gain[layer_index, 0]
        )
        grad_attn_all = gather_rows(short_one)
        grad_context = jnp.dot(
            jnp.concatenate(grad_attn_all), mat_out, preferred_element_type=single
        ).astype(bfloat)
        grad_mixed_bf, total = attend_back(qkv_bf, seg_row, seg_col, grad_context)
        all_tokens[layer_index] = jnp.stack([totals_one[:3], totals_two[:3]], axis=1).reshape(-1)
        own_columns[layer_index] = jnp.concatenate(
            [total[0, :head_cols], total[0, 2 * head_cols :], up_term]
        )
        pairs = ((rows_all, grad_mixed_bf), (grad_attn_all, context_rows))
        if layer_index:
            input_part = right_product(grad_mixed_bf, mat_qkv)
            both, across, block_last = half_sums(input_part, weight_grads(*pairs))
        else:
            small = jnp.concatenate(all_tokens + own_columns).reshape(model_width, -1)
            high = small.astype(bfloat)
            low = (small - high.astype(single)).astype(bfloat)
            count = small.shape[1]
            rest = jnp.zeros((model_width, 128 - 2 * count), bfloat)
            extra = jnp.concatenate([high, low, rest], axis=1)
            sums_attn = sum_owned(weight_grads(*pairs, extra=extra), "dp", PLANE)
            block_cols = three_cols + head_cols
            small = sums_attn[:, block_cols : block_cols + count]
            small = small + sums_attn[:, block_cols + count : block_cols + 2 * count]
            sums_attn = sums_attn[:, :block_cols]
            both, across, small = half_sums(right_product(grad_mixed_bf, mat_qkv), small)
            small = spread(small.reshape(1, -1), both_axes)
            early = sum_halves(
                jnp.concatenate([sums_ffn[0].astype(single), sums_attn], axis=1), first_half
            )
            small, early = lax.optimization_barrier((small, early))
            upstream = grad_one + add_halves(both, across)
    small, sums_ffn[1] = lax.optimization_barrier((small, sums_ffn[1]))
    small = small.reshape(2, 16, tensor_count, -1)
    small = jnp.swapaxes(jnp.sum(small, axis=0), 0, 1).reshape(tensor_count, -1)
    token_count = LAYERS * 6 * model_width
    over_tokens = jnp.sum(small[:, :token_count], axis=0).reshape(LAYERS, 3, 2, model_width)
    over_tokens = unmix_features(over_tokens)
    over_columns = jnp.swapaxes(small[:, token_count:].reshape(tensor_count, LAYERS, -1), 0, 1)
    total_qv = over_columns[:, :, : 2 * head_cols].reshape(LAYERS, tensor_count, 2, head_cols)
    total_qv = jnp.swapaxes(total_qv, 1, 2).reshape(LAYERS, 2, model_width)
    total_up = over_columns[:, :, 2 * head_cols :].reshape(LAYERS, -1)
    late = sum_halves(sums_ffn[1], first_half)
    sums_first = jnp.concatenate([late[:, :two_hidden], early[:, two_hidden:]], axis=1)
    sums_last = jnp.concatenate([early[:, :two_hidden], late[:, two_hidden:]], axis=1)
    cut_out = two_hidden + three_cols
    grad_weights = []
    for sums in (sums_first, sums_last):
        grad_weights.append(
            (
                sums[:, two_hidden:cut_out].reshape(owner_rows, 3, head_cols),
                sums[:, cut_out:],
                sums[:, :hidden_cols],
                sums[:, hidden_cols:two_hidden],
            )
        )
    return (
        unmix_features(current[:own_rows]),
        unmix_features(upstream[:own_rows]),
        jnp.stack([part[0] for part in grad_weights]),
        jnp.stack([part[1] for part in grad_weights]),
        jnp.stack([part[2] for part in grad_weights]),
        jnp.stack([part[3] for part in grad_weights]),
        total_qv,
        over_tokens[:, 2],
        total_up,
        over_tokens[:, 0],
        over_tokens[:, 1],
    )


def solution(mesh):
    placed = (
        P(("dp", "tensor"), None),
        P("dp", None),
        P(None, "dp", None, "tensor"),
        P(None, "dp", "tensor"),
        P(None, "dp", "tensor"),
        P(None, "dp", "tensor"),
        P(),
        P(),
        P(),
        P(),
        P(),
        P(("dp", "tensor"), None),
    )
    return jax.shard_map(
        shards,
        mesh=mesh,
        in_specs=placed,
        out_specs=(
            P(("dp", "tensor"), None),
            P(("dp", "tensor"), None),
            P(None, "dp", None, "tensor"),
            P(None, "dp", "tensor"),
            P(None, "dp", "tensor"),
            P(None, "dp", "tensor"),
            P(),
            P(),
            P(),
            P(),
            P(),
        ),
        check_vma=False,
    )
```

```python
import jax
import jax.numpy as jnp
from jax import lax
from jax.experimental import pallas as pl
from jax.experimental.pallas import tpu as pltpu
from jax.sharding import PartitionSpec as P

HEADS = 16
HEAD_DIM = 64
LAYERS = 2


NORM_EPS = 1e-12
HALF_ROOT = 0.7071067811865476
DENSITY = 0.3989422804014327


def normal_cdf(values):
    return 0.5 * (1.0 + lax.erf(values * HALF_ROOT))


def gelu_slope(values):
    return normal_cdf(values) + values * jnp.exp(-0.5 * values * values) * DENSITY


def layer_norm(activations, gain_row, shift_row):
    center = activations - jnp.mean(activations, axis=-1, keepdims=True)
    inv_std = lax.rsqrt(jnp.mean(center * center, axis=-1, keepdims=True) + NORM_EPS)
    normed = center * inv_std
    return (normed * gain_row + shift_row, normed, inv_std)


def norm_back(upstream, normed, inv_std, gain_row):
    scaled = upstream * gain_row
    return inv_std * (
        scaled
        - jnp.mean(scaled, axis=-1, keepdims=True)
        - normed * jnp.mean(scaled * normed, axis=-1, keepdims=True)
    )


def attention_weights(qkv_ref, seg_row, seg_col, head):
    width = HEADS // 4 * HEAD_DIM
    cols = [slice(third * width + head * HEAD_DIM, third * width + (head + 1) * HEAD_DIM) for third in range(3)]
    query = qkv_ref[:, cols[0]] * jnp.bfloat16(HEAD_DIM**-0.5)
    key = qkv_ref[:, cols[1]]
    value = qkv_ref[:, cols[2]]
    scores = right_product(key, query)
    scores = jnp.where(seg_col[...] == seg_row[...], scores, -1e30)
    raised = jnp.exp(scores - jnp.max(scores, axis=0, keepdims=True))
    probs = raised * (1.0 / jnp.sum(raised, axis=0, keepdims=True))
    return query, key, value, probs, cols


def attend_kernel(qkv_ref, seg_row, seg_col, context_ref):
    for head in range(context_ref.shape[1] // HEAD_DIM):
        _, _, value, probs, cols = attention_weights(qkv_ref, seg_row, seg_col, head)
        context = outer_sum(value, probs.astype(jnp.bfloat16))
        context_ref[:, cols[0]] = context.T.astype(jnp.bfloat16)


def attend_back_kernel(qkv_ref, seg_row, seg_col, grad_ref, mixed_ref, total_ref):
    total_ref[...] = jnp.zeros_like(total_ref)
    for head in range(grad_ref.shape[1] // HEAD_DIM):
        query, key, value, probs, cols = attention_weights(qkv_ref, seg_row, seg_col, head)
        grad = grad_ref[:, cols[0]]
        grad_probs = right_product(value, grad)
        row_dot = jnp.sum(probs * grad_probs, axis=0, keepdims=True)
        grad_scores = (probs * (grad_probs - row_dot)).astype(jnp.bfloat16)
        grad_query = outer_sum(key, grad_scores).T * (HEAD_DIM**-0.5)
        grad_key = jnp.dot(grad_scores, query, preferred_element_type=jnp.float32)
        grad_value = jnp.dot(
            probs.astype(jnp.bfloat16), grad, preferred_element_type=jnp.float32
        )
        for col, part in zip(cols, (grad_query, grad_key, grad_value)):
            mixed_ref[:, col] = part.astype(jnp.bfloat16)
            total_ref[0:1, col] = jnp.sum(part, axis=0, keepdims=True)


def attention_cost(rows, cols, products, moved):
    return pl.CostEstimate(
        flops=2 * products * rows * rows * (cols // 3),
        transcendentals=rows * rows * (cols // 3 // HEAD_DIM),
        bytes_accessed=2 * rows * moved,
    )


def attend(qkv_bf, seg_row, seg_col):
    rows, cols = qkv_bf.shape
    return pl.pallas_call(
        attend_kernel,
        out_shape=jax.ShapeDtypeStruct((rows, cols // 3), jnp.bfloat16),
        cost_estimate=attention_cost(rows, cols, 2, cols + cols // 3),
    )(qkv_bf, seg_row, seg_col)


def attend_back(qkv_bf, seg_row, seg_col, grad_context):
    rows, cols = qkv_bf.shape
    return pl.pallas_call(
        attend_back_kernel,
        out_shape=(
            jax.ShapeDtypeStruct((rows, cols), jnp.bfloat16),
            jax.ShapeDtypeStruct((8, cols), jnp.float32),
        ),
        cost_estimate=attention_cost(rows, cols, 5, 2 * cols + cols // 3),
    )(qkv_bf, seg_row, seg_col, grad_context)


def right_product(left_side, right_side):
    return lax.dot_general(
        left_side, right_side, (((1,), (1,)), ((), ())), preferred_element_type=jnp.float32
    )


def outer_sum(left_side, right_side):
    return lax.dot_general(
        left_side, right_side, (((0,), (0,)), ((), ())), preferred_element_type=jnp.float32
    )


def weight_grads_kernel(*refs):
    result = refs[-1]
    first = 0
    left_over = len(refs) % 3
    if left_over == 2:
        extra_ref = refs[-2]
        result[:, result.shape[1] - extra_ref.shape[1] :] = extra_ref[...]
        refs = refs[:-2] + refs[-1:]
    for near_ref, far_ref, right_ref in zip(refs[0:-1:3], refs[1:-1:3], refs[2:-1:3]):
        last = first + right_ref.shape[1]
        half = near_ref.shape[0]
        block = outer_sum(near_ref[...], right_ref[:half, :])
        block = block + outer_sum(far_ref[...], right_ref[half:, :])
        result[:, first:last] = block.astype(jnp.bfloat16)
        first = last


def weight_grads(*pairs, extra=None):
    tile = 256
    half, width = pairs[0][0][0].shape
    total = sum(right.shape[1] for _, right in pairs)
    specs, operands = [], []
    for left, right in pairs:
        specs += [pl.BlockSpec((half, tile), lambda i: (0, i))] * 2
        specs.append(pl.BlockSpec(right.shape, lambda i: (0, 0)))
        operands += [left[0], left[1], right]
    flops = 4 * half * width * total
    moved = sum(2 * operand.size for operand in operands) + 2 * width * total
    if extra is not None:
        specs.append(pl.BlockSpec((tile, extra.shape[1]), lambda i: (i, 0)))
        operands.append(extra)
        total += extra.shape[1]
    return pl.pallas_call(
        weight_grads_kernel,
        grid=(width // tile,),
        in_specs=specs,
        out_specs=pl.BlockSpec((tile, total), lambda i: (i, 0)),
        out_shape=jax.ShapeDtypeStruct((width, total), jnp.bfloat16),
        cost_estimate=pl.CostEstimate(flops=flops, transcendentals=0, bytes_accessed=moved),
    )(*operands)


def swap(values, bit):
    return lax.ppermute(values, "tensor", [(i, i ^ bit) for i in range(4)])


def with_neighbour(own):
    return jnp.concatenate([own, swap(own, 2)], axis=0)


def gather_rows(pair):
    return pair, swap(pair, 1)


def half_sums(partial_sum, held=None):
    half = partial_sum.shape[0] // 2
    part = partial_sum.astype(jnp.bfloat16)
    both = part[:half].astype(jnp.float32) + swap(part[half:], 1).astype(jnp.float32)
    both = both.astype(jnp.bfloat16)
    across = swap(both, 2)
    if held is not None:
        across, held = lax.optimization_barrier((across, held))
    return both, across, held


def add_halves(both, across):
    quarter = both.shape[0] // 2
    across = jnp.concatenate([across[quarter:], across[:quarter]], axis=0)
    return both.astype(jnp.float32) + across.astype(jnp.float32)


def sum_rows(partial_sum):
    both, across, _ = half_sums(partial_sum)
    return add_halves(both, across)


def norm_back_kernel(
    before_ref, both_ref, across_ref, normed_ref, inv_ref, gain_ref, grad_ref, short_ref, total_ref
):
    rows, width = before_ref.shape
    quarter = rows // 2
    total_ref[...] = jnp.zeros_like(total_ref)
    for half in range(2):
        here = slice(half * quarter, (half + 1) * quarter)
        there = slice((1 - half) * quarter, (2 - half) * quarter)
        upstream = both_ref[here, :].astype(jnp.float32) + across_ref[there, :].astype(jnp.float32)
        upstream = before_ref[here, :] + upstream
        normed = normed_ref[here, :]
        scaled = upstream * gain_ref[...]
        mean = jnp.sum(scaled, axis=1, keepdims=True) * (1.0 / width)
        slope = jnp.sum(scaled * normed, axis=1, keepdims=True) * (1.0 / width)
        grad = inv_ref[here, :] * (scaled - mean - normed * slope)
        grad_ref[here, :] = grad
        short_ref[here, :] = grad.astype(jnp.bfloat16)
        if not half:
            total_ref[0:1, :] = jnp.sum(upstream * normed, axis=0, keepdims=True)
            total_ref[1:2, :] = jnp.sum(upstream, axis=0, keepdims=True)
            total_ref[2:3, :] = jnp.sum(grad, axis=0, keepdims=True)


def norm_back_sum(before, both, across, normed, inv_std, gain_row):
    rows, width = before.shape
    return pl.pallas_call(
        norm_back_kernel,
        out_shape=(
            jax.ShapeDtypeStruct((rows, width), jnp.float32),
            jax.ShapeDtypeStruct((rows, width), jnp.bfloat16),
            jax.ShapeDtypeStruct((8, width), jnp.float32),
        ),
        cost_estimate=pl.CostEstimate(
            flops=16 * rows * width, transcendentals=0, bytes_accessed=18 * rows * width
        ),
    )(before, both, across, normed, inv_std, gain_row.reshape(1, width))


PLANE = [[half * 16 + place for place in range(16)] for half in range(2)]


def swap_half(values):
    return lax.ppermute(values, "dp", [(i, i ^ 16) for i in range(32)])


def mix_features(values):
    lead = values.shape[:-1]
    values = values.reshape(lead + (2, 16, 32))
    return jnp.swapaxes(values, -3, -2).reshape(lead + (1024,))


def unmix_features(values):
    lead = values.shape[:-1]
    values = values.reshape(lead + (16, 2, 32))
    return jnp.swapaxes(values, -3, -2).reshape(lead + (1024,))


def pair_halves(shard, first_half):
    other = swap_half(shard)
    return jnp.where(
        first_half, jnp.concatenate([shard, other]), jnp.concatenate([other, shard])
    )


def spread(shard, axes, groups=None):
    count = lax.axis_size(axes) if groups is None else len(groups[0])
    copies = jnp.broadcast_to(shard[None], (count,) + shard.shape)
    copies = copies.reshape((count * shard.shape[0],) + shard.shape[1:])
    return lax.all_to_all(copies, axes, 0, 0, tiled=True, axis_index_groups=groups)


def sum_owned(partial_sum, axes, groups=None):
    count = lax.axis_size(axes) if groups is None else len(groups[0])
    pieces = lax.all_to_all(partial_sum, axes, 0, 0, tiled=True, axis_index_groups=groups)
    pieces = pieces.reshape((count, -1) + partial_sum.shape[1:])
    return jnp.sum(pieces.astype(jnp.float32), axis=0)


def sum_halves(pair, first_half):
    rows = pair.shape[0] // 2
    own = jnp.where(first_half, pair[:rows], pair[rows:])
    other = jnp.where(first_half, pair[rows:], pair[:rows])
    return own.astype(jnp.float32) + swap_half(other.astype(jnp.bfloat16)).astype(jnp.float32)


def shards(
    hidden_in,
    segments,
    w_qkv,
    w_out,
    w_up,
    w_down,
    qv_bias,
    proj_bias,
    up_bias,
    ln_gain,
    ln_shift,
    cotangent,
):
    single = jnp.float32
    bfloat = jnp.bfloat16
    model_width = hidden_in.shape[1]
    tensor_count = lax.axis_size("tensor")
    tensor_pos = lax.axis_index("tensor")
    head_count = HEADS // tensor_count
    head_cols = head_count * HEAD_DIM
    hidden_cols = w_up.shape[2]
    seq_count, seq_length = segments.shape
    all_rows = seq_count * seq_length
    owner_rows = model_width // lax.axis_size("dp")
    own_rows = hidden_in.shape[0]
    three_cols = 3 * head_cols
    seg_local = jnp.concatenate(
        [
            lax.dynamic_slice_in_dim(segments, (tensor_pos ^ bit) * own_rows, own_rows, 1)
            for bit in (0, 2, 1, 3)
        ],
        axis=1,
    )

    seg_row, seg_col = seg_local, seg_local.reshape(-1, 1)

    def shard_of(layer_index):
        return (
            w_qkv[layer_index].reshape(owner_rows, three_cols),
            w_out[layer_index],
            w_up[layer_index],
            w_down[layer_index],
        )

    first_half = lax.axis_index("dp") < 16
    first, second = shard_of(0), shard_of(1)
    early = jnp.concatenate(first[:2], axis=1)
    middle_part = jnp.concatenate(first[2:] + second[:2], axis=1)
    late = jnp.concatenate(second[2:], axis=1)
    early = spread(early, "dp").reshape(2, 16, owner_rows, -1)
    early = jnp.swapaxes(early, 0, 1).reshape(model_width, -1)

    def gather_plane(shard):
        return lax.all_gather(shard, "dp", axis=0, tiled=True, axis_index_groups=PLANE)

    middle_part = gather_plane(pair_halves(middle_part, first_half))
    late_pair = pair_halves(late, first_half)
    two_hidden = 2 * hidden_cols
    all_weights = [
        (
            early[:, :three_cols],
            early[:, three_cols:],
            middle_part[:, :hidden_cols],
            middle_part[:, hidden_cols:two_hidden],
        ),
        (
            middle_part[:, two_hidden : two_hidden + three_cols],
            middle_part[:, two_hidden + three_cols :],
        ),
    ]
    proj_bias = mix_features(proj_bias)
    ln_gain = mix_features(ln_gain)
    ln_shift = mix_features(ln_shift)

    current = with_neighbour(mix_features(hidden_in))
    cotangent = mix_features(cotangent)
    cotangent_across = swap(cotangent, 2)
    stored = []
    for layer_index in range(LAYERS):
        mat_qkv, mat_out, mat_up, mat_down = all_weights[layer_index]
        rows_all = gather_rows(current.astype(bfloat))
        mixed_rows = jnp.dot(
            jnp.concatenate(rows_all), mat_qkv, preferred_element_type=single
        )
        bias_here = lax.dynamic_slice_in_dim(
            qv_bias[layer_index], tensor_pos * head_cols, head_cols, 1
        )
        bias_three = jnp.concatenate(
            [bias_here[0], jnp.zeros((head_cols,), single), bias_here[1]]
        )
        qkv_bf = (mixed_rows + bias_three).astype(bfloat)
        context_rows = attend(qkv_bf, seg_row, seg_col)
        if not layer_index:
            context_rows, cotangent_across, late_pair = lax.optimization_barrier(
                (context_rows, cotangent_across, late_pair)
            )
            late = gather_plane(late_pair)
            all_weights[1] = all_weights[1] + (late[:, :hidden_cols], late[:, hidden_cols:])
        resid_one = (
            current + sum_rows(right_product(context_rows, mat_out)) + proj_bias[layer_index, 0]
        )
        middle, normed_one, inv_one = layer_norm(
            resid_one, ln_gain[layer_index, 0], ln_shift[layer_index, 0]
        )
        middle_all = gather_rows(middle.astype(bfloat))
        up_here = lax.dynamic_slice_in_dim(
            up_bias[layer_index], tensor_pos * hidden_cols, hidden_cols, 0
        )
        hidden_pre = jnp.dot(jnp.concatenate(middle_all), mat_up, preferred_element_type=single) + up_here
        hidden_bf = (hidden_pre * normal_cdf(hidden_pre)).astype(bfloat)
        resid_two = (
            middle + sum_rows(right_product(hidden_bf, mat_down)) + proj_bias[layer_index, 1]
        )
        output_rows, normed_two, inv_two = layer_norm(
            resid_two, ln_gain[layer_index, 1], ln_shift[layer_index, 1]
        )
        stored.append(
            (
                rows_all,
                qkv_bf,
                context_rows,
                normed_one,
                inv_one,
                middle_all,
                hidden_pre,
                hidden_bf,
                normed_two,
                inv_two,
            )
        )
        current = output_rows
    upstream = jnp.concatenate([cotangent, cotangent_across])
    sums_ffn = []
    both_axes = ("dp", "tensor")
    all_tokens, own_columns = [None] * LAYERS, [None] * LAYERS
    for layer_index in reversed(range(LAYERS)):
        (
            rows_all,
            qkv_bf,
            context_rows,
            normed_one,
            inv_one,
            middle_all,
            hidden_pre,
            hidden_bf,
            normed_two,
            inv_two,
        ) = stored[layer_index]
        mat_qkv, mat_out, mat_up, mat_down = all_weights[layer_index]
        gain_two = ln_gain[layer_index, 1]
        if layer_index:
            grad_two = norm_back(upstream, normed_two, inv_two, gain_two)
            short_two = grad_two.astype(bfloat)
            own_up = upstream[:own_rows]
            totals_two = [own_up * normed_two[:own_rows], own_up, grad_two[:own_rows]]
            totals_two = jnp.stack([jnp.sum(part, axis=0) for part in totals_two])
        else:
            grad_two, short_two, totals_two = norm_back_sum(
                grad_one, both, across, normed_two, inv_two, gain_two
            )
        grad_ffn_all = gather_rows(short_two)
        grad_hidden = jnp.dot(jnp.concatenate(grad_ffn_all), mat_down, preferred_element_type=single)
        grad_pre = grad_hidden * gelu_slope(hidden_pre)
        grad_pre_bf = grad_pre.astype(bfloat)
        up_term = jnp.sum(grad_pre, axis=0)
        block_ffn = weight_grads(
            (middle_all, grad_pre_bf),
            (grad_ffn_all, hidden_bf),
            extra=None if layer_index else block_last,
        )
        both, across, _ = half_sums(right_product(grad_pre_bf, mat_up), block_ffn)
        sums_ffn.append(
            lax.psum_scatter(
                block_ffn, "dp", scatter_dimension=0, tiled=True, axis_index_groups=PLANE
            )
        )
        grad_one, short_one, totals_one = norm_back_sum(
            grad_two, both, across, normed_one, inv_one, ln_gain[layer_index, 0]
        )
        grad_attn_all = gather_rows(short_one)
        grad_context = jnp.dot(
            jnp.concatenate(grad_attn_all), mat_out, preferred_element_type=single
        ).astype(bfloat)
        grad_mixed_bf, total = attend_back(qkv_bf, seg_row, seg_col, grad_context)
        all_tokens[layer_index] = jnp.stack([totals_one[:3], totals_two[:3]], axis=1).reshape(-1)
        own_columns[layer_index] = jnp.concatenate(
            [total[0, :head_cols], total[0, 2 * head_cols :], up_term]
        )
        pairs = ((rows_all, grad_mixed_bf), (grad_attn_all, context_rows))
        if layer_index:
            input_part = right_product(grad_mixed_bf, mat_qkv)
            both, across, block_last = half_sums(input_part, weight_grads(*pairs))
        else:
            small = jnp.concatenate(all_tokens + own_columns).reshape(model_width, -1)
            high = small.astype(bfloat)
            low = (small - high.astype(single)).astype(bfloat)
            count = small.shape[1]
            rest = jnp.zeros((model_width, 128 - 2 * count), bfloat)
            extra = jnp.concatenate([high, low, rest], axis=1)
            sums_attn = sum_owned(weight_grads(*pairs, extra=extra), "dp", PLANE)
            block_cols = three_cols + head_cols
            small = sums_attn[:, block_cols : block_cols + count]
            small = small + sums_attn[:, block_cols + count : block_cols + 2 * count]
            sums_attn = sums_attn[:, :block_cols]
            both, across, small = half_sums(right_product(grad_mixed_bf, mat_qkv), small)
            small = spread(small.reshape(1, -1), both_axes)
            early = sum_halves(
                jnp.concatenate([sums_ffn[0].astype(single), sums_attn], axis=1), first_half
            )
            small, early = lax.optimization_barrier((small, early))
            upstream = grad_one + add_halves(both, across)
    small, sums_ffn[1] = lax.optimization_barrier((small, sums_ffn[1]))
    small = small.reshape(2, 16, tensor_count, -1)
    small = jnp.swapaxes(jnp.sum(small, axis=0), 0, 1).reshape(tensor_count, -1)
    token_count = LAYERS * 6 * model_width
    over_tokens = jnp.sum(small[:, :token_count], axis=0).reshape(LAYERS, 3, 2, model_width)
    over_tokens = unmix_features(over_tokens)
    over_columns = jnp.swapaxes(small[:, token_count:].reshape(tensor_count, LAYERS, -1), 0, 1)
    total_qv = over_columns[:, :, : 2 * head_cols].reshape(LAYERS, tensor_count, 2, head_cols)
    total_qv = jnp.swapaxes(total_qv, 1, 2).reshape(LAYERS, 2, model_width)
    total_up = over_columns[:, :, 2 * head_cols :].reshape(LAYERS, -1)
    late = sum_halves(sums_ffn[1], first_half)
    sums_first = jnp.concatenate([late[:, :two_hidden], early[:, two_hidden:]], axis=1)
    sums_last = jnp.concatenate([early[:, :two_hidden], late[:, two_hidden:]], axis=1)
    cut_out = two_hidden + three_cols
    grad_weights = []
    for sums in (sums_first, sums_last):
        grad_weights.append(
            (
                sums[:, two_hidden:cut_out].reshape(owner_rows, 3, head_cols),
                sums[:, cut_out:],
                sums[:, :hidden_cols],
                sums[:, hidden_cols:two_hidden],
            )
        )
    return (
        unmix_features(current[:own_rows]),
        unmix_features(upstream[:own_rows]),
        jnp.stack([part[0] for part in grad_weights]),
        jnp.stack([part[1] for part in grad_weights]),
        jnp.stack([part[2] for part in grad_weights]),
        jnp.stack([part[3] for part in grad_weights]),
        total_qv,
        over_tokens[:, 2],
        total_up,
        over_tokens[:, 0],
        over_tokens[:, 1],
    )


def solution(mesh):
    placed = (
        P(("dp", "tensor"), None),
        P("dp", None),
        P(None, "dp", None, "tensor"),
        P(None, "dp", "tensor"),
        P(None, "dp", "tensor"),
        P(None, "dp", "tensor"),
        P(),
        P(),
        P(),
        P(),
        P(),
        P(("dp", "tensor"), None),
    )
    return jax.shard_map(
        shards,
        mesh=mesh,
        in_specs=placed,
        out_specs=(
            P(("dp", "tensor"), None),
            P(("dp", "tensor"), None),
            P(None, "dp", None, "tensor"),
            P(None, "dp", "tensor"),
            P(None, "dp", "tensor"),
            P(None, "dp", "tensor"),
            P(),
            P(),
            P(),
            P(),
            P(),
        ),
        check_vma=False,
    )
```
